256 devices in a mesh: section: 16 (over x, y), col: 16 (over z, core).
Axes of the slice: x: 4, y: 4, z: 8, core: 2. Of those that a mesh axis runs over, the one named last changes fastest.
Arguments:
- features: bfloat16 [4, 32, 65536], P(None, 'section', 'col'), may hold values from -48 to 48
- weights: bfloat16 [16, 512, 4, 128, 128], P('section', 'col'), may hold values from -0.375 to 0.375
- sources: int32 [16, 512, 4], P('section', 'col'), may hold values from 0 to 511, as said below
- bias: float32 [16, 65536], P('section', 'col'), may hold values from -0.3 to 0.3
- batch_rows: int32 [4], replicated, may hold values from 1 to 32, as said below
Outputs:
- final_act: bfloat16 [4, 32, 65536], P(None, 'section', 'col')
The draws below stay inside these ranges and needn't reach their ends.
Inputs may be any that keep to these rules, and one draw needn't show every extreme that they name: In every layer, the sources of all block columns c with c // 32 = d name exactly 2 distinct blocks b with b // 32 = e, for every pair d, e. `batch_rows`: some micro-batch has exactly 32 live rows.
All inputs are finite; a program needn't handle non-finite values.
Results may differ from the reference program's by a relative error of at most 0.033.
Values may be sent and summed in bfloat16 or wider, within the bound.
A program may use at most 64 MiB of HBM per device.

```python
import jax
import jax.numpy as jnp
from jax import lax

NEUR = 65536
BLK = 128
KNZ = 4
CAP = 2
ROWS = 32
M_BATCH = 4
NBLK = 512
DEV_BLK = 32
LAYERS = 16
N_COL = 16


def draw_sources(key, part):
    dev_blocks = NBLK // N_COL
    pool_size = N_COL * CAP

    def one_device(dev_key):
        keys = jax.random.split(dev_key, N_COL + 1)
        picks = jax.vmap(lambda one_key: jax.random.permutation(one_key, dev_blocks)[:CAP])(keys[:N_COL])
        offsets = dev_blocks * jnp.arange(N_COL, dtype=jnp.int32)[:, None]
        pool = (picks.astype(jnp.int32) + offsets).reshape(pool_size)
        order = jax.random.permutation(keys[N_COL], dev_blocks * KNZ).astype(jnp.int32)
        return pool[order % pool_size].reshape(dev_blocks, KNZ)

    def one_layer(layer_key):
        return jax.vmap(one_device)(jax.random.split(layer_key, N_COL)).reshape(NBLK, KNZ)
    return jax.vmap(one_layer)(jax.random.split(key, LAYERS)).astype(jnp.int32)


def draw_batch_rows(key, part):
    first_key = jax.random.fold_in(key, 11)
    second_key = jax.random.fold_in(key, 23)
    counts = jax.random.randint(first_key, (M_BATCH,), 1, ROWS + 1, dtype=jnp.int32)
    fullest = jax.random.randint(second_key, (), 0, M_BATCH, dtype=jnp.int32)
    slots = jnp.arange(M_BATCH, dtype=jnp.int32)
    return jnp.where(slots == fullest, jnp.int32(ROWS), counts).astype(jnp.int32)


def block_scale(own_key, dims, cuts, low, high):
    def one(position, blocks):
        heights = jax.random.uniform(jax.random.fold_in(jax.random.fold_in(own_key, 6), position), (blocks,), jnp.float32, low / len(cuts), high / len(cuts))
        return jnp.repeat(jnp.exp(heights), dims[position] // blocks).reshape((-1,) + (1,) * (len(dims) - position - 1))

    level = one(*cuts[0])
    for cut in cuts[1:]:
        level = level * one(*cut)
    return level


def centred(rng, dims, deviation, limit, shards=(), kind=jnp.bfloat16):
    values = deviation * jax.random.normal(rng, dims, jnp.float32)
    if shards:
        values = values * block_scale(rng, dims, shards, -0.22, 0.18)
    return jnp.clip(values, -limit, limit).astype(kind)


def setup_inputs(seed: int = 0) -> dict:
    key_list = jax.random.split(jax.random.key(seed), 6)
    features = centred(key_list[0], (M_BATCH, ROWS, NEUR), 8.0, 48.0, ((1, 16), (2, 16)))
    weights = centred(key_list[1], (LAYERS, NBLK, KNZ, BLK, BLK), (KNZ * BLK // 2) ** -0.5, 0.375, ((0, 16), (1, 16)))
    sources = draw_sources(jax.random.fold_in(key_list[5], 71), 0)
    bias = jnp.clip(jax.random.uniform(key_list[3], (LAYERS, NEUR), jnp.float32, -0.3, 0.3) * block_scale(key_list[3], (LAYERS, NEUR), ((0, 16), (1, 16)), -0.4, 0.0), -0.3, 0.3)
    batch_rows = draw_batch_rows(jax.random.fold_in(key_list[5], 71), 0)
    return dict(features=features, weights=weights, sources=sources, bias=bias, batch_rows=batch_rows)


def reference(features, weights, sources, bias, batch_rows):
    row_total = M_BATCH * ROWS
    groups = NBLK // DEV_BLK
    activity = features.reshape(row_total, NBLK, BLK).transpose(1, 0, 2)
    for layer_idx in range(LAYERS):
        layer_w = weights[layer_idx].reshape(groups, DEV_BLK, KNZ, BLK, BLK)
        layer_s = sources[layer_idx].reshape(groups, DEV_BLK, KNZ)
        layer_b = bias[layer_idx].reshape(groups, DEV_BLK, 1, BLK)

        def group_step(group_args, current=activity):
            block_w, block_s, block_b = group_args
            picked = current[block_s].astype(jnp.float32)
            preact = jnp.einsum("ckrb,ckbo->cro", picked, block_w.astype(jnp.float32))
            return jnp.clip(preact + block_b, 0.0, 32.0).astype(jnp.bfloat16)

        activity = lax.map(group_step, (layer_w, layer_s, layer_b)).reshape(NBLK, row_total, BLK)
    result = activity.transpose(1, 0, 2).reshape(M_BATCH, ROWS, NEUR)
    row_mask = jnp.arange(ROWS, dtype=jnp.int32)[None, :] < batch_rows[:, None]
    return jnp.where(row_mask[:, :, None], result, jnp.zeros_like(result)).astype(jnp.bfloat16)
```

```python
import functools

import jax
import jax.numpy as jnp
from jax import lax
from jax.experimental import pallas as pl
from jax.experimental.pallas import tpu as pltpu
from jax.sharding import PartitionSpec as P

CAP = 2
MESH_ID = pl.DeviceIdType.MESH


def from_behind(x, axis, by):
    size = lax.axis_size(axis)
    pairs = [(i, i + by) for i in range(size) if 0 <= i + by < size]
    return lax.ppermute(x, axis, pairs)


def request_lists(pattern_table, owners, blocks_own, slot_total):
    dest_entries = pattern_table.reshape(owners, -1)
    block_total = owners * blocks_own
    catalog = jnp.arange(block_total, dtype=jnp.int32)
    wanted = jnp.any(dest_entries[:, :, None] == catalog[None, None, :], axis=1)
    wanted = wanted.reshape(owners, owners, blocks_own)
    block_ranks = jnp.cumsum(wanted.astype(jnp.int32), axis=2) - 1
    slot_ids = jnp.arange(slot_total, dtype=jnp.int32)
    chosen = wanted[:, :, None, :] & (block_ranks[:, :, None, :] == slot_ids[None, None, :, None])
    local_ids = jnp.arange(blocks_own, dtype=jnp.int32)
    positions = jnp.sum(chosen.astype(jnp.int32) * local_ids[None, None, None, :], axis=3)
    present = jnp.any(chosen, axis=3)
    return (positions, present)


def exchange_kernel(sections, owners, send_ref, recv_ref, send_sem, recv_sem):
    me_s = lax.axis_index("section")
    me_c = lax.axis_index("col")
    nxt = lax.rem(me_s + 1, sections)
    prv = lax.rem(me_s + sections - 1, sections)
    barrier = pltpu.get_barrier_semaphore()
    for d in range(owners):
        pl.semaphore_signal(barrier, inc=1, device_id=(prv, d), device_id_type=MESH_ID)
    pl.semaphore_wait(barrier, owners)
    copies = []
    for d in range(owners):
        copy = pltpu.make_async_remote_copy(
            src_ref=send_ref.at[d],
            dst_ref=recv_ref.at[me_c],
            send_sem=send_sem.at[d],
            recv_sem=recv_sem.at[me_c],
            device_id=(nxt, d),
            device_id_type=MESH_ID,
        )
        copy.start()
        copies.append(copy)
    for d in range(owners):
        copies[d].wait_send()
    for e in range(owners):
        pltpu.make_async_remote_copy(
            src_ref=send_ref.at[e],
            dst_ref=recv_ref.at[e],
            send_sem=send_sem.at[e],
            recv_sem=recv_sem.at[e],
            device_id=(prv, e),
            device_id_type=MESH_ID,
        ).wait_recv()


def exchange(send_buf, sections, owners):
    return pl.pallas_call(
        functools.partial(exchange_kernel, sections, owners),
        out_shape=jax.ShapeDtypeStruct(send_buf.shape, send_buf.dtype),
        in_specs=[pl.BlockSpec(memory_space=pltpu.VMEM)],
        out_specs=pl.BlockSpec(memory_space=pltpu.VMEM),
        scratch_shapes=[
            pltpu.SemaphoreType.DMA((owners,)),
            pltpu.SemaphoreType.DMA((owners,)),
        ],
        compiler_params=pltpu.CompilerParams(collective_id=0, has_side_effects=True),
    )(send_buf)


def body(features, weights, sources, bias, batch_rows):
    sections = lax.axis_size("section")
    owners = lax.axis_size("col")
    section_idx = lax.axis_index("section")
    col_idx = lax.axis_index("col")
    local_w = weights[0]
    blocks_own = local_w.shape[0]
    nonzero_count = local_w.shape[1]
    block_size = local_w.shape[2]
    local_src = sources[0].reshape(blocks_own * nonzero_count)
    local_bias = bias[0].reshape(blocks_own, 1, block_size)
    pattern_table = lax.all_gather(sources[0], "col", axis=0, tiled=True)
    positions, present = request_lists(pattern_table, owners, blocks_own, CAP)
    outgoing = lax.dynamic_index_in_dim(positions, col_idx, 1, keepdims=False)
    outgoing_next = from_behind(outgoing, "section", -1).reshape(owners * CAP)
    outgoing = outgoing.reshape(owners * CAP)
    incoming = lax.dynamic_index_in_dim(positions, col_idx, 0, keepdims=False)
    incoming_ok = lax.dynamic_index_in_dim(present, col_idx, 0, keepdims=False)
    global_ids = incoming + blocks_own * jnp.arange(owners, dtype=jnp.int32)[:, None]
    matches = (local_src[:, None] == global_ids.reshape(-1)[None, :]) & incoming_ok.reshape(-1)[
        None, :
    ]
    slot_of = jnp.sum(
        matches.astype(jnp.int32) * jnp.arange(owners * CAP, dtype=jnp.int32)[None, :], axis=1
    )
    all_inputs = lax.all_gather(features, "section", axis=1, tiled=True)
    batches = all_inputs.shape[0]
    row_total = all_inputs.shape[1]
    piece_total = batches
    tick_total = piece_total + sections - 1
    blocks_in = all_inputs.reshape(batches, row_total, blocks_own, block_size)
    blocks_in = blocks_in.transpose(0, 2, 1, 3)
    first_payload = jnp.take(blocks_in, outgoing, axis=1).reshape(
        batches, owners, CAP, row_total, block_size
    )
    first_recv = lax.all_to_all(first_payload, "col", split_axis=1, concat_axis=1, tiled=True)

    def combine(received):
        flat_recv = received.reshape(owners * CAP, row_total, block_size)
        picked = jnp.take(flat_recv, slot_of, axis=0).reshape(
            blocks_own, nonzero_count, row_total, block_size
        )
        preact = jnp.einsum("ckrb,ckbo->cro", picked, local_w, preferred_element_type=jnp.float32)
        return jnp.clip(preact + local_bias, 0.0, 32.0).astype(jnp.bfloat16)

    def tick(tick_idx, carry):
        carried, finished = carry
        entering = lax.dynamic_index_in_dim(
            first_recv, jnp.minimum(tick_idx, piece_total - 1), 0, keepdims=False
        )
        current = jnp.where(section_idx == 0, entering, carried)
        layer_out = combine(current)
        slot_idx = jnp.clip(tick_idx - sections + 1, 0, piece_total - 1)
        storing = (section_idx == sections - 1) & (tick_idx >= sections - 1)
        existing = lax.dynamic_index_in_dim(finished, slot_idx, 0, keepdims=False)
        finished = lax.dynamic_update_index_in_dim(
            finished, jnp.where(storing, layer_out, existing), slot_idx, 0
        )
        send_buf = jnp.take(layer_out, outgoing_next, axis=0).reshape(
            owners, CAP, row_total, block_size
        )
        passed = exchange(send_buf, sections, owners)
        return (passed, finished)

    initial = (
        jnp.zeros((owners, CAP, row_total, block_size), jnp.bfloat16),
        jnp.zeros((piece_total, blocks_own, row_total, block_size), jnp.bfloat16),
    )
    carried, finished = lax.fori_loop(0, tick_total, tick, initial)
    completed = finished.transpose(0, 2, 1, 3).reshape(
        batches, row_total, blocks_own * block_size
    )
    own_rows = row_total // sections
    outgoing_rows = completed.reshape(batches, sections, own_rows, blocks_own * block_size)
    gathered = lax.all_to_all(outgoing_rows, "section", split_axis=1, concat_axis=1, tiled=True)
    own_result = gathered[:, sections - 1]
    row_ids = section_idx * own_rows + jnp.arange(own_rows, dtype=jnp.int32)
    row_mask = row_ids[None, :] < batch_rows[:, None]
    return jnp.where(row_mask[:, :, None], own_result, jnp.zeros_like(own_result))


def solution(mesh):
    in_specs = (
        P(None, "section", "col"),
        P("section", "col", None, None, None),
        P("section", "col", None),
        P("section", "col"),
        P(),
    )
    out_specs = P(None, "section", "col")
    return jax.shard_map(body, mesh=mesh, in_specs=in_specs, out_specs=out_specs, check_vma=False)
```

```python
import functools

import jax
import jax.numpy as jnp
from jax import lax
from jax.experimental import pallas as pl
from jax.experimental.pallas import tpu as pltpu
from jax.sharding import PartitionSpec as P

CAP = 2
MESH_ID = pl.DeviceIdType.MESH


def from_behind(x, axis, by):
    size = lax.axis_size(axis)
    pairs = [(i, i + by) for i in range(size) if 0 <= i + by < size]
    return lax.ppermute(x, axis, pairs)


def request_lists(pattern_table, owners, blocks_own, slot_total):
    dest_entries = pattern_table.reshape(owners, -1)
    block_total = owners * blocks_own
    catalog = jnp.arange(block_total, dtype=jnp.int32)
    wanted = jnp.any(dest_entries[:, :, None] == catalog[None, None, :], axis=1)
    wanted = wanted.reshape(owners, owners, blocks_own)
    block_ranks = jnp.cumsum(wanted.astype(jnp.int32), axis=2) - 1
    slot_ids = jnp.arange(slot_total, dtype=jnp.int32)
    chosen = wanted[:, :, None, :] & (block_ranks[:, :, None, :] == slot_ids[None, None, :, None])
    local_ids = jnp.arange(blocks_own, dtype=jnp.int32)
    positions = jnp.sum(chosen.astype(jnp.int32) * local_ids[None, None, None, :], axis=3)
    present = jnp.any(chosen, axis=3)
    return (positions, present)


def pipeline_kernel(
    sections, owners, batches, first_ref, w_ref, b_ref, slot_ref, next_ref,
    out_ref, *scratch,
):
    recv = scratch[:batches]
    send = scratch[batches:2 * batches]
    send_sem, recv_sem, local_sem = scratch[2 * batches:]
    me_s = lax.axis_index("section")
    me_c = lax.axis_index("col")
    blocks_own = w_ref.shape[0]
    nonzero_count = w_ref.shape[1]
    barrier = pltpu.get_barrier_semaphore()

    @pl.when(me_s > 0)
    def _():
        for d in range(owners):
            pl.semaphore_signal(barrier, inc=1, device_id=(me_s - 1, d), device_id_type=MESH_ID)

    @pl.when(me_s < sections - 1)
    def _():
        for d in range(owners):
            pl.semaphore_signal(barrier, inc=1, device_id=(me_s + 1, d), device_id_type=MESH_ID)

    peers = owners * (
        (me_s > 0).astype(jnp.int32) + (me_s < sections - 1).astype(jnp.int32)
    )
    pl.semaphore_wait(barrier, peers)

    @pl.when(me_s == 0)
    def _():
        for m in range(batches):
            first = pltpu.make_async_copy(first_ref.at[m], recv[m], local_sem)
            first.start()
            first.wait()

    def outgoing_copy(m, d):
        return pltpu.make_async_remote_copy(
            src_ref=send[m].at[pl.ds(d * CAP, CAP)],
            dst_ref=recv[m].at[pl.ds(me_c * CAP, CAP)],
            send_sem=send_sem.at[m, d],
            recv_sem=recv_sem.at[m, me_c],
            device_id=(me_s + 1, d),
            device_id_type=MESH_ID,
        )

    for m in range(batches):

        @pl.when(me_s > 0)
        def _():
            for e in range(owners):
                pltpu.make_async_remote_copy(
                    src_ref=send[m].at[pl.ds(e * CAP, CAP)],
                    dst_ref=recv[m].at[pl.ds(e * CAP, CAP)],
                    send_sem=send_sem.at[m, e],
                    recv_sem=recv_sem.at[m, e],
                    device_id=(me_s - 1, e),
                    device_id_type=MESH_ID,
                ).wait_recv()

        def block_step(j, carry):
            acc = None
            for k in range(nonzero_count):
                picked = recv[m][slot_ref[j * nonzero_count + k]]
                term = jnp.dot(picked, w_ref[j, k], preferred_element_type=jnp.float32)
                acc = term if acc is None else acc + term
            out_ref[m, j] = jnp.clip(acc + b_ref[j], 0.0, 32.0).astype(out_ref.dtype)
            return carry

        lax.fori_loop(0, blocks_own, block_step, 0)

        @pl.when(me_s < sections - 1)
        def _():
            def stage(i, carry):
                send[m][i] = out_ref[m, next_ref[i]]
                return carry

            lax.fori_loop(0, owners * CAP, stage, 0)
            for d in range(owners):
                outgoing_copy(m, d).start()

    @pl.when(me_s < sections - 1)
    def _():
        for m in range(batches):
            for d in range(owners):
                outgoing_copy(m, d).wait_send()


def run_pipeline(first_recv, local_w, local_bias, slot_of, outgoing_next, sections, owners):
    batches = first_recv.shape[0]
    blocks_own = local_w.shape[0]
    rows = first_recv.shape[2]
    block_size = local_w.shape[-1]
    vmem = pl.BlockSpec(memory_space=pltpu.VMEM)
    smem = pl.BlockSpec(memory_space=pltpu.SMEM)
    return pl.pallas_call(
        functools.partial(pipeline_kernel, sections, owners, batches),
        out_shape=jax.ShapeDtypeStruct((batches, blocks_own, rows, block_size), jnp.bfloat16),
        in_specs=[vmem, vmem, vmem, smem, smem],
        out_specs=vmem,
        scratch_shapes=[
            *[pltpu.VMEM(first_recv.shape[1:], jnp.bfloat16) for _ in range(2 * batches)],
            pltpu.SemaphoreType.DMA((batches, owners)),
            pltpu.SemaphoreType.DMA((batches, owners)),
            pltpu.SemaphoreType.DMA(()),
        ],
        compiler_params=pltpu.CompilerParams(collective_id=0, has_side_effects=True),
    )(first_recv, local_w, local_bias, slot_of, outgoing_next)


def body(features, weights, sources, bias, batch_rows):
    sections = lax.axis_size("section")
    owners = lax.axis_size("col")
    section_idx = lax.axis_index("section")
    col_idx = lax.axis_index("col")
    local_w = weights[0]
    blocks_own = local_w.shape[0]
    nonzero_count = local_w.shape[1]
    block_size = local_w.shape[2]
    local_src = sources[0].reshape(blocks_own * nonzero_count)
    pattern_table = lax.all_gather(sources[0], "col", axis=0, tiled=True)
    positions, present = request_lists(pattern_table, owners, blocks_own, CAP)
    outgoing = lax.dynamic_index_in_dim(positions, col_idx, 1, keepdims=False)
    outgoing_next = from_behind(outgoing, "section", -1).reshape(owners * CAP)
    outgoing = outgoing.reshape(owners * CAP)
    incoming = lax.dynamic_index_in_dim(positions, col_idx, 0, keepdims=False)
    incoming_ok = lax.dynamic_index_in_dim(present, col_idx, 0, keepdims=False)
    global_ids = incoming + blocks_own * jnp.arange(owners, dtype=jnp.int32)[:, None]
    matches = (local_src[:, None] == global_ids.reshape(-1)[None, :]) & incoming_ok.reshape(-1)[
        None, :
    ]
    slot_of = jnp.sum(
        matches.astype(jnp.int32) * jnp.arange(owners * CAP, dtype=jnp.int32)[None, :], axis=1
    )
    all_inputs = lax.all_gather(features, "section", axis=1, tiled=True)
    batches = all_inputs.shape[0]
    row_total = all_inputs.shape[1]
    blocks_in = all_inputs.reshape(batches, row_total, blocks_own, block_size)
    blocks_in = blocks_in.transpose(0, 2, 1, 3)
    first_payload = jnp.take(blocks_in, outgoing, axis=1).reshape(
        batches, owners, CAP, row_total, block_size
    )
    first_recv = lax.all_to_all(first_payload, "col", split_axis=1, concat_axis=1, tiled=True)

    first_recv = first_recv.reshape(batches, owners * CAP, row_total, block_size)
    finished = run_pipeline(
        first_recv, local_w, bias[0].reshape(blocks_own, 1, block_size), slot_of,
        outgoing_next, sections, owners,
    )
    completed = finished.transpose(0, 2, 1, 3).reshape(
        batches, row_total, blocks_own * block_size
    )
    own_rows = row_total // sections
    outgoing_rows = completed.reshape(batches, sections, own_rows, blocks_own * block_size)
    gathered = lax.all_to_all(outgoing_rows, "section", split_axis=1, concat_axis=1, tiled=True)
    own_result = gathered[:, sections - 1]
    row_ids = section_idx * own_rows + jnp.arange(own_rows, dtype=jnp.int32)
    row_mask = row_ids[None, :] < batch_rows[:, None]
    return jnp.where(row_mask[:, :, None], own_result, jnp.zeros_like(own_result))


def solution(mesh):
    in_specs = (
        P(None, "section", "col"),
        P("section", "col", None, None, None),
        P("section", "col", None),
        P("section", "col"),
        P(),
    )
    out_specs = P(None, "section", "col")
    return jax.shard_map(body, mesh=mesh, in_specs=in_specs, out_specs=out_specs, check_vma=False)
```

```python
import functools

import jax
import jax.numpy as jnp
from jax import lax
from jax.experimental import pallas as pl
from jax.experimental.pallas import tpu as pltpu
from jax.sharding import PartitionSpec as P

CAP = 2
MESH_ID = pl.DeviceIdType.MESH


def from_behind(x, axis, by):
    size = lax.axis_size(axis)
    pairs = [(i, i + by) for i in range(size) if 0 <= i + by < size]
    return lax.ppermute(x, axis, pairs)


def request_lists(pattern_table, owners, blocks_own, slot_total):
    dest_entries = pattern_table.reshape(owners, -1)
    block_total = owners * blocks_own
    catalog = jnp.arange(block_total, dtype=jnp.int32)
    wanted = jnp.any(dest_entries[:, :, None] == catalog[None, None, :], axis=1)
    wanted = wanted.reshape(owners, owners, blocks_own)
    block_ranks = jnp.cumsum(wanted.astype(jnp.int32), axis=2) - 1
    slot_ids = jnp.arange(slot_total, dtype=jnp.int32)
    chosen = wanted[:, :, None, :] & (block_ranks[:, :, None, :] == slot_ids[None, None, :, None])
    local_ids = jnp.arange(blocks_own, dtype=jnp.int32)
    positions = jnp.sum(chosen.astype(jnp.int32) * local_ids[None, None, None, :], axis=3)
    present = jnp.any(chosen, axis=3)
    return (positions, present)


def pipeline_kernel(
    sections, owners, batches, first_ref, w_ref, b_ref, slot_ref, next_ref,
    out_ref, *scratch,
):
    recv = scratch[:batches]
    send = scratch[batches:2 * batches]
    send_sem, recv_sem, local_sem = scratch[2 * batches:]
    me_s = lax.axis_index("section")
    me_c = lax.axis_index("col")
    blocks_own = w_ref.shape[0]
    nonzero_count = slot_ref.shape[0] // blocks_own
    barrier = pltpu.get_barrier_semaphore()

    @pl.when(me_s > 0)
    def _():
        for d in range(owners):
            pl.semaphore_signal(barrier, inc=1, device_id=(me_s - 1, d), device_id_type=MESH_ID)

    @pl.when(me_s < sections - 1)
    def _():
        for d in range(owners):
            pl.semaphore_signal(barrier, inc=1, device_id=(me_s + 1, d), device_id_type=MESH_ID)

    peers = owners * (
        (me_s > 0).astype(jnp.int32) + (me_s < sections - 1).astype(jnp.int32)
    )
    pl.semaphore_wait(barrier, peers)

    @pl.when(me_s == 0)
    def _():
        for m in range(batches):
            first = pltpu.make_async_copy(first_ref.at[m], recv[m], local_sem)
            first.start()
            first.wait()

    def outgoing_copy(m, d):
        return pltpu.make_async_remote_copy(
            src_ref=send[m].at[pl.ds(d * CAP, CAP)],
            dst_ref=recv[m].at[pl.ds(me_c * CAP, CAP)],
            send_sem=send_sem.at[m, d],
            recv_sem=recv_sem.at[m, me_c],
            device_id=(me_s + 1, d),
            device_id_type=MESH_ID,
        )

    for m in range(batches):

        @pl.when(me_s > 0)
        def _():
            for e in range(owners):
                pltpu.make_async_remote_copy(
                    src_ref=send[m].at[pl.ds(e * CAP, CAP)],
                    dst_ref=recv[m].at[pl.ds(e * CAP, CAP)],
                    send_sem=send_sem.at[m, e],
                    recv_sem=recv_sem.at[m, e],
                    device_id=(me_s - 1, e),
                    device_id_type=MESH_ID,
                ).wait_recv()

        def block_step(j, carry):
            picked = jnp.concatenate(
                [recv[m][slot_ref[j * nonzero_count + k]] for k in range(nonzero_count)], axis=-1
            )
            acc = jnp.dot(picked, w_ref[j], preferred_element_type=jnp.float32)
            out_ref[m, j] = jnp.clip(acc + b_ref[j], 0.0, 32.0).astype(out_ref.dtype)
            return carry

        lax.fori_loop(0, blocks_own, block_step, 0, unroll=True)

        @pl.when(me_s < sections - 1)
        def _():
            def stage(i, carry):
                send[m][i] = out_ref[m, next_ref[i]]
                return carry

            lax.fori_loop(0, owners * CAP, stage, 0, unroll=True)
            for d in range(owners):
                outgoing_copy(m, d).start()

    @pl.when(me_s < sections - 1)
    def _():
        for m in range(batches):
            for d in range(owners):
                outgoing_copy(m, d).wait_send()


def run_pipeline(first_recv, local_w, local_bias, slot_of, outgoing_next, sections, owners):
    batches = first_recv.shape[0]
    blocks_own = local_w.shape[0]
    rows = first_recv.shape[2]
    block_size = local_w.shape[-1]
    vmem = pl.BlockSpec(memory_space=pltpu.VMEM)
    smem = pl.BlockSpec(memory_space=pltpu.SMEM)
    return pl.pallas_call(
        functools.partial(pipeline_kernel, sections, owners, batches),
        out_shape=jax.ShapeDtypeStruct((batches, blocks_own, rows, block_size), jnp.bfloat16),
        in_specs=[vmem, vmem, vmem, smem, smem],
        out_specs=vmem,
        scratch_shapes=[
            *[pltpu.VMEM(first_recv.shape[1:], jnp.bfloat16) for _ in range(2 * batches)],
            pltpu.SemaphoreType.DMA((batches, owners)),
            pltpu.SemaphoreType.DMA((batches, owners)),
            pltpu.SemaphoreType.DMA(()),
        ],
        compiler_params=pltpu.CompilerParams(collective_id=0, has_side_effects=True),
    )(first_recv, local_w, local_bias, slot_of, outgoing_next)


def body(features, weights, sources, bias, batch_rows):
    sections = lax.axis_size("section")
    owners = lax.axis_size("col")
    section_idx = lax.axis_index("section")
    col_idx = lax.axis_index("col")
    local_w = weights[0]
    blocks_own = local_w.shape[0]
    nonzero_count = local_w.shape[1]
    block_size = local_w.shape[2]
    local_src = sources[0].reshape(blocks_own * nonzero_count)
    pattern_table = lax.all_gather(sources[0], "col", axis=0, tiled=True)
    positions, present = request_lists(pattern_table, owners, blocks_own, CAP)
    outgoing = lax.dynamic_index_in_dim(positions, col_idx, 1, keepdims=False)
    outgoing_next = from_behind(outgoing, "section", -1).reshape(owners * CAP)
    outgoing = outgoing.reshape(owners * CAP)
    incoming = lax.dynamic_index_in_dim(positions, col_idx, 0, keepdims=False)
    incoming_ok = lax.dynamic_index_in_dim(present, col_idx, 0, keepdims=False)
    global_ids = incoming + blocks_own * jnp.arange(owners, dtype=jnp.int32)[:, None]
    matches = (local_src[:, None] == global_ids.reshape(-1)[None, :]) & incoming_ok.reshape(-1)[
        None, :
    ]
    slot_of = jnp.sum(
        matches.astype(jnp.int32) * jnp.arange(owners * CAP, dtype=jnp.int32)[None, :], axis=1
    )
    all_inputs = lax.all_gather(features, "section", axis=1, tiled=True)
    batches = all_inputs.shape[0]
    row_total = all_inputs.shape[1]
    blocks_in = all_inputs.reshape(batches, row_total, blocks_own, block_size)
    blocks_in = blocks_in.transpose(0, 2, 1, 3)
    first_payload = jnp.take(blocks_in, outgoing, axis=1).reshape(
        batches, owners, CAP, row_total, block_size
    )
    first_recv = lax.all_to_all(first_payload, "col", split_axis=1, concat_axis=1, tiled=True)

    first_recv = first_recv.reshape(batches, owners * CAP, row_total, block_size)
    finished = run_pipeline(
        first_recv, local_w.reshape(blocks_own, nonzero_count * block_size, block_size), bias[0].reshape(blocks_own, 1, block_size), slot_of,
        outgoing_next, sections, owners,
    )
    completed = finished.transpose(0, 2, 1, 3).reshape(
        batches, row_total, blocks_own * block_size
    )
    own_rows = row_total // sections
    outgoing_rows = completed.reshape(batches, sections, own_rows, blocks_own * block_size)
    gathered = lax.all_to_all(outgoing_rows, "section", split_axis=1, concat_axis=1, tiled=True)
    own_result = gathered[:, sections - 1]
    row_ids = section_idx * own_rows + jnp.arange(own_rows, dtype=jnp.int32)
    row_mask = row_ids[None, :] < batch_rows[:, None]
    return jnp.where(row_mask[:, :, None], own_result, jnp.zeros_like(own_result))


def solution(mesh):
    in_specs = (
        P(None, "section", "col"),
        P("section", "col", None, None, None),
        P("section", "col", None),
        P("section", "col"),
        P(),
    )
    out_specs = P(None, "section", "col")
    return jax.shard_map(body, mesh=mesh, in_specs=in_specs, out_specs=out_specs, check_vma=False)
```

```python
import functools

import jax
import jax.numpy as jnp
from jax import lax
from jax.experimental import pallas as pl
from jax.experimental.pallas import tpu as pltpu
from jax.sharding import PartitionSpec as P

CAP = 2
MESH_ID = pl.DeviceIdType.MESH


def from_behind(x, axis, by):
    size = lax.axis_size(axis)
    pairs = [(i, i + by) for i in range(size) if 0 <= i + by < size]
    return lax.ppermute(x, axis, pairs)


def request_lists(pattern_table, owners, blocks_own, slot_total):
    dest_entries = pattern_table.reshape(owners, -1)
    block_total = owners * blocks_own
    catalog = jnp.arange(block_total, dtype=jnp.int32)
    wanted = jnp.any(dest_entries[:, :, None] == catalog[None, None, :], axis=1)
    wanted = wanted.reshape(owners, owners, blocks_own)
    block_ranks = jnp.cumsum(wanted.astype(jnp.int32), axis=2) - 1
    slot_ids = jnp.arange(slot_total, dtype=jnp.int32)
    chosen = wanted[:, :, None, :] & (block_ranks[:, :, None, :] == slot_ids[None, None, :, None])
    local_ids = jnp.arange(blocks_own, dtype=jnp.int32)
    positions = jnp.sum(chosen.astype(jnp.int32) * local_ids[None, None, None, :], axis=3)
    present = jnp.any(chosen, axis=3)
    return (positions, present)


def pipeline_kernel(
    sections, owners, batches, first_ref, w_ref, b_ref, slot_ref, next_ref,
    out_ref, *scratch,
):
    recv = scratch[:batches]
    send = scratch[batches:2 * batches]
    send_sem, recv_sem, local_sem = scratch[2 * batches:]
    me_s = lax.axis_index("section")
    me_c = lax.axis_index("col")
    blocks_own = w_ref.shape[0]
    nonzero_count = slot_ref.shape[0] // blocks_own
    barrier = pltpu.get_barrier_semaphore()

    @pl.when(me_s > 0)
    def _():
        for d in range(owners):
            pl.semaphore_signal(barrier, inc=1, device_id=(me_s - 1, d), device_id_type=MESH_ID)

    @pl.when(me_s < sections - 1)
    def _():
        for d in range(owners):
            pl.semaphore_signal(barrier, inc=1, device_id=(me_s + 1, d), device_id_type=MESH_ID)

    peers = owners * (
        (me_s > 0).astype(jnp.int32) + (me_s < sections - 1).astype(jnp.int32)
    )
    pl.semaphore_wait(barrier, peers)

    @pl.when(me_s == 0)
    def _():
        for m in range(batches):
            first = pltpu.make_async_copy(first_ref.at[m], recv[m], local_sem)
            first.start()
            first.wait()

    def outgoing_copy(m, d):
        return pltpu.make_async_remote_copy(
            src_ref=send[m].at[pl.ds(d * CAP, CAP)],
            dst_ref=recv[m].at[pl.ds(me_c * CAP, CAP)],
            send_sem=send_sem.at[m, d],
            recv_sem=recv_sem.at[m, me_c],
            device_id=(me_s + 1, d),
            device_id_type=MESH_ID,
        )

    for m in range(batches):

        @pl.when(me_s > 0)
        def _():
            for e in range(owners):
                pltpu.make_async_remote_copy(
                    src_ref=send[m].at[pl.ds(e * CAP, CAP)],
                    dst_ref=recv[m].at[pl.ds(e * CAP, CAP)],
                    send_sem=send_sem.at[m, e],
                    recv_sem=recv_sem.at[m, e],
                    device_id=(me_s - 1, e),
                    device_id_type=MESH_ID,
                ).wait_recv()

        def block_step(j, carry):
            picked = jnp.concatenate(
                [recv[m][slot_ref[j * nonzero_count + k]] for k in range(nonzero_count)], axis=-1
            )
            acc = jnp.dot(picked, w_ref[j], preferred_element_type=jnp.float32)
            out_ref[m, j] = jnp.clip(acc + b_ref[j], 0.0, 32.0).astype(out_ref.dtype)
            return carry

        lax.fori_loop(0, blocks_own, block_step, 0, unroll=True)

        @pl.when(me_s < sections - 1)
        def _():
            def stage(i, carry):
                send[m][i] = out_ref[m, next_ref[i]]
                return carry

            lax.fori_loop(0, owners * CAP, stage, 0, unroll=True)
            for d in range(owners):
                outgoing_copy(m, d).start()

    @pl.when(me_s < sections - 1)
    def _():
        for m in range(batches):
            for d in range(owners):
                outgoing_copy(m, d).wait_send()


def run_pipeline(first_recv, local_w, local_bias, slot_of, outgoing_next, sections, owners):
    batches = first_recv.shape[0]
    blocks_own = local_w.shape[0]
    rows = first_recv.shape[2]
    block_size = local_w.shape[-1]
    vmem = pl.BlockSpec(memory_space=pltpu.VMEM)
    smem = pl.BlockSpec(memory_space=pltpu.SMEM)
    return pl.pallas_call(
        functools.partial(pipeline_kernel, sections, owners, batches),
        out_shape=jax.ShapeDtypeStruct((batches, blocks_own, rows, block_size), jnp.bfloat16),
        in_specs=[vmem, vmem, vmem, smem, smem],
        out_specs=vmem,
        scratch_shapes=[
            *[pltpu.VMEM(first_recv.shape[1:], jnp.bfloat16) for _ in range(2 * batches)],
            pltpu.SemaphoreType.DMA((batches, owners)),
            pltpu.SemaphoreType.DMA((batches, owners)),
            pltpu.SemaphoreType.DMA(()),
        ],
        compiler_params=pltpu.CompilerParams(collective_id=0, has_side_effects=True),
    )(first_recv, local_w, local_bias, slot_of, outgoing_next)


def pattern_kernel(sections, owners, src_ref, own_ref, nxt_ref, *sems):
    own_send, own_recv, nxt_send, nxt_recv, local_sem = sems
    me_s = lax.axis_index("section")
    me_c = lax.axis_index("col")
    barrier = pltpu.get_barrier_semaphore()
    for d in range(owners):

        @pl.when(me_c != d)
        def _():
            pl.semaphore_signal(barrier, inc=1, device_id=(me_s, d), device_id_type=MESH_ID)

    @pl.when(me_s > 0)
    def _():
        for d in range(owners):
            pl.semaphore_signal(barrier, inc=1, device_id=(me_s - 1, d), device_id_type=MESH_ID)

    @pl.when(me_s < sections - 1)
    def _():
        for d in range(owners):
            pl.semaphore_signal(barrier, inc=1, device_id=(me_s + 1, d), device_id_type=MESH_ID)

    peers = (owners - 1) + owners * (
        (me_s > 0).astype(jnp.int32) + (me_s < sections - 1).astype(jnp.int32)
    )
    pl.semaphore_wait(barrier, peers)

    def own_copy(d, e):
        return pltpu.make_async_remote_copy(
            src_ref=src_ref,
            dst_ref=own_ref.at[e],
            send_sem=own_send.at[d],
            recv_sem=own_recv.at[e],
            device_id=(me_s, d),
            device_id_type=MESH_ID,
        )

    def nxt_copy(dev_s, d, e):
        return pltpu.make_async_remote_copy(
            src_ref=src_ref,
            dst_ref=nxt_ref.at[e],
            send_sem=nxt_send.at[d],
            recv_sem=nxt_recv.at[e],
            device_id=(dev_s, d),
            device_id_type=MESH_ID,
        )

    for d in range(owners):

        @pl.when(me_c != d)
        def _():
            own_copy(d, me_c).start()

    @pl.when(me_s > 0)
    def _():
        for d in range(owners):
            nxt_copy(me_s - 1, d, me_c).start()

    mine = pltpu.make_async_copy(src_ref, own_ref.at[me_c], local_sem)
    mine.start()
    mine.wait()
    for d in range(owners):

        @pl.when(me_c != d)
        def _():
            own_copy(d, me_c).wait_send()
            own_copy(d, d).wait_recv()

    @pl.when(me_s > 0)
    def _():
        for d in range(owners):
            nxt_copy(me_s - 1, d, me_c).wait_send()

    @pl.when(me_s < sections - 1)
    def _():
        for e in range(owners):
            nxt_copy(me_s + 1, e, e).wait_recv()

    @pl.when(me_s == sections - 1)
    def _():
        nxt_ref[...] = jnp.zeros_like(nxt_ref)


def exchange_patterns(local_sources, sections, owners):
    table = jax.ShapeDtypeStruct((owners,) + local_sources.shape, local_sources.dtype)
    vmem = pl.BlockSpec(memory_space=pltpu.VMEM)
    return pl.pallas_call(
        functools.partial(pattern_kernel, sections, owners),
        out_shape=(table, table),
        in_specs=[vmem],
        out_specs=(vmem, vmem),
        scratch_shapes=[pltpu.SemaphoreType.DMA((owners,)) for _ in range(4)]
        + [pltpu.SemaphoreType.DMA(())],
        compiler_params=pltpu.CompilerParams(collective_id=1, has_side_effects=True),
    )(local_sources)


def body(features, weights, sources, bias, batch_rows):
    sections = lax.axis_size("section")
    owners = lax.axis_size("col")
    section_idx = lax.axis_index("section")
    col_idx = lax.axis_index("col")
    local_w = weights[0]
    blocks_own = local_w.shape[0]
    nonzero_count = local_w.shape[1]
    block_size = local_w.shape[2]
    local_src = sources[0].reshape(blocks_own * nonzero_count)
    own_table, next_table = exchange_patterns(sources[0], sections, owners)
    both_positions, both_present = jax.vmap(
        lambda table: request_lists(table, owners, blocks_own, CAP)
    )(jnp.stack([own_table, next_table]))
    positions, present = both_positions[0], both_present[0]
    outgoing = lax.dynamic_index_in_dim(positions, col_idx, 1, keepdims=False)
    outgoing = outgoing.reshape(owners * CAP)
    outgoing_next = lax.dynamic_index_in_dim(both_positions[1], col_idx, 1, keepdims=False)
    outgoing_next = outgoing_next.reshape(owners * CAP)
    incoming = lax.dynamic_index_in_dim(positions, col_idx, 0, keepdims=False)
    incoming_ok = lax.dynamic_index_in_dim(present, col_idx, 0, keepdims=False)
    global_ids = incoming + blocks_own * jnp.arange(owners, dtype=jnp.int32)[:, None]
    matches = (local_src[:, None] == global_ids.reshape(-1)[None, :]) & incoming_ok.reshape(-1)[
        None, :
    ]
    slot_of = jnp.sum(
        matches.astype(jnp.int32) * jnp.arange(owners * CAP, dtype=jnp.int32)[None, :], axis=1
    )
    all_inputs = lax.all_gather(features, "section", axis=1, tiled=True)
    batches = all_inputs.shape[0]
    row_total = all_inputs.shape[1]
    blocks_in = all_inputs.reshape(batches, row_total, blocks_own, block_size)
    blocks_in = blocks_in.transpose(0, 2, 1, 3)
    first_payload = jnp.take(blocks_in, outgoing, axis=1).reshape(
        batches, owners, CAP, row_total, block_size
    )
    first_recv = lax.all_to_all(first_payload, "col", split_axis=1, concat_axis=1, tiled=True)

    first_recv = first_recv.reshape(batches, owners * CAP, row_total, block_size)
    finished = run_pipeline(
        first_recv, local_w.reshape(blocks_own, nonzero_count * block_size, block_size), bias[0].reshape(blocks_own, 1, block_size), slot_of,
        outgoing_next, sections, owners,
    )
    completed = finished.transpose(0, 2, 1, 3).reshape(
        batches, row_total, blocks_own * block_size
    )
    own_rows = row_total // sections
    outgoing_rows = completed.reshape(batches, sections, own_rows, blocks_own * block_size)
    gathered = lax.all_to_all(outgoing_rows, "section", split_axis=1, concat_axis=1, tiled=True)
    own_result = gathered[:, sections - 1]
    row_ids = section_idx * own_rows + jnp.arange(own_rows, dtype=jnp.int32)
    row_mask = row_ids[None, :] < batch_rows[:, None]
    return jnp.where(row_mask[:, :, None], own_result, jnp.zeros_like(own_result))


def solution(mesh):
    in_specs = (
        P(None, "section", "col"),
        P("section", "col", None, None, None),
        P("section", "col", None),
        P("section", "col"),
        P(),
    )
    out_specs = P(None, "section", "col")
    return jax.shard_map(body, mesh=mesh, in_specs=in_specs, out_specs=out_specs, check_vma=False)
```

```python
import functools

import jax
import jax.numpy as jnp
from jax import lax
from jax.experimental import pallas as pl
from jax.experimental.pallas import tpu as pltpu
from jax.sharding import PartitionSpec as P

CAP = 2
MESH_ID = pl.DeviceIdType.MESH


def from_behind(x, axis, by):
    size = lax.axis_size(axis)
    pairs = [(i, i + by) for i in range(size) if 0 <= i + by < size]
    return lax.ppermute(x, axis, pairs)


def request_lists(pattern_table, owners, blocks_own, slot_total):
    dest_entries = pattern_table.reshape(owners, -1)
    block_total = owners * blocks_own
    catalog = jnp.arange(block_total, dtype=jnp.int32)
    wanted = jnp.any(dest_entries[:, :, None] == catalog[None, None, :], axis=1)
    wanted = wanted.reshape(owners, owners, blocks_own)
    block_ranks = jnp.cumsum(wanted.astype(jnp.int32), axis=2) - 1
    slot_ids = jnp.arange(slot_total, dtype=jnp.int32)
    chosen = wanted[:, :, None, :] & (block_ranks[:, :, None, :] == slot_ids[None, None, :, None])
    local_ids = jnp.arange(blocks_own, dtype=jnp.int32)
    positions = jnp.sum(chosen.astype(jnp.int32) * local_ids[None, None, None, :], axis=3)
    present = jnp.any(chosen, axis=3)
    return (positions, present)


def pipeline_kernel(
    sections, owners, batches, first_ref, w_ref, b_ref, slot_ref, next_ref,
    out_ref, *scratch,
):
    recv = scratch[:batches]
    send = scratch[batches:2 * batches]
    send_sem, recv_sem, local_sem = scratch[2 * batches:]
    me_s = lax.axis_index("section")
    me_c = lax.axis_index("col")
    blocks_own = w_ref.shape[0]
    nonzero_count = slot_ref.shape[0] // blocks_own
    barrier = pltpu.get_barrier_semaphore()

    @pl.when(me_s > 0)
    def _():
        for d in range(owners):
            pl.semaphore_signal(barrier, inc=1, device_id=(me_s - 1, d), device_id_type=MESH_ID)

    @pl.when(me_s < sections - 1)
    def _():
        for d in range(owners):
            pl.semaphore_signal(barrier, inc=1, device_id=(me_s + 1, d), device_id_type=MESH_ID)

    peers = owners * (
        (me_s > 0).astype(jnp.int32) + (me_s < sections - 1).astype(jnp.int32)
    )
    pl.semaphore_wait(barrier, peers)

    @pl.when(me_s == 0)
    def _():
        for m in range(batches):
            first = pltpu.make_async_copy(first_ref.at[m], recv[m], local_sem)
            first.start()
            first.wait()

    def outgoing_copy(m, d):
        return pltpu.make_async_remote_copy(
            src_ref=send[m].at[pl.ds(d * CAP, CAP)],
            dst_ref=recv[m].at[pl.ds(me_c * CAP, CAP)],
            send_sem=send_sem.at[m, d],
            recv_sem=recv_sem.at[m, me_c],
            device_id=(me_s + 1, d),
            device_id_type=MESH_ID,
        )

    for m in range(batches):

        @pl.when(me_s > 0)
        def _():
            for e in range(owners):
                pltpu.make_async_remote_copy(
                    src_ref=send[m].at[pl.ds(e * CAP, CAP)],
                    dst_ref=recv[m].at[pl.ds(e * CAP, CAP)],
                    send_sem=send_sem.at[m, e],
                    recv_sem=recv_sem.at[m, e],
                    device_id=(me_s - 1, e),
                    device_id_type=MESH_ID,
                ).wait_recv()

        def block_step(j, carry):
            picked = jnp.concatenate(
                [recv[m][slot_ref[j * nonzero_count + k]] for k in range(nonzero_count)], axis=-1
            )
            acc = jnp.dot(picked, w_ref[j], preferred_element_type=jnp.float32)
            out_ref[m, j] = jnp.clip(acc + b_ref[j], 0.0, 32.0).astype(out_ref.dtype)
            return carry

        lax.fori_loop(0, blocks_own, block_step, 0, unroll=True)

        @pl.when(me_s < sections - 1)
        def _():
            def stage(i, carry):
                send[m][i] = out_ref[m, next_ref[i]]
                return carry

            lax.fori_loop(0, owners * CAP, stage, 0, unroll=True)
            for d in range(owners):
                outgoing_copy(m, d).start()

    @pl.when(me_s < sections - 1)
    def _():
        for m in range(batches):
            for d in range(owners):
                outgoing_copy(m, d).wait_send()


def run_pipeline(first_recv, local_w, local_bias, slot_of, outgoing_next, sections, owners):
    batches = first_recv.shape[0]
    blocks_own = local_w.shape[0]
    rows = first_recv.shape[2]
    block_size = local_w.shape[-1]
    vmem = pl.BlockSpec(memory_space=pltpu.VMEM)
    smem = pl.BlockSpec(memory_space=pltpu.SMEM)
    return pl.pallas_call(
        functools.partial(pipeline_kernel, sections, owners, batches),
        out_shape=jax.ShapeDtypeStruct((batches, blocks_own, rows, block_size), jnp.bfloat16),
        in_specs=[vmem, vmem, vmem, smem, smem],
        out_specs=vmem,
        scratch_shapes=[
            *[pltpu.VMEM(first_recv.shape[1:], jnp.bfloat16) for _ in range(2 * batches)],
            pltpu.SemaphoreType.DMA((batches, owners)),
            pltpu.SemaphoreType.DMA((batches, owners)),
            pltpu.SemaphoreType.DMA(()),
        ],
        compiler_params=pltpu.CompilerParams(collective_id=0, has_side_effects=True),
    )(first_recv, local_w, local_bias, slot_of, outgoing_next)


def pattern_kernel(sections, owners, src_ref, feat_ref, own_ref, nxt_ref, rows_ref, *sems):
    own_send, own_recv, nxt_send, nxt_recv, local_sem, rows_send, rows_recv, rows_sem = sems
    me_s = lax.axis_index("section")
    me_c = lax.axis_index("col")
    barrier = pltpu.get_barrier_semaphore()
    for d in range(owners):

        @pl.when(me_c != d)
        def _():
            pl.semaphore_signal(barrier, inc=1, device_id=(me_s, d), device_id_type=MESH_ID)

    @pl.when(me_s > 0)
    def _():
        for d in range(owners):
            pl.semaphore_signal(barrier, inc=1, device_id=(me_s - 1, d), device_id_type=MESH_ID)

    @pl.when(me_s < sections - 1)
    def _():
        for d in range(owners):
            pl.semaphore_signal(barrier, inc=1, device_id=(me_s + 1, d), device_id_type=MESH_ID)

    @pl.when(me_s > 0)
    def _():
        pl.semaphore_signal(barrier, inc=1, device_id=(0, me_c), device_id_type=MESH_ID)

    @pl.when(me_s == 0)
    def _():
        for r in range(1, sections):
            pl.semaphore_signal(barrier, inc=1, device_id=(r, me_c), device_id_type=MESH_ID)

    is_first = (me_s == 0).astype(jnp.int32)
    peers = (owners - 1) + owners * (
        (me_s > 0).astype(jnp.int32) + (me_s < sections - 1).astype(jnp.int32)
    ) + is_first * (sections - 1) + (1 - is_first)
    pl.semaphore_wait(barrier, peers)

    def own_copy(d, e):
        return pltpu.make_async_remote_copy(
            src_ref=src_ref,
            dst_ref=own_ref.at[e],
            send_sem=own_send.at[d],
            recv_sem=own_recv.at[e],
            device_id=(me_s, d),
            device_id_type=MESH_ID,
        )

    def nxt_copy(dev_s, d, e):
        return pltpu.make_async_remote_copy(
            src_ref=src_ref,
            dst_ref=nxt_ref.at[e],
            send_sem=nxt_send.at[d],
            recv_sem=nxt_recv.at[e],
            device_id=(dev_s, d),
            device_id_type=MESH_ID,
        )

    for d in range(owners):

        @pl.when(me_c != d)
        def _():
            own_copy(d, me_c).start()

    @pl.when(me_s > 0)
    def _():
        for d in range(owners):
            nxt_copy(me_s - 1, d, me_c).start()

    def rows_copy(r):
        return pltpu.make_async_remote_copy(
            src_ref=feat_ref,
            dst_ref=rows_ref.at[r],
            send_sem=rows_send,
            recv_sem=rows_recv.at[r],
            device_id=(0, me_c),
            device_id_type=MESH_ID,
        )

    @pl.when(me_s > 0)
    def _():
        rows_copy(me_s).start()

    @pl.when(me_s == 0)
    def _():
        own_rows = pltpu.make_async_copy(feat_ref, rows_ref.at[0], rows_sem)
        own_rows.start()
        own_rows.wait()

    mine = pltpu.make_async_copy(src_ref, own_ref.at[me_c], local_sem)
    mine.start()
    mine.wait()
    for d in range(owners):

        @pl.when(me_c != d)
        def _():
            own_copy(d, me_c).wait_send()
            own_copy(d, d).wait_recv()

    @pl.when(me_s > 0)
    def _():
        for d in range(owners):
            nxt_copy(me_s - 1, d, me_c).wait_send()

    @pl.when(me_s < sections - 1)
    def _():
        for e in range(owners):
            nxt_copy(me_s + 1, e, e).wait_recv()

    @pl.when(me_s == sections - 1)
    def _():
        nxt_ref[...] = jnp.zeros_like(nxt_ref)

    @pl.when(me_s > 0)
    def _():
        rows_copy(me_s).wait_send()
        rows_ref[...] = jnp.zeros_like(rows_ref)

    @pl.when(me_s == 0)
    def _():
        for r in range(1, sections):
            rows_copy(r).wait_recv()


def exchange_patterns(local_sources, features, sections, owners):
    table = jax.ShapeDtypeStruct((owners,) + local_sources.shape, local_sources.dtype)
    rows = jax.ShapeDtypeStruct((sections,) + features.shape, features.dtype)
    vmem = pl.BlockSpec(memory_space=pltpu.VMEM)
    return pl.pallas_call(
        functools.partial(pattern_kernel, sections, owners),
        out_shape=(table, table, rows),
        in_specs=[vmem, vmem],
        out_specs=(vmem, vmem, vmem),
        scratch_shapes=[pltpu.SemaphoreType.DMA((owners,)) for _ in range(4)]
        + [
            pltpu.SemaphoreType.DMA(()),
            pltpu.SemaphoreType.DMA(()),
            pltpu.SemaphoreType.DMA((sections,)),
            pltpu.SemaphoreType.DMA(()),
        ],
        compiler_params=pltpu.CompilerParams(collective_id=1, has_side_effects=True),
    )(local_sources, features)


def body(features, weights, sources, bias, batch_rows):
    sections = lax.axis_size("section")
    owners = lax.axis_size("col")
    section_idx = lax.axis_index("section")
    col_idx = lax.axis_index("col")
    local_w = weights[0]
    blocks_own = local_w.shape[0]
    nonzero_count = local_w.shape[1]
    block_size = local_w.shape[2]
    local_src = sources[0].reshape(blocks_own * nonzero_count)
    own_table, next_table, row_parts = exchange_patterns(sources[0], features, sections, owners)
    both_positions, both_present = jax.vmap(
        lambda table: request_lists(table, owners, blocks_own, CAP)
    )(jnp.stack([own_table, next_table]))
    positions, present = both_positions[0], both_present[0]
    outgoing = lax.dynamic_index_in_dim(positions, col_idx, 1, keepdims=False)
    outgoing = outgoing.reshape(owners * CAP)
    outgoing_next = lax.dynamic_index_in_dim(both_positions[1], col_idx, 1, keepdims=False)
    outgoing_next = outgoing_next.reshape(owners * CAP)
    incoming = lax.dynamic_index_in_dim(positions, col_idx, 0, keepdims=False)
    incoming_ok = lax.dynamic_index_in_dim(present, col_idx, 0, keepdims=False)
    global_ids = incoming + blocks_own * jnp.arange(owners, dtype=jnp.int32)[:, None]
    matches = (local_src[:, None] == global_ids.reshape(-1)[None, :]) & incoming_ok.reshape(-1)[
        None, :
    ]
    slot_of = jnp.sum(
        matches.astype(jnp.int32) * jnp.arange(owners * CAP, dtype=jnp.int32)[None, :], axis=1
    )
    batches = features.shape[0]
    row_total = features.shape[1] * sections
    all_inputs = row_parts.transpose(1, 0, 2, 3).reshape(batches, row_total, -1)
    blocks_in = all_inputs.reshape(batches, row_total, blocks_own, block_size)
    blocks_in = blocks_in.transpose(0, 2, 1, 3)
    first_payload = jnp.take(blocks_in, outgoing, axis=1).reshape(
        batches, owners, CAP, row_total, block_size
    )
    first_recv = lax.all_to_all(first_payload, "col", split_axis=1, concat_axis=1, tiled=True)

    first_recv = first_recv.reshape(batches, owners * CAP, row_total, block_size)
    finished = run_pipeline(
        first_recv, local_w.reshape(blocks_own, nonzero_count * block_size, block_size), bias[0].reshape(blocks_own, 1, block_size), slot_of,
        outgoing_next, sections, owners,
    )
    completed = finished.transpose(0, 2, 1, 3).reshape(
        batches, row_total, blocks_own * block_size
    )
    own_rows = row_total // sections
    outgoing_rows = completed.reshape(batches, sections, own_rows, blocks_own * block_size)
    gathered = lax.all_to_all(outgoing_rows, "section", split_axis=1, concat_axis=1, tiled=True)
    own_result = gathered[:, sections - 1]
    row_ids = section_idx * own_rows + jnp.arange(own_rows, dtype=jnp.int32)
    row_mask = row_ids[None, :] < batch_rows[:, None]
    return jnp.where(row_mask[:, :, None], own_result, jnp.zeros_like(own_result))


def solution(mesh):
    in_specs = (
        P(None, "section", "col"),
        P("section", "col", None, None, None),
        P("section", "col", None),
        P("section", "col"),
        P(),
    )
    out_specs = P(None, "section", "col")
    return jax.shard_map(body, mesh=mesh, in_specs=in_specs, out_specs=out_specs, check_vma=False)
```

```python
import functools

import jax
import jax.numpy as jnp
from jax import lax
from jax.experimental import pallas as pl
from jax.experimental.pallas import tpu as pltpu
from jax.sharding import PartitionSpec as P

CAP = 2
MESH_ID = pl.DeviceIdType.MESH


def from_behind(x, axis, by):
    size = lax.axis_size(axis)
    pairs = [(i, i + by) for i in range(size) if 0 <= i + by < size]
    return lax.ppermute(x, axis, pairs)


def request_lists(pattern_table, owners, blocks_own, slot_total):
    dest_entries = pattern_table.reshape(owners, -1)
    block_total = owners * blocks_own
    catalog = jnp.arange(block_total, dtype=jnp.int32)
    wanted = jnp.any(dest_entries[:, :, None] == catalog[None, None, :], axis=1)
    wanted = wanted.reshape(owners, owners, blocks_own)
    block_ranks = jnp.cumsum(wanted.astype(jnp.int32), axis=2) - 1
    slot_ids = jnp.arange(slot_total, dtype=jnp.int32)
    chosen = wanted[:, :, None, :] & (block_ranks[:, :, None, :] == slot_ids[None, None, :, None])
    local_ids = jnp.arange(blocks_own, dtype=jnp.int32)
    positions = jnp.sum(chosen.astype(jnp.int32) * local_ids[None, None, None, :], axis=3)
    present = jnp.any(chosen, axis=3)
    return (positions, present)


def pipeline_kernel(
    sections, owners, batches, first_ref, w_ref, b_ref, slot_ref, next_ref,
    out_ref, *scratch,
):
    recv = scratch[:batches]
    send = scratch[batches:2 * batches]
    send_sem, recv_sem, local_sem = scratch[2 * batches:]
    me_s = lax.axis_index("section")
    me_c = lax.axis_index("col")
    blocks_own = w_ref.shape[0]
    nonzero_count = slot_ref.shape[0] // blocks_own
    barrier = pltpu.get_barrier_semaphore()

    @pl.when(me_s > 0)
    def _():
        for d in range(owners):
            pl.semaphore_signal(barrier, inc=1, device_id=(me_s - 1, d), device_id_type=MESH_ID)

    @pl.when(me_s < sections - 1)
    def _():
        for d in range(owners):
            pl.semaphore_signal(barrier, inc=1, device_id=(me_s + 1, d), device_id_type=MESH_ID)

    peers = owners * (
        (me_s > 0).astype(jnp.int32) + (me_s < sections - 1).astype(jnp.int32)
    )
    pl.semaphore_wait(barrier, peers)

    @pl.when(me_s == 0)
    def _():
        for m in range(batches):
            first = pltpu.make_async_copy(first_ref.at[m], recv[m], local_sem)
            first.start()
            first.wait()

    def outgoing_copy(m, d):
        return pltpu.make_async_remote_copy(
            src_ref=send[m].at[pl.ds(d * CAP, CAP)],
            dst_ref=recv[m].at[pl.ds(me_c * CAP, CAP)],
            send_sem=send_sem.at[m, d],
            recv_sem=recv_sem.at[m, me_c],
            device_id=(me_s + 1, d),
            device_id_type=MESH_ID,
        )

    for m in range(batches):

        @pl.when(me_s > 0)
        def _():
            for e in range(owners):
                pltpu.make_async_remote_copy(
                    src_ref=send[m].at[pl.ds(e * CAP, CAP)],
                    dst_ref=recv[m].at[pl.ds(e * CAP, CAP)],
                    send_sem=send_sem.at[m, e],
                    recv_sem=recv_sem.at[m, e],
                    device_id=(me_s - 1, e),
                    device_id_type=MESH_ID,
                ).wait_recv()

        def block_step(j, carry):
            picked = jnp.concatenate(
                [recv[m][slot_ref[j * nonzero_count + k]] for k in range(nonzero_count)], axis=-1
            )
            acc = jnp.dot(picked, w_ref[j], preferred_element_type=jnp.float32)
            out_ref[m, j] = jnp.clip(acc + b_ref[j], 0.0, 32.0).astype(out_ref.dtype)
            return carry

        lax.fori_loop(0, blocks_own, block_step, 0, unroll=True)

        @pl.when(me_s < sections - 1)
        def _():
            def stage(i, carry):
                send[m][i] = out_ref[m, next_ref[i]]
                return carry

            lax.fori_loop(0, owners * CAP, stage, 0, unroll=True)
            for d in range(owners):
                outgoing_copy(m, d).start()

    @pl.when(me_s < sections - 1)
    def _():
        for m in range(batches):
            for d in range(owners):
                outgoing_copy(m, d).wait_send()


def run_pipeline(first_recv, local_w, local_bias, slot_of, outgoing_next, sections, owners):
    batches = first_recv.shape[0]
    blocks_own = local_w.shape[0]
    rows = first_recv.shape[2]
    block_size = local_w.shape[-1]
    vmem = pl.BlockSpec(memory_space=pltpu.VMEM)
    smem = pl.BlockSpec(memory_space=pltpu.SMEM)
    return pl.pallas_call(
        functools.partial(pipeline_kernel, sections, owners, batches),
        out_shape=jax.ShapeDtypeStruct((batches, blocks_own, rows, block_size), jnp.bfloat16),
        in_specs=[vmem, vmem, vmem, smem, smem],
        out_specs=vmem,
        scratch_shapes=[
            *[pltpu.VMEM(first_recv.shape[1:], jnp.bfloat16) for _ in range(2 * batches)],
            pltpu.SemaphoreType.DMA((batches, owners)),
            pltpu.SemaphoreType.DMA((batches, owners)),
            pltpu.SemaphoreType.DMA(()),
        ],
        compiler_params=pltpu.CompilerParams(collective_id=0, has_side_effects=True),
    )(first_recv, local_w, local_bias, slot_of, outgoing_next)


def pattern_kernel(sections, owners, src_ref, feat_ref, own_ref, nxt_ref, rows_ref, *sems):
    own_send, own_recv, nxt_send, nxt_recv, local_sem, rows_send, rows_recv, rows_sem = sems
    me_s = lax.axis_index("section")
    me_c = lax.axis_index("col")
    barrier = pltpu.get_barrier_semaphore()
    for d in range(owners):

        @pl.when(me_c != d)
        def _():
            pl.semaphore_signal(barrier, inc=1, device_id=(me_s, d), device_id_type=MESH_ID)

    @pl.when(me_s > 0)
    def _():
        for d in range(owners):
            pl.semaphore_signal(barrier, inc=1, device_id=(me_s - 1, d), device_id_type=MESH_ID)

    @pl.when(me_s < sections - 1)
    def _():
        for d in range(owners):
            pl.semaphore_signal(barrier, inc=1, device_id=(me_s + 1, d), device_id_type=MESH_ID)

    @pl.when(me_s > 0)
    def _():
        pl.semaphore_signal(barrier, inc=1, device_id=(0, me_c), device_id_type=MESH_ID)

    @pl.when(me_s == 0)
    def _():
        for r in range(1, sections):
            pl.semaphore_signal(barrier, inc=1, device_id=(r, me_c), device_id_type=MESH_ID)

    is_first = (me_s == 0).astype(jnp.int32)
    peers = (owners - 1) + owners * (
        (me_s > 0).astype(jnp.int32) + (me_s < sections - 1).astype(jnp.int32)
    ) + is_first * (sections - 1) + (1 - is_first)
    pl.semaphore_wait(barrier, peers)

    def own_copy(d, e):
        return pltpu.make_async_remote_copy(
            src_ref=src_ref,
            dst_ref=own_ref.at[e],
            send_sem=own_send.at[d],
            recv_sem=own_recv.at[e],
            device_id=(me_s, d),
            device_id_type=MESH_ID,
        )

    def nxt_copy(dev_s, d, e):
        return pltpu.make_async_remote_copy(
            src_ref=src_ref,
            dst_ref=nxt_ref.at[e],
            send_sem=nxt_send.at[d],
            recv_sem=nxt_recv.at[e],
            device_id=(dev_s, d),
            device_id_type=MESH_ID,
        )

    for d in range(owners):

        @pl.when(me_c != d)
        def _():
            own_copy(d, me_c).start()

    @pl.when(me_s > 0)
    def _():
        for d in range(owners):
            nxt_copy(me_s - 1, d, me_c).start()

    def rows_copy(r):
        return pltpu.make_async_remote_copy(
            src_ref=feat_ref,
            dst_ref=rows_ref.at[r],
            send_sem=rows_send,
            recv_sem=rows_recv.at[r],
            device_id=(0, me_c),
            device_id_type=MESH_ID,
        )

    @pl.when(me_s > 0)
    def _():
        rows_copy(me_s).start()

    @pl.when(me_s == 0)
    def _():
        own_rows = pltpu.make_async_copy(feat_ref, rows_ref.at[0], rows_sem)
        own_rows.start()
        own_rows.wait()

    mine = pltpu.make_async_copy(src_ref, own_ref.at[me_c], local_sem)
    mine.start()
    mine.wait()
    for d in range(owners):

        @pl.when(me_c != d)
        def _():
            own_copy(d, me_c).wait_send()
            own_copy(d, d).wait_recv()

    @pl.when(me_s > 0)
    def _():
        for d in range(owners):
            nxt_copy(me_s - 1, d, me_c).wait_send()

    @pl.when(me_s < sections - 1)
    def _():
        for e in range(owners):
            nxt_copy(me_s + 1, e, e).wait_recv()

    @pl.when(me_s == sections - 1)
    def _():
        nxt_ref[...] = jnp.zeros_like(nxt_ref)

    @pl.when(me_s > 0)
    def _():
        rows_copy(me_s).wait_send()
        rows_ref[...] = jnp.zeros_like(rows_ref)

    @pl.when(me_s == 0)
    def _():
        for r in range(1, sections):
            rows_copy(r).wait_recv()


def exchange_patterns(local_sources, features, sections, owners):
    table = jax.ShapeDtypeStruct((owners,) + local_sources.shape, local_sources.dtype)
    rows = jax.ShapeDtypeStruct((sections,) + features.shape, features.dtype)
    vmem = pl.BlockSpec(memory_space=pltpu.VMEM)
    return pl.pallas_call(
        functools.partial(pattern_kernel, sections, owners),
        out_shape=(table, table, rows),
        in_specs=[vmem, vmem],
        out_specs=(vmem, vmem, vmem),
        scratch_shapes=[pltpu.SemaphoreType.DMA((owners,)) for _ in range(4)]
        + [
            pltpu.SemaphoreType.DMA(()),
            pltpu.SemaphoreType.DMA(()),
            pltpu.SemaphoreType.DMA((sections,)),
            pltpu.SemaphoreType.DMA(()),
        ],
        compiler_params=pltpu.CompilerParams(collective_id=1, has_side_effects=True),
    )(local_sources, features)


def body(features, weights, sources, bias, batch_rows):
    sections = lax.axis_size("section")
    owners = lax.axis_size("col")
    section_idx = lax.axis_index("section")
    col_idx = lax.axis_index("col")
    local_w = weights[0]
    blocks_own = local_w.shape[0]
    nonzero_count = local_w.shape[1]
    block_size = local_w.shape[2]
    local_src = sources[0].reshape(blocks_own * nonzero_count)
    own_table, next_table, row_parts = exchange_patterns(sources[0], features, sections, owners)
    both_positions, both_present = jax.vmap(
        lambda table: request_lists(table, owners, blocks_own, CAP)
    )(jnp.stack([own_table, next_table]))
    positions, present = both_positions[0], both_present[0]
    outgoing = lax.dynamic_index_in_dim(positions, col_idx, 1, keepdims=False)
    outgoing = outgoing.reshape(owners * CAP)
    outgoing_next = lax.dynamic_index_in_dim(both_positions[1], col_idx, 1, keepdims=False)
    outgoing_next = outgoing_next.reshape(owners * CAP)
    incoming = lax.dynamic_index_in_dim(positions, col_idx, 0, keepdims=False)
    incoming_ok = lax.dynamic_index_in_dim(present, col_idx, 0, keepdims=False)
    global_ids = incoming + blocks_own * jnp.arange(owners, dtype=jnp.int32)[:, None]
    matches = (local_src[:, None] == global_ids.reshape(-1)[None, :]) & incoming_ok.reshape(-1)[
        None, :
    ]
    slot_of = jnp.sum(
        matches.astype(jnp.int32) * jnp.arange(owners * CAP, dtype=jnp.int32)[None, :], axis=1
    )
    batches = features.shape[0]
    row_total = features.shape[1] * sections
    all_inputs = row_parts.transpose(1, 0, 2, 3).reshape(batches, row_total, -1)
    blocks_in = all_inputs.reshape(batches, row_total, blocks_own, block_size)
    blocks_in = blocks_in.transpose(0, 2, 1, 3)
    first_payload = jnp.take(blocks_in, outgoing, axis=1).reshape(
        batches, owners, CAP, row_total, block_size
    )
    first_recv = lax.all_to_all(first_payload, "col", split_axis=1, concat_axis=1, tiled=True)

    piece_rows = 16
    splits = row_total // piece_rows
    first_recv = first_recv.reshape(batches, owners * CAP, splits, piece_rows, block_size)
    first_recv = first_recv.transpose(0, 2, 1, 3, 4).reshape(
        batches * splits, owners * CAP, piece_rows, block_size
    )
    finished = run_pipeline(
        first_recv, local_w.reshape(blocks_own, nonzero_count * block_size, block_size), bias[0].reshape(blocks_own, 1, block_size), slot_of,
        outgoing_next, sections, owners,
    )
    finished = finished.reshape(batches, splits, blocks_own, piece_rows, block_size)
    completed = finished.transpose(0, 1, 3, 2, 4).reshape(
        batches, row_total, blocks_own * block_size
    )
    own_rows = row_total // sections
    outgoing_rows = completed.reshape(batches, sections, own_rows, blocks_own * block_size)
    gathered = lax.all_to_all(outgoing_rows, "section", split_axis=1, concat_axis=1, tiled=True)
    own_result = gathered[:, sections - 1]
    row_ids = section_idx * own_rows + jnp.arange(own_rows, dtype=jnp.int32)
    row_mask = row_ids[None, :] < batch_rows[:, None]
    return jnp.where(row_mask[:, :, None], own_result, jnp.zeros_like(own_result))


def solution(mesh):
    in_specs = (
        P(None, "section", "col"),
        P("section", "col", None, None, None),
        P("section", "col", None),
        P("section", "col"),
        P(),
    )
    out_specs = P(None, "section", "col")
    return jax.shard_map(body, mesh=mesh, in_specs=in_specs, out_specs=out_specs, check_vma=False)
```

```python
import functools

import jax
import jax.numpy as jnp
from jax import lax
from jax.experimental import pallas as pl
from jax.experimental.pallas import tpu as pltpu
from jax.sharding import PartitionSpec as P

CAP = 2
MESH_ID = pl.DeviceIdType.MESH


def from_behind(x, axis, by):
    size = lax.axis_size(axis)
    pairs = [(i, i + by) for i in range(size) if 0 <= i + by < size]
    return lax.ppermute(x, axis, pairs)


def request_lists(pattern_table, owners, blocks_own, slot_total):
    dest_entries = pattern_table.reshape(owners, -1)
    block_total = owners * blocks_own
    catalog = jnp.arange(block_total, dtype=jnp.int32)
    wanted = jnp.any(dest_entries[:, :, None] == catalog[None, None, :], axis=1)
    wanted = wanted.reshape(owners, owners, blocks_own)
    local_rows = jnp.arange(blocks_own, dtype=jnp.int32)
    below = local_rows[:, None] <= local_rows[None, :]
    block_ranks = jnp.einsum(
        "abi,ij->abj", wanted.astype(jnp.float32), below.astype(jnp.float32)
    ).astype(jnp.int32) - 1
    slot_ids = jnp.arange(slot_total, dtype=jnp.int32)
    chosen = wanted[:, :, None, :] & (block_ranks[:, :, None, :] == slot_ids[None, None, :, None])
    local_ids = jnp.arange(blocks_own, dtype=jnp.int32)
    positions = jnp.sum(chosen.astype(jnp.int32) * local_ids[None, None, None, :], axis=3)
    present = jnp.any(chosen, axis=3)
    return (positions, present)


def pipeline_kernel(
    sections, owners, batches, first_ref, w_ref, b_ref, slot_ref, next_ref, first_list_ref,
    out_ref, *scratch,
):
    recv = scratch[:batches]
    send = scratch[batches:2 * batches]
    send0 = scratch[2 * batches:3 * batches]
    send_sem, recv_sem, local_sem, send0_sem = scratch[3 * batches:]
    me_s = lax.axis_index("section")
    me_c = lax.axis_index("col")
    blocks_own = w_ref.shape[0]
    nonzero_count = slot_ref.shape[0] // blocks_own
    barrier = pltpu.get_barrier_semaphore()

    @pl.when(me_s > 0)
    def _():
        for d in range(owners):
            pl.semaphore_signal(barrier, inc=1, device_id=(me_s - 1, d), device_id_type=MESH_ID)

    @pl.when(me_s < sections - 1)
    def _():
        for d in range(owners):
            pl.semaphore_signal(barrier, inc=1, device_id=(me_s + 1, d), device_id_type=MESH_ID)

    @pl.when(me_s == 0)
    def _():
        for d in range(owners):

            @pl.when(me_c != d)
            def _():
                pl.semaphore_signal(barrier, inc=1, device_id=(0, d), device_id_type=MESH_ID)

    is_first = (me_s == 0).astype(jnp.int32)
    peers = owners * (
        (me_s > 0).astype(jnp.int32) + (me_s < sections - 1).astype(jnp.int32)
    ) + is_first * (owners - 1)
    pl.semaphore_wait(barrier, peers)

    def first_copy(m, d):
        return pltpu.make_async_remote_copy(
            src_ref=send0[m].at[pl.ds(d * CAP, CAP)],
            dst_ref=recv[m].at[pl.ds(me_c * CAP, CAP)],
            send_sem=send0_sem.at[m, d],
            recv_sem=recv_sem.at[m, me_c],
            device_id=(0, d),
            device_id_type=MESH_ID,
        )

    def first_local(m):
        return pltpu.make_async_copy(
            send0[m].at[pl.ds(me_c * CAP, CAP)],
            recv[m].at[pl.ds(me_c * CAP, CAP)],
            local_sem.at[m],
        )

    @pl.when(me_s == 0)
    def _():
        for m in range(batches):

            def stage_first(i, carry):
                send0[m][i] = first_ref[m, first_list_ref[i]]
                return carry

            lax.fori_loop(0, owners * CAP, stage_first, 0, unroll=True)
            for d in range(owners):

                @pl.when(me_c != d)
                def _():
                    first_copy(m, d).start()

            first_local(m).start()

    def outgoing_copy(m, d):
        return pltpu.make_async_remote_copy(
            src_ref=send[m].at[pl.ds(d * CAP, CAP)],
            dst_ref=recv[m].at[pl.ds(me_c * CAP, CAP)],
            send_sem=send_sem.at[m, d],
            recv_sem=recv_sem.at[m, me_c],
            device_id=(me_s + 1, d),
            device_id_type=MESH_ID,
        )

    for m in range(batches):

        @pl.when(me_s == 0)
        def _():
            first_local(m).wait()
            for e in range(owners):

                @pl.when(me_c != e)
                def _():
                    pltpu.make_async_remote_copy(
                        src_ref=send0[m].at[pl.ds(e * CAP, CAP)],
                        dst_ref=recv[m].at[pl.ds(e * CAP, CAP)],
                        send_sem=send0_sem.at[m, e],
                        recv_sem=recv_sem.at[m, e],
                        device_id=(0, e),
                        device_id_type=MESH_ID,
                    ).wait_recv()

        @pl.when(me_s > 0)
        def _():
            for e in range(owners):
                pltpu.make_async_remote_copy(
                    src_ref=send[m].at[pl.ds(e * CAP, CAP)],
                    dst_ref=recv[m].at[pl.ds(e * CAP, CAP)],
                    send_sem=send_sem.at[m, e],
                    recv_sem=recv_sem.at[m, e],
                    device_id=(me_s - 1, e),
                    device_id_type=MESH_ID,
                ).wait_recv()

        def block_step(j, carry):
            picked = jnp.concatenate(
                [recv[m][slot_ref[j * nonzero_count + k]] for k in range(nonzero_count)], axis=-1
            )
            acc = jnp.dot(picked, w_ref[j], preferred_element_type=jnp.float32)
            out_ref[m, j] = jnp.clip(acc + b_ref[j], 0.0, 32.0).astype(out_ref.dtype)
            return carry

        lax.fori_loop(0, blocks_own, block_step, 0, unroll=True)

        @pl.when(me_s < sections - 1)
        def _():
            def stage(i, carry):
                send[m][i] = out_ref[m, next_ref[i]]
                return carry

            lax.fori_loop(0, owners * CAP, stage, 0, unroll=True)
            for d in range(owners):
                outgoing_copy(m, d).start()

    @pl.when(me_s < sections - 1)
    def _():
        for m in range(batches):
            for d in range(owners):
                outgoing_copy(m, d).wait_send()

    @pl.when(me_s == 0)
    def _():
        for m in range(batches):
            for d in range(owners):

                @pl.when(me_c != d)
                def _():
                    first_copy(m, d).wait_send()


def run_pipeline(
    first_blocks, local_w, local_bias, slot_of, outgoing_next, outgoing, sections, owners
):
    batches = first_blocks.shape[0]
    blocks_own = local_w.shape[0]
    rows = first_blocks.shape[2]
    slots_shape = (owners * CAP,) + first_blocks.shape[2:]
    block_size = local_w.shape[-1]
    vmem = pl.BlockSpec(memory_space=pltpu.VMEM)
    smem = pl.BlockSpec(memory_space=pltpu.SMEM)
    return pl.pallas_call(
        functools.partial(pipeline_kernel, sections, owners, batches),
        out_shape=jax.ShapeDtypeStruct((batches, blocks_own, rows, block_size), jnp.bfloat16),
        in_specs=[vmem, vmem, vmem, smem, smem, smem],
        out_specs=vmem,
        scratch_shapes=[
            *[pltpu.VMEM(slots_shape, jnp.bfloat16) for _ in range(3 * batches)],
            pltpu.SemaphoreType.DMA((batches, owners)),
            pltpu.SemaphoreType.DMA((batches, owners)),
            pltpu.SemaphoreType.DMA((batches,)),
            pltpu.SemaphoreType.DMA((batches, owners)),
        ],
        compiler_params=pltpu.CompilerParams(collective_id=0, has_side_effects=True),
    )(first_blocks, local_w, local_bias, slot_of, outgoing_next, outgoing)


def pattern_kernel(sections, owners, src_ref, feat_ref, own_ref, nxt_ref, rows_ref, *sems):
    own_send, own_recv, nxt_send, nxt_recv, local_sem, rows_send, rows_recv, rows_sem = sems
    me_s = lax.axis_index("section")
    me_c = lax.axis_index("col")
    barrier = pltpu.get_barrier_semaphore()
    for d in range(owners):

        @pl.when(me_c != d)
        def _():
            pl.semaphore_signal(barrier, inc=1, device_id=(me_s, d), device_id_type=MESH_ID)

    @pl.when(me_s > 0)
    def _():
        for d in range(owners):
            pl.semaphore_signal(barrier, inc=1, device_id=(me_s - 1, d), device_id_type=MESH_ID)

    @pl.when(me_s < sections - 1)
    def _():
        for d in range(owners):
            pl.semaphore_signal(barrier, inc=1, device_id=(me_s + 1, d), device_id_type=MESH_ID)

    @pl.when(me_s > 0)
    def _():
        pl.semaphore_signal(barrier, inc=1, device_id=(0, me_c), device_id_type=MESH_ID)

    @pl.when(me_s == 0)
    def _():
        for r in range(1, sections):
            pl.semaphore_signal(barrier, inc=1, device_id=(r, me_c), device_id_type=MESH_ID)

    is_first = (me_s == 0).astype(jnp.int32)
    peers = (owners - 1) + owners * (
        (me_s > 0).astype(jnp.int32) + (me_s < sections - 1).astype(jnp.int32)
    ) + is_first * (sections - 1) + (1 - is_first)
    pl.semaphore_wait(barrier, peers)

    def own_copy(d, e):
        return pltpu.make_async_remote_copy(
            src_ref=src_ref,
            dst_ref=own_ref.at[e],
            send_sem=own_send.at[d],
            recv_sem=own_recv.at[e],
            device_id=(me_s, d),
            device_id_type=MESH_ID,
        )

    def nxt_copy(dev_s, d, e):
        return pltpu.make_async_remote_copy(
            src_ref=src_ref,
            dst_ref=nxt_ref.at[e],
            send_sem=nxt_send.at[d],
            recv_sem=nxt_recv.at[e],
            device_id=(dev_s, d),
            device_id_type=MESH_ID,
        )

    for d in range(owners):

        @pl.when(me_c != d)
        def _():
            own_copy(d, me_c).start()

    @pl.when(me_s > 0)
    def _():
        for d in range(owners):
            nxt_copy(me_s - 1, d, me_c).start()

    def rows_copy(r):
        return pltpu.make_async_remote_copy(
            src_ref=feat_ref,
            dst_ref=rows_ref.at[r],
            send_sem=rows_send,
            recv_sem=rows_recv.at[r],
            device_id=(0, me_c),
            device_id_type=MESH_ID,
        )

    @pl.when(me_s > 0)
    def _():
        rows_copy(me_s).start()

    @pl.when(me_s == 0)
    def _():
        own_rows = pltpu.make_async_copy(feat_ref, rows_ref.at[0], rows_sem)
        own_rows.start()
        own_rows.wait()

    mine = pltpu.make_async_copy(src_ref, own_ref.at[me_c], local_sem)
    mine.start()
    mine.wait()
    for d in range(owners):

        @pl.when(me_c != d)
        def _():
            own_copy(d, me_c).wait_send()
            own_copy(d, d).wait_recv()

    @pl.when(me_s > 0)
    def _():
        for d in range(owners):
            nxt_copy(me_s - 1, d, me_c).wait_send()

    @pl.when(me_s < sections - 1)
    def _():
        for e in range(owners):
            nxt_copy(me_s + 1, e, e).wait_recv()

    @pl.when(me_s == sections - 1)
    def _():
        nxt_ref[...] = jnp.zeros_like(nxt_ref)

    @pl.when(me_s > 0)
    def _():
        rows_copy(me_s).wait_send()
        rows_ref[...] = jnp.zeros_like(rows_ref)

    @pl.when(me_s == 0)
    def _():
        for r in range(1, sections):
            rows_copy(r).wait_recv()


def exchange_patterns(local_sources, features, sections, owners):
    table = jax.ShapeDtypeStruct((owners,) + local_sources.shape, local_sources.dtype)
    rows = jax.ShapeDtypeStruct((sections,) + features.shape, features.dtype)
    vmem = pl.BlockSpec(memory_space=pltpu.VMEM)
    return pl.pallas_call(
        functools.partial(pattern_kernel, sections, owners),
        out_shape=(table, table, rows),
        in_specs=[vmem, vmem],
        out_specs=(vmem, vmem, vmem),
        scratch_shapes=[pltpu.SemaphoreType.DMA((owners,)) for _ in range(4)]
        + [
            pltpu.SemaphoreType.DMA(()),
            pltpu.SemaphoreType.DMA(()),
            pltpu.SemaphoreType.DMA((sections,)),
            pltpu.SemaphoreType.DMA(()),
        ],
        compiler_params=pltpu.CompilerParams(collective_id=1, has_side_effects=True),
    )(local_sources, features)


def body(features, weights, sources, bias, batch_rows):
    sections = lax.axis_size("section")
    owners = lax.axis_size("col")
    section_idx = lax.axis_index("section")
    col_idx = lax.axis_index("col")
    local_w = weights[0]
    blocks_own = local_w.shape[0]
    nonzero_count = local_w.shape[1]
    block_size = local_w.shape[2]
    local_src = sources[0].reshape(blocks_own * nonzero_count)
    own_table, next_table, row_parts = exchange_patterns(sources[0], features, sections, owners)
    both_positions, both_present = jax.vmap(
        lambda table: request_lists(table, owners, blocks_own, CAP)
    )(jnp.stack([own_table, next_table]))
    positions, present = both_positions[0], both_present[0]
    outgoing = lax.dynamic_index_in_dim(positions, col_idx, 1, keepdims=False)
    outgoing = outgoing.reshape(owners * CAP)
    outgoing_next = lax.dynamic_index_in_dim(both_positions[1], col_idx, 1, keepdims=False)
    outgoing_next = outgoing_next.reshape(owners * CAP)
    incoming = lax.dynamic_index_in_dim(positions, col_idx, 0, keepdims=False)
    incoming_ok = lax.dynamic_index_in_dim(present, col_idx, 0, keepdims=False)
    global_ids = incoming + blocks_own * jnp.arange(owners, dtype=jnp.int32)[:, None]
    matches = (local_src[:, None] == global_ids.reshape(-1)[None, :]) & incoming_ok.reshape(-1)[
        None, :
    ]
    slot_of = jnp.sum(
        matches.astype(jnp.int32) * jnp.arange(owners * CAP, dtype=jnp.int32)[None, :], axis=1
    )
    batches = features.shape[0]
    row_total = features.shape[1] * sections
    all_inputs = row_parts.transpose(1, 0, 2, 3).reshape(batches, row_total, -1)
    piece_rows = 16
    splits = row_total // piece_rows
    first_blocks = all_inputs.reshape(batches * splits, piece_rows, blocks_own, block_size)
    first_blocks = first_blocks.transpose(0, 2, 1, 3)
    finished = run_pipeline(
        first_blocks,
        local_w.reshape(blocks_own, nonzero_count * block_size, block_size),
        bias[0].reshape(blocks_own, 1, block_size),
        slot_of,
        outgoing_next,
        outgoing,
        sections,
        owners,
    )
    finished = finished.reshape(batches, splits, blocks_own, piece_rows, block_size)
    completed = finished.transpose(0, 1, 3, 2, 4).reshape(
        batches, row_total, blocks_own * block_size
    )
    own_rows = row_total // sections
    outgoing_rows = completed.reshape(batches, sections, own_rows, blocks_own * block_size)
    gathered = lax.all_to_all(outgoing_rows, "section", split_axis=1, concat_axis=1, tiled=True)
    own_result = gathered[:, sections - 1]
    row_ids = section_idx * own_rows + jnp.arange(own_rows, dtype=jnp.int32)
    row_mask = row_ids[None, :] < batch_rows[:, None]
    return jnp.where(row_mask[:, :, None], own_result, jnp.zeros_like(own_result))


def solution(mesh):
    in_specs = (
        P(None, "section", "col"),
        P("section", "col", None, None, None),
        P("section", "col", None),
        P("section", "col"),
        P(),
    )
    out_specs = P(None, "section", "col")
    return jax.shard_map(body, mesh=mesh, in_specs=in_specs, out_specs=out_specs, check_vma=False)
```

```python
import functools

import jax
import jax.numpy as jnp
from jax import lax
from jax.experimental import pallas as pl
from jax.experimental.pallas import tpu as pltpu
from jax.sharding import PartitionSpec as P

CAP = 2
MESH_ID = pl.DeviceIdType.MESH


def from_behind(x, axis, by):
    size = lax.axis_size(axis)
    pairs = [(i, i + by) for i in range(size) if 0 <= i + by < size]
    return lax.ppermute(x, axis, pairs)


def request_lists(pattern_table, owners, blocks_own, slot_total):
    dest_entries = pattern_table.reshape(owners, -1)
    block_total = owners * blocks_own
    catalog = jnp.arange(block_total, dtype=jnp.int32)
    wanted = jnp.any(dest_entries[:, :, None] == catalog[None, None, :], axis=1)
    wanted = wanted.reshape(owners, owners, blocks_own)
    local_rows = jnp.arange(blocks_own, dtype=jnp.int32)
    below = local_rows[:, None] <= local_rows[None, :]
    block_ranks = jnp.einsum(
        "abi,ij->abj", wanted.astype(jnp.float32), below.astype(jnp.float32)
    ).astype(jnp.int32) - 1
    slot_ids = jnp.arange(slot_total, dtype=jnp.int32)
    chosen = wanted[:, :, None, :] & (block_ranks[:, :, None, :] == slot_ids[None, None, :, None])
    local_ids = jnp.arange(blocks_own, dtype=jnp.int32)
    positions = jnp.sum(chosen.astype(jnp.int32) * local_ids[None, None, None, :], axis=3)
    present = jnp.any(chosen, axis=3)
    return (positions, present)


def pipeline_kernel(
    sections, owners, batches, first_ref, w_ref, b_ref, slot_ref, next_ref, first_list_ref,
    out_ref, *scratch,
):
    recv = scratch[:batches]
    send = scratch[batches:2 * batches]
    send0 = scratch[2 * batches:3 * batches]
    send_sem, recv_sem, local_sem, send0_sem = scratch[3 * batches:]
    me_s = lax.axis_index("section")
    me_c = lax.axis_index("col")
    blocks_own = w_ref.shape[0]
    nonzero_count = slot_ref.shape[0] // blocks_own
    barrier = pltpu.get_barrier_semaphore()

    @pl.when(me_s > 0)
    def _():
        for d in range(owners):
            pl.semaphore_signal(barrier, inc=1, device_id=(me_s - 1, d), device_id_type=MESH_ID)

    @pl.when(me_s < sections - 1)
    def _():
        for d in range(owners):
            pl.semaphore_signal(barrier, inc=1, device_id=(me_s + 1, d), device_id_type=MESH_ID)

    @pl.when(me_s == 0)
    def _():
        for d in range(owners):

            @pl.when(me_c != d)
            def _():
                pl.semaphore_signal(barrier, inc=1, device_id=(0, d), device_id_type=MESH_ID)

    is_first = (me_s == 0).astype(jnp.int32)
    peers = owners * (
        (me_s > 0).astype(jnp.int32) + (me_s < sections - 1).astype(jnp.int32)
    ) + is_first * (owners - 1)
    pl.semaphore_wait(barrier, peers)

    def first_copy(m, d):
        return pltpu.make_async_remote_copy(
            src_ref=send0[m].at[pl.ds(d * CAP, CAP)],
            dst_ref=recv[m].at[pl.ds(me_c * CAP, CAP)],
            send_sem=send0_sem.at[m, d],
            recv_sem=recv_sem.at[m, me_c],
            device_id=(0, d),
            device_id_type=MESH_ID,
        )

    def first_local(m):
        return pltpu.make_async_copy(
            send0[m].at[pl.ds(me_c * CAP, CAP)],
            recv[m].at[pl.ds(me_c * CAP, CAP)],
            local_sem.at[m],
        )

    @pl.when(me_s == 0)
    def _():
        for m in range(batches):

            def stage_first(i, carry):
                send0[m][i] = first_ref[m, first_list_ref[i]]
                return carry

            lax.fori_loop(0, owners * CAP, stage_first, 0, unroll=True)
            for d in range(owners):

                @pl.when(me_c != d)
                def _():
                    first_copy(m, d).start()

            first_local(m).start()

    def outgoing_copy(m, d):
        return pltpu.make_async_remote_copy(
            src_ref=send[m].at[pl.ds(d * CAP, CAP)],
            dst_ref=recv[m].at[pl.ds(me_c * CAP, CAP)],
            send_sem=send_sem.at[m, d],
            recv_sem=recv_sem.at[m, me_c],
            device_id=(me_s + 1, d),
            device_id_type=MESH_ID,
        )

    for m in range(batches):

        @pl.when(me_s == 0)
        def _():
            first_local(m).wait()
            for e in range(owners):

                @pl.when(me_c != e)
                def _():
                    pltpu.make_async_remote_copy(
                        src_ref=send0[m].at[pl.ds(e * CAP, CAP)],
                        dst_ref=recv[m].at[pl.ds(e * CAP, CAP)],
                        send_sem=send0_sem.at[m, e],
                        recv_sem=recv_sem.at[m, e],
                        device_id=(0, e),
                        device_id_type=MESH_ID,
                    ).wait_recv()

        @pl.when(me_s > 0)
        def _():
            for e in range(owners):
                pltpu.make_async_remote_copy(
                    src_ref=send[m].at[pl.ds(e * CAP, CAP)],
                    dst_ref=recv[m].at[pl.ds(e * CAP, CAP)],
                    send_sem=send_sem.at[m, e],
                    recv_sem=recv_sem.at[m, e],
                    device_id=(me_s - 1, e),
                    device_id_type=MESH_ID,
                ).wait_recv()

        def block_step(j, carry):
            picked = jnp.concatenate(
                [recv[m][slot_ref[j * nonzero_count + k]] for k in range(nonzero_count)], axis=-1
            )
            acc = jnp.dot(picked, w_ref[j], preferred_element_type=jnp.float32)
            out_ref[m, j] = jnp.clip(acc + b_ref[j], 0.0, 32.0).astype(out_ref.dtype)
            return carry

        lax.fori_loop(0, blocks_own, block_step, 0, unroll=True)

        @pl.when(me_s < sections - 1)
        def _():
            def stage(i, carry):
                send[m][i] = out_ref[m, next_ref[i]]
                return carry

            lax.fori_loop(0, owners * CAP, stage, 0, unroll=True)
            for d in range(owners):
                outgoing_copy(m, d).start()

    @pl.when(me_s < sections - 1)
    def _():
        for m in range(batches):
            for d in range(owners):
                outgoing_copy(m, d).wait_send()

    @pl.when(me_s == 0)
    def _():
        for m in range(batches):
            for d in range(owners):

                @pl.when(me_c != d)
                def _():
                    first_copy(m, d).wait_send()


def run_pipeline(
    first_blocks, local_w, local_bias, slot_of, outgoing_next, outgoing, sections, owners
):
    batches = first_blocks.shape[0]
    blocks_own = local_w.shape[0]
    rows = first_blocks.shape[2]
    slots_shape = (owners * CAP,) + first_blocks.shape[2:]
    block_size = local_w.shape[-1]
    vmem = pl.BlockSpec(memory_space=pltpu.VMEM)
    smem = pl.BlockSpec(memory_space=pltpu.SMEM)
    return pl.pallas_call(
        functools.partial(pipeline_kernel, sections, owners, batches),
        out_shape=jax.ShapeDtypeStruct((batches, blocks_own, rows, block_size), jnp.bfloat16),
        in_specs=[vmem, vmem, vmem, smem, smem, smem],
        out_specs=vmem,
        scratch_shapes=[
            *[pltpu.VMEM(slots_shape, jnp.bfloat16) for _ in range(3 * batches)],
            pltpu.SemaphoreType.DMA((batches, owners)),
            pltpu.SemaphoreType.DMA((batches, owners)),
            pltpu.SemaphoreType.DMA((batches,)),
            pltpu.SemaphoreType.DMA((batches, owners)),
        ],
        compiler_params=pltpu.CompilerParams(collective_id=0, has_side_effects=True),
    )(first_blocks, local_w, local_bias, slot_of, outgoing_next, outgoing)


def pattern_kernel(sections, owners, src_ref, feat_ref, own_ref, nxt_ref, rows_ref, *sems):
    own_send, own_recv, nxt_send, nxt_recv, local_sem, rows_send, rows_recv, rows_sem = sems
    me_s = lax.axis_index("section")
    me_c = lax.axis_index("col")
    barrier = pltpu.get_barrier_semaphore()
    for d in range(owners):

        @pl.when(me_c != d)
        def _():
            pl.semaphore_signal(barrier, inc=1, device_id=(me_s, d), device_id_type=MESH_ID)

    @pl.when(me_s > 0)
    def _():
        for d in range(owners):
            pl.semaphore_signal(barrier, inc=1, device_id=(me_s - 1, d), device_id_type=MESH_ID)

    @pl.when(me_s < sections - 1)
    def _():
        for d in range(owners):
            pl.semaphore_signal(barrier, inc=1, device_id=(me_s + 1, d), device_id_type=MESH_ID)

    @pl.when(me_s > 0)
    def _():
        pl.semaphore_signal(barrier, inc=1, device_id=(0, me_c), device_id_type=MESH_ID)

    @pl.when(me_s == 0)
    def _():
        for r in range(1, sections):
            pl.semaphore_signal(barrier, inc=1, device_id=(r, me_c), device_id_type=MESH_ID)

    is_first = (me_s == 0).astype(jnp.int32)
    peers = (owners - 1) + owners * (
        (me_s > 0).astype(jnp.int32) + (me_s < sections - 1).astype(jnp.int32)
    ) + is_first * (sections - 1) + (1 - is_first)
    pl.semaphore_wait(barrier, peers)

    def own_copy(d, e):
        return pltpu.make_async_remote_copy(
            src_ref=src_ref,
            dst_ref=own_ref.at[e],
            send_sem=own_send.at[d],
            recv_sem=own_recv.at[e],
            device_id=(me_s, d),
            device_id_type=MESH_ID,
        )

    def nxt_copy(dev_s, d, e):
        return pltpu.make_async_remote_copy(
            src_ref=src_ref,
            dst_ref=nxt_ref.at[e],
            send_sem=nxt_send.at[d],
            recv_sem=nxt_recv.at[e],
            device_id=(dev_s, d),
            device_id_type=MESH_ID,
        )

    for d in range(owners):

        @pl.when(me_c != d)
        def _():
            own_copy(d, me_c).start()

    @pl.when(me_s > 0)
    def _():
        for d in range(owners):
            nxt_copy(me_s - 1, d, me_c).start()

    def rows_copy(r):
        return pltpu.make_async_remote_copy(
            src_ref=feat_ref,
            dst_ref=rows_ref.at[r],
            send_sem=rows_send,
            recv_sem=rows_recv.at[r],
            device_id=(0, me_c),
            device_id_type=MESH_ID,
        )

    @pl.when(me_s > 0)
    def _():
        rows_copy(me_s).start()

    @pl.when(me_s == 0)
    def _():
        own_rows = pltpu.make_async_copy(feat_ref, rows_ref.at[0], rows_sem)
        own_rows.start()
        own_rows.wait()

    mine = pltpu.make_async_copy(src_ref, own_ref.at[me_c], local_sem)
    mine.start()
    mine.wait()
    for d in range(owners):

        @pl.when(me_c != d)
        def _():
            own_copy(d, me_c).wait_send()
            own_copy(d, d).wait_recv()

    @pl.when(me_s > 0)
    def _():
        for d in range(owners):
            nxt_copy(me_s - 1, d, me_c).wait_send()

    @pl.when(me_s < sections - 1)
    def _():
        for e in range(owners):
            nxt_copy(me_s + 1, e, e).wait_recv()

    @pl.when(me_s == sections - 1)
    def _():
        nxt_ref[...] = jnp.zeros_like(nxt_ref)

    @pl.when(me_s > 0)
    def _():
        rows_copy(me_s).wait_send()
        rows_ref[...] = jnp.zeros_like(rows_ref)

    @pl.when(me_s == 0)
    def _():
        for r in range(1, sections):
            rows_copy(r).wait_recv()


def exchange_patterns(local_sources, features, sections, owners):
    table = jax.ShapeDtypeStruct((owners,) + local_sources.shape, local_sources.dtype)
    rows = jax.ShapeDtypeStruct((sections,) + features.shape, features.dtype)
    vmem = pl.BlockSpec(memory_space=pltpu.VMEM)
    return pl.pallas_call(
        functools.partial(pattern_kernel, sections, owners),
        out_shape=(table, table, rows),
        in_specs=[vmem, vmem],
        out_specs=(vmem, vmem, vmem),
        scratch_shapes=[pltpu.SemaphoreType.DMA((owners,)) for _ in range(4)]
        + [
            pltpu.SemaphoreType.DMA(()),
            pltpu.SemaphoreType.DMA(()),
            pltpu.SemaphoreType.DMA((sections,)),
            pltpu.SemaphoreType.DMA(()),
        ],
        compiler_params=pltpu.CompilerParams(collective_id=1, has_side_effects=True),
    )(local_sources, features)


def body(features, weights, sources, bias, batch_rows):
    sections = lax.axis_size("section")
    owners = lax.axis_size("col")
    section_idx = lax.axis_index("section")
    col_idx = lax.axis_index("col")
    local_w = weights[0]
    blocks_own = local_w.shape[0]
    nonzero_count = local_w.shape[1]
    block_size = local_w.shape[2]
    local_src = sources[0].reshape(blocks_own * nonzero_count)
    own_table, next_table, row_parts = exchange_patterns(sources[0], features, sections, owners)
    both_positions, both_present = jax.vmap(
        lambda table: request_lists(table, owners, blocks_own, CAP)
    )(jnp.stack([own_table, next_table]))
    positions, present = both_positions[0], both_present[0]
    outgoing = lax.dynamic_index_in_dim(positions, col_idx, 1, keepdims=False)
    outgoing = outgoing.reshape(owners * CAP)
    outgoing_next = lax.dynamic_index_in_dim(both_positions[1], col_idx, 1, keepdims=False)
    outgoing_next = outgoing_next.reshape(owners * CAP)
    incoming = lax.dynamic_index_in_dim(positions, col_idx, 0, keepdims=False)
    incoming_ok = lax.dynamic_index_in_dim(present, col_idx, 0, keepdims=False)
    global_ids = incoming + blocks_own * jnp.arange(owners, dtype=jnp.int32)[:, None]
    matches = (local_src[:, None] == global_ids.reshape(-1)[None, :]) & incoming_ok.reshape(-1)[
        None, :
    ]
    slot_of = jnp.sum(
        matches.astype(jnp.int32) * jnp.arange(owners * CAP, dtype=jnp.int32)[None, :], axis=1
    )
    batches = features.shape[0]
    row_total = features.shape[1] * sections
    all_inputs = row_parts.transpose(1, 0, 2, 3).reshape(batches, row_total, -1)
    piece_rows = 8
    splits = row_total // piece_rows
    first_blocks = all_inputs.reshape(batches * splits, piece_rows, blocks_own, block_size)
    first_blocks = first_blocks.transpose(0, 2, 1, 3)
    finished = run_pipeline(
        first_blocks,
        local_w.reshape(blocks_own, nonzero_count * block_size, block_size),
        bias[0].reshape(blocks_own, 1, block_size),
        slot_of,
        outgoing_next,
        outgoing,
        sections,
        owners,
    )
    finished = finished.reshape(batches, splits, blocks_own, piece_rows, block_size)
    completed = finished.transpose(0, 1, 3, 2, 4).reshape(
        batches, row_total, blocks_own * block_size
    )
    own_rows = row_total // sections
    outgoing_rows = completed.reshape(batches, sections, own_rows, blocks_own * block_size)
    gathered = lax.all_to_all(outgoing_rows, "section", split_axis=1, concat_axis=1, tiled=True)
    own_result = gathered[:, sections - 1]
    row_ids = section_idx * own_rows + jnp.arange(own_rows, dtype=jnp.int32)
    row_mask = row_ids[None, :] < batch_rows[:, None]
    return jnp.where(row_mask[:, :, None], own_result, jnp.zeros_like(own_result))


def solution(mesh):
    in_specs = (
        P(None, "section", "col"),
        P("section", "col", None, None, None),
        P("section", "col", None),
        P("section", "col"),
        P(),
    )
    out_specs = P(None, "section", "col")
    return jax.shard_map(body, mesh=mesh, in_specs=in_specs, out_specs=out_specs, check_vma=False)
```

```python
import functools

import jax
import jax.numpy as jnp
from jax import lax
from jax.experimental import pallas as pl
from jax.experimental.pallas import tpu as pltpu
from jax.sharding import PartitionSpec as P

CAP = 2
MESH_ID = pl.DeviceIdType.MESH


def from_behind(x, axis, by):
    size = lax.axis_size(axis)
    pairs = [(i, i + by) for i in range(size) if 0 <= i + by < size]
    return lax.ppermute(x, axis, pairs)


def request_lists(pattern_table, owners, blocks_own, slot_total):
    dest_entries = pattern_table.reshape(owners, -1)
    block_total = owners * blocks_own
    catalog = jnp.arange(block_total, dtype=jnp.int32)
    wanted = jnp.any(dest_entries[:, :, None] == catalog[None, None, :], axis=1)
    wanted = wanted.reshape(owners, owners, blocks_own)
    local_rows = jnp.arange(blocks_own, dtype=jnp.int32)
    below = local_rows[:, None] <= local_rows[None, :]
    block_ranks = jnp.einsum(
        "abi,ij->abj", wanted.astype(jnp.float32), below.astype(jnp.float32)
    ).astype(jnp.int32) - 1
    slot_ids = jnp.arange(slot_total, dtype=jnp.int32)
    chosen = wanted[:, :, None, :] & (block_ranks[:, :, None, :] == slot_ids[None, None, :, None])
    local_ids = jnp.arange(blocks_own, dtype=jnp.int32)
    positions = jnp.sum(chosen.astype(jnp.int32) * local_ids[None, None, None, :], axis=3)
    present = jnp.any(chosen, axis=3)
    return (positions, present)


def pipeline_kernel(
    sections, owners, batches, first_ref, w_ref, b_ref, slot_ref, next_ref, first_list_ref,
    out_ref, *scratch,
):
    recv = scratch[:batches]
    send = scratch[batches:2 * batches]
    send0 = scratch[2 * batches:3 * batches]
    send_sem, recv_sem, local_sem, send0_sem = scratch[3 * batches:]
    me_s = lax.axis_index("section")
    me_c = lax.axis_index("col")
    blocks_own = w_ref.shape[0]
    nonzero_count = slot_ref.shape[0] // blocks_own
    barrier = pltpu.get_barrier_semaphore()

    @pl.when(me_s > 0)
    def _():
        for d in range(owners):
            pl.semaphore_signal(barrier, inc=1, device_id=(me_s - 1, d), device_id_type=MESH_ID)

    @pl.when(me_s < sections - 1)
    def _():
        for d in range(owners):
            pl.semaphore_signal(barrier, inc=1, device_id=(me_s + 1, d), device_id_type=MESH_ID)

    @pl.when(me_s == 0)
    def _():
        for d in range(owners):

            @pl.when(me_c != d)
            def _():
                pl.semaphore_signal(barrier, inc=1, device_id=(0, d), device_id_type=MESH_ID)

    is_first = (me_s == 0).astype(jnp.int32)
    peers = owners * (
        (me_s > 0).astype(jnp.int32) + (me_s < sections - 1).astype(jnp.int32)
    ) + is_first * (owners - 1)
    pl.semaphore_wait(barrier, peers)

    def first_copy(m, d):
        return pltpu.make_async_remote_copy(
            src_ref=send0[m].at[pl.ds(d * CAP, CAP)],
            dst_ref=recv[m].at[pl.ds(me_c * CAP, CAP)],
            send_sem=send0_sem.at[m, d],
            recv_sem=recv_sem.at[m, me_c],
            device_id=(0, d),
            device_id_type=MESH_ID,
        )

    def first_local(m):
        return pltpu.make_async_copy(
            send0[m].at[pl.ds(me_c * CAP, CAP)],
            recv[m].at[pl.ds(me_c * CAP, CAP)],
            local_sem.at[m],
        )

    def first_send(m):
        @pl.when(me_s == 0)
        def _():
            def stage_first(i, carry):
                send0[m][i] = first_ref[m, first_list_ref[i]]
                return carry

            lax.fori_loop(0, owners * CAP, stage_first, 0, unroll=True)
            for d in range(owners):

                @pl.when(me_c != d)
                def _():
                    first_copy(m, d).start()

            first_local(m).start()

    ahead = 2
    for m in range(min(ahead, batches)):
        first_send(m)

    def outgoing_copy(m, d):
        return pltpu.make_async_remote_copy(
            src_ref=send[m].at[pl.ds(d * CAP, CAP)],
            dst_ref=recv[m].at[pl.ds(me_c * CAP, CAP)],
            send_sem=send_sem.at[m, d],
            recv_sem=recv_sem.at[m, me_c],
            device_id=(me_s + 1, d),
            device_id_type=MESH_ID,
        )

    for m in range(batches):

        @pl.when(me_s == 0)
        def _():
            first_local(m).wait()
            for e in range(owners):

                @pl.when(me_c != e)
                def _():
                    pltpu.make_async_remote_copy(
                        src_ref=send0[m].at[pl.ds(e * CAP, CAP)],
                        dst_ref=recv[m].at[pl.ds(e * CAP, CAP)],
                        send_sem=send0_sem.at[m, e],
                        recv_sem=recv_sem.at[m, e],
                        device_id=(0, e),
                        device_id_type=MESH_ID,
                    ).wait_recv()

        @pl.when(me_s > 0)
        def _():
            for e in range(owners):
                pltpu.make_async_remote_copy(
                    src_ref=send[m].at[pl.ds(e * CAP, CAP)],
                    dst_ref=recv[m].at[pl.ds(e * CAP, CAP)],
                    send_sem=send_sem.at[m, e],
                    recv_sem=recv_sem.at[m, e],
                    device_id=(me_s - 1, e),
                    device_id_type=MESH_ID,
                ).wait_recv()

        def block_step(j, carry):
            picked = jnp.concatenate(
                [recv[m][slot_ref[j * nonzero_count + k]] for k in range(nonzero_count)], axis=-1
            )
            acc = jnp.dot(picked, w_ref[j], preferred_element_type=jnp.float32)
            out_ref[m, j] = jnp.clip(acc + b_ref[j], 0.0, 32.0).astype(out_ref.dtype)
            return carry

        lax.fori_loop(0, blocks_own, block_step, 0, unroll=True)

        @pl.when(me_s < sections - 1)
        def _():
            def stage(i, carry):
                send[m][i] = out_ref[m, next_ref[i]]
                return carry

            lax.fori_loop(0, owners * CAP, stage, 0, unroll=True)
            for d in range(owners):
                outgoing_copy(m, d).start()

        if m + ahead < batches:
            first_send(m + ahead)

    @pl.when(me_s < sections - 1)
    def _():
        for m in range(batches):
            for d in range(owners):
                outgoing_copy(m, d).wait_send()

    @pl.when(me_s == 0)
    def _():
        for m in range(batches):
            for d in range(owners):

                @pl.when(me_c != d)
                def _():
                    first_copy(m, d).wait_send()


def run_pipeline(
    first_blocks, local_w, local_bias, slot_of, outgoing_next, outgoing, sections, owners
):
    batches = first_blocks.shape[0]
    blocks_own = local_w.shape[0]
    rows = first_blocks.shape[2]
    slots_shape = (owners * CAP,) + first_blocks.shape[2:]
    block_size = local_w.shape[-1]
    vmem = pl.BlockSpec(memory_space=pltpu.VMEM)
    smem = pl.BlockSpec(memory_space=pltpu.SMEM)
    return pl.pallas_call(
        functools.partial(pipeline_kernel, sections, owners, batches),
        out_shape=jax.ShapeDtypeStruct((batches, blocks_own, rows, block_size), jnp.bfloat16),
        in_specs=[vmem, vmem, vmem, smem, smem, smem],
        out_specs=vmem,
        scratch_shapes=[
            *[pltpu.VMEM(slots_shape, jnp.bfloat16) for _ in range(3 * batches)],
            pltpu.SemaphoreType.DMA((batches, owners)),
            pltpu.SemaphoreType.DMA((batches, owners)),
            pltpu.SemaphoreType.DMA((batches,)),
            pltpu.SemaphoreType.DMA((batches, owners)),
        ],
        compiler_params=pltpu.CompilerParams(collective_id=0, has_side_effects=True),
    )(first_blocks, local_w, local_bias, slot_of, outgoing_next, outgoing)


def pattern_kernel(sections, owners, src_ref, feat_ref, own_ref, nxt_ref, rows_ref, *sems):
    own_send, own_recv, nxt_send, nxt_recv, local_sem, rows_send, rows_recv, rows_sem = sems
    me_s = lax.axis_index("section")
    me_c = lax.axis_index("col")
    barrier = pltpu.get_barrier_semaphore()
    for d in range(owners):

        @pl.when(me_c != d)
        def _():
            pl.semaphore_signal(barrier, inc=1, device_id=(me_s, d), device_id_type=MESH_ID)

    @pl.when(me_s > 0)
    def _():
        for d in range(owners):
            pl.semaphore_signal(barrier, inc=1, device_id=(me_s - 1, d), device_id_type=MESH_ID)

    @pl.when(me_s < sections - 1)
    def _():
        for d in range(owners):
            pl.semaphore_signal(barrier, inc=1, device_id=(me_s + 1, d), device_id_type=MESH_ID)

    @pl.when(me_s > 0)
    def _():
        pl.semaphore_signal(barrier, inc=1, device_id=(0, me_c), device_id_type=MESH_ID)

    @pl.when(me_s == 0)
    def _():
        for r in range(1, sections):
            pl.semaphore_signal(barrier, inc=1, device_id=(r, me_c), device_id_type=MESH_ID)

    is_first = (me_s == 0).astype(jnp.int32)
    peers = (owners - 1) + owners * (
        (me_s > 0).astype(jnp.int32) + (me_s < sections - 1).astype(jnp.int32)
    ) + is_first * (sections - 1) + (1 - is_first)
    pl.semaphore_wait(barrier, peers)

    def own_copy(d, e):
        return pltpu.make_async_remote_copy(
            src_ref=src_ref,
            dst_ref=own_ref.at[e],
            send_sem=own_send.at[d],
            recv_sem=own_recv.at[e],
            device_id=(me_s, d),
            device_id_type=MESH_ID,
        )

    def nxt_copy(dev_s, d, e):
        return pltpu.make_async_remote_copy(
            src_ref=src_ref,
            dst_ref=nxt_ref.at[e],
            send_sem=nxt_send.at[d],
            recv_sem=nxt_recv.at[e],
            device_id=(dev_s, d),
            device_id_type=MESH_ID,
        )

    for d in range(owners):

        @pl.when(me_c != d)
        def _():
            own_copy(d, me_c).start()

    @pl.when(me_s > 0)
    def _():
        for d in range(owners):
            nxt_copy(me_s - 1, d, me_c).start()

    def rows_copy(r):
        return pltpu.make_async_remote_copy(
            src_ref=feat_ref,
            dst_ref=rows_ref.at[r],
            send_sem=rows_send,
            recv_sem=rows_recv.at[r],
            device_id=(0, me_c),
            device_id_type=MESH_ID,
        )

    @pl.when(me_s > 0)
    def _():
        rows_copy(me_s).start()

    @pl.when(me_s == 0)
    def _():
        own_rows = pltpu.make_async_copy(feat_ref, rows_ref.at[0], rows_sem)
        own_rows.start()
        own_rows.wait()

    mine = pltpu.make_async_copy(src_ref, own_ref.at[me_c], local_sem)
    mine.start()
    mine.wait()
    for d in range(owners):

        @pl.when(me_c != d)
        def _():
            own_copy(d, me_c).wait_send()
            own_copy(d, d).wait_recv()

    @pl.when(me_s > 0)
    def _():
        for d in range(owners):
            nxt_copy(me_s - 1, d, me_c).wait_send()

    @pl.when(me_s < sections - 1)
    def _():
        for e in range(owners):
            nxt_copy(me_s + 1, e, e).wait_recv()

    @pl.when(me_s == sections - 1)
    def _():
        nxt_ref[...] = jnp.zeros_like(nxt_ref)

    @pl.when(me_s > 0)
    def _():
        rows_copy(me_s).wait_send()
        rows_ref[...] = jnp.zeros_like(rows_ref)

    @pl.when(me_s == 0)
    def _():
        for r in range(1, sections):
            rows_copy(r).wait_recv()


def exchange_patterns(local_sources, features, sections, owners):
    table = jax.ShapeDtypeStruct((owners,) + local_sources.shape, local_sources.dtype)
    rows = jax.ShapeDtypeStruct((sections,) + features.shape, features.dtype)
    vmem = pl.BlockSpec(memory_space=pltpu.VMEM)
    return pl.pallas_call(
        functools.partial(pattern_kernel, sections, owners),
        out_shape=(table, table, rows),
        in_specs=[vmem, vmem],
        out_specs=(vmem, vmem, vmem),
        scratch_shapes=[pltpu.SemaphoreType.DMA((owners,)) for _ in range(4)]
        + [
            pltpu.SemaphoreType.DMA(()),
            pltpu.SemaphoreType.DMA(()),
            pltpu.SemaphoreType.DMA((sections,)),
            pltpu.SemaphoreType.DMA(()),
        ],
        compiler_params=pltpu.CompilerParams(collective_id=1, has_side_effects=True),
    )(local_sources, features)


def body(features, weights, sources, bias, batch_rows):
    sections = lax.axis_size("section")
    owners = lax.axis_size("col")
    section_idx = lax.axis_index("section")
    col_idx = lax.axis_index("col")
    local_w = weights[0]
    blocks_own = local_w.shape[0]
    nonzero_count = local_w.shape[1]
    block_size = local_w.shape[2]
    local_src = sources[0].reshape(blocks_own * nonzero_count)
    own_table, next_table, row_parts = exchange_patterns(sources[0], features, sections, owners)
    both_positions, both_present = jax.vmap(
        lambda table: request_lists(table, owners, blocks_own, CAP)
    )(jnp.stack([own_table, next_table]))
    positions, present = both_positions[0], both_present[0]
    outgoing = lax.dynamic_index_in_dim(positions, col_idx, 1, keepdims=False)
    outgoing = outgoing.reshape(owners * CAP)
    outgoing_next = lax.dynamic_index_in_dim(both_positions[1], col_idx, 1, keepdims=False)
    outgoing_next = outgoing_next.reshape(owners * CAP)
    incoming = lax.dynamic_index_in_dim(positions, col_idx, 0, keepdims=False)
    incoming_ok = lax.dynamic_index_in_dim(present, col_idx, 0, keepdims=False)
    global_ids = incoming + blocks_own * jnp.arange(owners, dtype=jnp.int32)[:, None]
    matches = (local_src[:, None] == global_ids.reshape(-1)[None, :]) & incoming_ok.reshape(-1)[
        None, :
    ]
    slot_of = jnp.sum(
        matches.astype(jnp.int32) * jnp.arange(owners * CAP, dtype=jnp.int32)[None, :], axis=1
    )
    batches = features.shape[0]
    row_total = features.shape[1] * sections
    all_inputs = row_parts.transpose(1, 0, 2, 3).reshape(batches, row_total, -1)
    piece_rows = 8
    splits = row_total // piece_rows
    first_blocks = all_inputs.reshape(batches * splits, piece_rows, blocks_own, block_size)
    first_blocks = first_blocks.transpose(0, 2, 1, 3)
    finished = run_pipeline(
        first_blocks,
        local_w.reshape(blocks_own, nonzero_count * block_size, block_size),
        bias[0].reshape(blocks_own, 1, block_size),
        slot_of,
        outgoing_next,
        outgoing,
        sections,
        owners,
    )
    finished = finished.reshape(batches, splits, blocks_own, piece_rows, block_size)
    completed = finished.transpose(0, 1, 3, 2, 4).reshape(
        batches, row_total, blocks_own * block_size
    )
    own_rows = row_total // sections
    outgoing_rows = completed.reshape(batches, sections, own_rows, blocks_own * block_size)
    gathered = lax.all_to_all(outgoing_rows, "section", split_axis=1, concat_axis=1, tiled=True)
    own_result = gathered[:, sections - 1]
    row_ids = section_idx * own_rows + jnp.arange(own_rows, dtype=jnp.int32)
    row_mask = row_ids[None, :] < batch_rows[:, None]
    return jnp.where(row_mask[:, :, None], own_result, jnp.zeros_like(own_result))


def solution(mesh):
    in_specs = (
        P(None, "section", "col"),
        P("section", "col", None, None, None),
        P("section", "col", None),
        P("section", "col"),
        P(),
    )
    out_specs = P(None, "section", "col")
    return jax.shard_map(body, mesh=mesh, in_specs=in_specs, out_specs=out_specs, check_vma=False)
```

```python
import functools

import jax
import jax.numpy as jnp
from jax import lax
from jax.experimental import pallas as pl
from jax.experimental.pallas import tpu as pltpu
from jax.sharding import PartitionSpec as P

CAP = 2
MESH_ID = pl.DeviceIdType.MESH


def from_behind(x, axis, by):
    size = lax.axis_size(axis)
    pairs = [(i, i + by) for i in range(size) if 0 <= i + by < size]
    return lax.ppermute(x, axis, pairs)


def request_lists(pattern_table, owners, blocks_own, slot_total):
    dest_entries = pattern_table.reshape(owners, -1)
    block_total = owners * blocks_own
    catalog = jnp.arange(block_total, dtype=jnp.int32)
    wanted = jnp.any(dest_entries[:, :, None] == catalog[None, None, :], axis=1)
    wanted = wanted.reshape(owners, owners, blocks_own)
    local_rows = jnp.arange(blocks_own, dtype=jnp.int32)
    below = local_rows[:, None] <= local_rows[None, :]
    block_ranks = jnp.einsum(
        "abi,ij->abj", wanted.astype(jnp.float32), below.astype(jnp.float32)
    ).astype(jnp.int32) - 1
    slot_ids = jnp.arange(slot_total, dtype=jnp.int32)
    chosen = wanted[:, :, None, :] & (block_ranks[:, :, None, :] == slot_ids[None, None, :, None])
    local_ids = jnp.arange(blocks_own, dtype=jnp.int32)
    positions = jnp.sum(chosen.astype(jnp.int32) * local_ids[None, None, None, :], axis=3)
    present = jnp.any(chosen, axis=3)
    return (positions, present)


def pipeline_kernel(
    sections, owners, batches, first_ref, w_ref, b_ref, slot_ref, next_ref, first_list_ref,
    out_ref, *scratch,
):
    recv = scratch[:batches]
    send0 = scratch[batches:2 * batches]
    send_sem, recv_sem, local_sem, send0_sem = scratch[2 * batches:]
    me_s = lax.axis_index("section")
    me_c = lax.axis_index("col")
    blocks_own = w_ref.shape[0]
    nonzero_count = slot_ref.shape[0] // blocks_own
    barrier = pltpu.get_barrier_semaphore()

    @pl.when(me_s > 0)
    def _():
        for d in range(owners):
            pl.semaphore_signal(barrier, inc=1, device_id=(me_s - 1, d), device_id_type=MESH_ID)

    @pl.when(me_s < sections - 1)
    def _():
        for d in range(owners):
            pl.semaphore_signal(barrier, inc=1, device_id=(me_s + 1, d), device_id_type=MESH_ID)

    @pl.when(me_s == 0)
    def _():
        for d in range(owners):

            @pl.when(me_c != d)
            def _():
                pl.semaphore_signal(barrier, inc=1, device_id=(0, d), device_id_type=MESH_ID)

    is_first = (me_s == 0).astype(jnp.int32)
    peers = owners * (
        (me_s > 0).astype(jnp.int32) + (me_s < sections - 1).astype(jnp.int32)
    ) + is_first * (owners - 1)
    pl.semaphore_wait(barrier, peers)

    def first_copy(m, d):
        return pltpu.make_async_remote_copy(
            src_ref=send0[m].at[pl.ds(d * CAP, CAP)],
            dst_ref=recv[m].at[pl.ds(me_c * CAP, CAP)],
            send_sem=send0_sem.at[m, d],
            recv_sem=recv_sem.at[m, me_c],
            device_id=(0, d),
            device_id_type=MESH_ID,
        )

    def first_local(m):
        return pltpu.make_async_copy(
            send0[m].at[pl.ds(me_c * CAP, CAP)],
            recv[m].at[pl.ds(me_c * CAP, CAP)],
            local_sem.at[m],
        )

    @pl.when(me_s == 0)
    def _():
        for m in range(batches):

            def stage_first(i, carry):
                send0[m][i] = first_ref[m, first_list_ref[i]]
                return carry

            lax.fori_loop(0, owners * CAP, stage_first, 0, unroll=True)
            for d in range(owners):

                @pl.when(me_c != d)
                def _():
                    first_copy(m, d).start()

            first_local(m).start()

    def outgoing_copy(m, d):
        return pltpu.make_async_remote_copy(
            src_ref=out_ref.at[m, pl.ds(d * CAP, CAP)],
            dst_ref=recv[m].at[pl.ds(me_c * CAP, CAP)],
            send_sem=send_sem.at[m, d],
            recv_sem=recv_sem.at[m, me_c],
            device_id=(me_s + 1, d),
            device_id_type=MESH_ID,
        )

    for m in range(batches):

        @pl.when(me_s == 0)
        def _():
            first_local(m).wait()
            for e in range(owners):

                @pl.when(me_c != e)
                def _():
                    pltpu.make_async_remote_copy(
                        src_ref=send0[m].at[pl.ds(e * CAP, CAP)],
                        dst_ref=recv[m].at[pl.ds(e * CAP, CAP)],
                        send_sem=send0_sem.at[m, e],
                        recv_sem=recv_sem.at[m, e],
                        device_id=(0, e),
                        device_id_type=MESH_ID,
                    ).wait_recv()

        @pl.when(me_s > 0)
        def _():
            for e in range(owners):
                pltpu.make_async_remote_copy(
                    src_ref=out_ref.at[m, pl.ds(e * CAP, CAP)],
                    dst_ref=recv[m].at[pl.ds(e * CAP, CAP)],
                    send_sem=send_sem.at[m, e],
                    recv_sem=recv_sem.at[m, e],
                    device_id=(me_s - 1, e),
                    device_id_type=MESH_ID,
                ).wait_recv()

        def block_step(j, carry):
            block = next_ref[j]
            picked = jnp.concatenate(
                [recv[m][slot_ref[block * nonzero_count + k]] for k in range(nonzero_count)],
                axis=-1,
            )
            acc = jnp.dot(picked, w_ref[block], preferred_element_type=jnp.float32)
            out_ref[m, j] = jnp.clip(acc + b_ref[block], 0.0, 32.0).astype(out_ref.dtype)
            return carry

        lax.fori_loop(0, blocks_own, block_step, 0, unroll=True)

        @pl.when(me_s < sections - 1)
        def _():
            for d in range(owners):
                outgoing_copy(m, d).start()

    @pl.when(me_s < sections - 1)
    def _():
        for m in range(batches):
            for d in range(owners):
                outgoing_copy(m, d).wait_send()

    @pl.when(me_s == 0)
    def _():
        for m in range(batches):
            for d in range(owners):

                @pl.when(me_c != d)
                def _():
                    first_copy(m, d).wait_send()


def run_pipeline(
    first_blocks, local_w, local_bias, slot_of, outgoing_next, outgoing, sections, owners
):
    batches = first_blocks.shape[0]
    blocks_own = local_w.shape[0]
    rows = first_blocks.shape[2]
    slots_shape = (owners * CAP,) + first_blocks.shape[2:]
    block_size = local_w.shape[-1]
    vmem = pl.BlockSpec(memory_space=pltpu.VMEM)
    smem = pl.BlockSpec(memory_space=pltpu.SMEM)
    return pl.pallas_call(
        functools.partial(pipeline_kernel, sections, owners, batches),
        out_shape=jax.ShapeDtypeStruct((batches, blocks_own, rows, block_size), jnp.bfloat16),
        in_specs=[vmem, vmem, vmem, smem, smem, smem],
        out_specs=vmem,
        scratch_shapes=[
            *[pltpu.VMEM(slots_shape, jnp.bfloat16) for _ in range(2 * batches)],
            pltpu.SemaphoreType.DMA((batches, owners)),
            pltpu.SemaphoreType.DMA((batches, owners)),
            pltpu.SemaphoreType.DMA((batches,)),
            pltpu.SemaphoreType.DMA((batches, owners)),
        ],
        compiler_params=pltpu.CompilerParams(collective_id=0, has_side_effects=True),
    )(first_blocks, local_w, local_bias, slot_of, outgoing_next, outgoing)


def pattern_kernel(sections, owners, src_ref, feat_ref, own_ref, nxt_ref, rows_ref, *sems):
    own_send, own_recv, nxt_send, nxt_recv, local_sem, rows_send, rows_recv, rows_sem = sems
    me_s = lax.axis_index("section")
    me_c = lax.axis_index("col")
    barrier = pltpu.get_barrier_semaphore()
    for d in range(owners):

        @pl.when(me_c != d)
        def _():
            pl.semaphore_signal(barrier, inc=1, device_id=(me_s, d), device_id_type=MESH_ID)

    @pl.when(me_s > 0)
    def _():
        for d in range(owners):
            pl.semaphore_signal(barrier, inc=1, device_id=(me_s - 1, d), device_id_type=MESH_ID)

    @pl.when(me_s < sections - 1)
    def _():
        for d in range(owners):
            pl.semaphore_signal(barrier, inc=1, device_id=(me_s + 1, d), device_id_type=MESH_ID)

    @pl.when(me_s > 0)
    def _():
        pl.semaphore_signal(barrier, inc=1, device_id=(0, me_c), device_id_type=MESH_ID)

    @pl.when(me_s == 0)
    def _():
        for r in range(1, sections):
            pl.semaphore_signal(barrier, inc=1, device_id=(r, me_c), device_id_type=MESH_ID)

    is_first = (me_s == 0).astype(jnp.int32)
    peers = (owners - 1) + owners * (
        (me_s > 0).astype(jnp.int32) + (me_s < sections - 1).astype(jnp.int32)
    ) + is_first * (sections - 1) + (1 - is_first)
    pl.semaphore_wait(barrier, peers)

    def own_copy(d, e):
        return pltpu.make_async_remote_copy(
            src_ref=src_ref,
            dst_ref=own_ref.at[e],
            send_sem=own_send.at[d],
            recv_sem=own_recv.at[e],
            device_id=(me_s, d),
            device_id_type=MESH_ID,
        )

    def nxt_copy(dev_s, d, e):
        return pltpu.make_async_remote_copy(
            src_ref=src_ref,
            dst_ref=nxt_ref.at[e],
            send_sem=nxt_send.at[d],
            recv_sem=nxt_recv.at[e],
            device_id=(dev_s, d),
            device_id_type=MESH_ID,
        )

    for d in range(owners):

        @pl.when(me_c != d)
        def _():
            own_copy(d, me_c).start()

    @pl.when(me_s > 0)
    def _():
        for d in range(owners):
            nxt_copy(me_s - 1, d, me_c).start()

    def rows_copy(r):
        return pltpu.make_async_remote_copy(
            src_ref=feat_ref,
            dst_ref=rows_ref.at[r],
            send_sem=rows_send,
            recv_sem=rows_recv.at[r],
            device_id=(0, me_c),
            device_id_type=MESH_ID,
        )

    @pl.when(me_s > 0)
    def _():
        rows_copy(me_s).start()

    @pl.when(me_s == 0)
    def _():
        own_rows = pltpu.make_async_copy(feat_ref, rows_ref.at[0], rows_sem)
        own_rows.start()
        own_rows.wait()

    mine = pltpu.make_async_copy(src_ref, own_ref.at[me_c], local_sem)
    mine.start()
    mine.wait()
    for d in range(owners):

        @pl.when(me_c != d)
        def _():
            own_copy(d, me_c).wait_send()
            own_copy(d, d).wait_recv()

    @pl.when(me_s > 0)
    def _():
        for d in range(owners):
            nxt_copy(me_s - 1, d, me_c).wait_send()

    @pl.when(me_s < sections - 1)
    def _():
        for e in range(owners):
            nxt_copy(me_s + 1, e, e).wait_recv()

    @pl.when(me_s == sections - 1)
    def _():
        nxt_ref[...] = jnp.zeros_like(nxt_ref)

    @pl.when(me_s > 0)
    def _():
        rows_copy(me_s).wait_send()
        rows_ref[...] = jnp.zeros_like(rows_ref)

    @pl.when(me_s == 0)
    def _():
        for r in range(1, sections):
            rows_copy(r).wait_recv()


def exchange_patterns(local_sources, features, sections, owners):
    table = jax.ShapeDtypeStruct((owners,) + local_sources.shape, local_sources.dtype)
    rows = jax.ShapeDtypeStruct((sections,) + features.shape, features.dtype)
    vmem = pl.BlockSpec(memory_space=pltpu.VMEM)
    return pl.pallas_call(
        functools.partial(pattern_kernel, sections, owners),
        out_shape=(table, table, rows),
        in_specs=[vmem, vmem],
        out_specs=(vmem, vmem, vmem),
        scratch_shapes=[pltpu.SemaphoreType.DMA((owners,)) for _ in range(4)]
        + [
            pltpu.SemaphoreType.DMA(()),
            pltpu.SemaphoreType.DMA(()),
            pltpu.SemaphoreType.DMA((sections,)),
            pltpu.SemaphoreType.DMA(()),
        ],
        compiler_params=pltpu.CompilerParams(collective_id=1, has_side_effects=True),
    )(local_sources, features)


def body(features, weights, sources, bias, batch_rows):
    sections = lax.axis_size("section")
    owners = lax.axis_size("col")
    section_idx = lax.axis_index("section")
    col_idx = lax.axis_index("col")
    local_w = weights[0]
    blocks_own = local_w.shape[0]
    nonzero_count = local_w.shape[1]
    block_size = local_w.shape[2]
    local_src = sources[0].reshape(blocks_own * nonzero_count)
    own_table, next_table, row_parts = exchange_patterns(sources[0], features, sections, owners)
    both_positions, both_present = jax.vmap(
        lambda table: request_lists(table, owners, blocks_own, CAP)
    )(jnp.stack([own_table, next_table]))
    positions, present = both_positions[0], both_present[0]
    outgoing = lax.dynamic_index_in_dim(positions, col_idx, 1, keepdims=False)
    outgoing = outgoing.reshape(owners * CAP)
    outgoing_next = lax.dynamic_index_in_dim(both_positions[1], col_idx, 1, keepdims=False)
    outgoing_next = jnp.where(
        section_idx == sections - 1,
        jnp.arange(owners * CAP, dtype=jnp.int32),
        outgoing_next.reshape(owners * CAP),
    )
    incoming = lax.dynamic_index_in_dim(positions, col_idx, 0, keepdims=False)
    incoming_ok = lax.dynamic_index_in_dim(present, col_idx, 0, keepdims=False)
    global_ids = incoming + blocks_own * jnp.arange(owners, dtype=jnp.int32)[:, None]
    matches = (local_src[:, None] == global_ids.reshape(-1)[None, :]) & incoming_ok.reshape(-1)[
        None, :
    ]
    slot_of = jnp.sum(
        matches.astype(jnp.int32) * jnp.arange(owners * CAP, dtype=jnp.int32)[None, :], axis=1
    )
    batches = features.shape[0]
    row_total = features.shape[1] * sections
    all_inputs = row_parts.transpose(1, 0, 2, 3).reshape(batches, row_total, -1)
    piece_rows = 8
    splits = row_total // piece_rows
    first_blocks = all_inputs.reshape(batches * splits, piece_rows, blocks_own, block_size)
    first_blocks = first_blocks.transpose(0, 2, 1, 3)
    finished = run_pipeline(
        first_blocks,
        local_w.reshape(blocks_own, nonzero_count * block_size, block_size),
        bias[0].reshape(blocks_own, 1, block_size),
        slot_of,
        outgoing_next,
        outgoing,
        sections,
        owners,
    )
    finished = finished.reshape(batches, splits, blocks_own, piece_rows, block_size)
    completed = finished.transpose(0, 1, 3, 2, 4).reshape(
        batches, row_total, blocks_own * block_size
    )
    own_rows = row_total // sections
    outgoing_rows = completed.reshape(batches, sections, own_rows, blocks_own * block_size)
    gathered = lax.all_to_all(outgoing_rows, "section", split_axis=1, concat_axis=1, tiled=True)
    own_result = gathered[:, sections - 1]
    row_ids = section_idx * own_rows + jnp.arange(own_rows, dtype=jnp.int32)
    row_mask = row_ids[None, :] < batch_rows[:, None]
    return jnp.where(row_mask[:, :, None], own_result, jnp.zeros_like(own_result))


def solution(mesh):
    in_specs = (
        P(None, "section", "col"),
        P("section", "col", None, None, None),
        P("section", "col", None),
        P("section", "col"),
        P(),
    )
    out_specs = P(None, "section", "col")
    return jax.shard_map(body, mesh=mesh, in_specs=in_specs, out_specs=out_specs, check_vma=False)
```

```python
import functools

import jax
import jax.numpy as jnp
from jax import lax
from jax.experimental import pallas as pl
from jax.experimental.pallas import tpu as pltpu
from jax.sharding import PartitionSpec as P

CAP = 2
MESH_ID = pl.DeviceIdType.MESH


def from_behind(x, axis, by):
    size = lax.axis_size(axis)
    pairs = [(i, i + by) for i in range(size) if 0 <= i + by < size]
    return lax.ppermute(x, axis, pairs)


def request_lists(pattern_table, owners, blocks_own, slot_total):
    dest_entries = pattern_table.reshape(owners, -1)
    block_total = owners * blocks_own
    catalog = jnp.arange(block_total, dtype=jnp.int32)
    wanted = jnp.any(dest_entries[:, :, None] == catalog[None, None, :], axis=1)
    wanted = wanted.reshape(owners, owners, blocks_own)
    local_rows = jnp.arange(blocks_own, dtype=jnp.int32)
    below = local_rows[:, None] <= local_rows[None, :]
    block_ranks = jnp.einsum(
        "abi,ij->abj", wanted.astype(jnp.float32), below.astype(jnp.float32)
    ).astype(jnp.int32) - 1
    slot_ids = jnp.arange(slot_total, dtype=jnp.int32)
    chosen = wanted[:, :, None, :] & (block_ranks[:, :, None, :] == slot_ids[None, None, :, None])
    local_ids = jnp.arange(blocks_own, dtype=jnp.int32)
    positions = jnp.sum(chosen.astype(jnp.int32) * local_ids[None, None, None, :], axis=3)
    present = jnp.any(chosen, axis=3)
    return (positions, present)


def pipeline_kernel(
    sections, owners, batches, first_ref, w_ref, b_ref, slot_ref, next_ref, first_list_ref,
    out_ref, *scratch,
):
    recv = scratch[:batches]
    send0 = scratch[batches:2 * batches]
    send_sem, recv_sem, local_sem, send0_sem = scratch[2 * batches:]
    me_s = lax.axis_index("section")
    me_c = lax.axis_index("col")
    blocks_own = w_ref.shape[0]
    nonzero_count = slot_ref.shape[0] // blocks_own
    barrier = pltpu.get_barrier_semaphore()

    @pl.when(me_s > 0)
    def _():
        for d in range(owners):
            pl.semaphore_signal(barrier, inc=1, device_id=(me_s - 1, d), device_id_type=MESH_ID)

    @pl.when(me_s < sections - 1)
    def _():
        for d in range(owners):
            pl.semaphore_signal(barrier, inc=1, device_id=(me_s + 1, d), device_id_type=MESH_ID)

    @pl.when(me_s == 0)
    def _():
        for d in range(owners):

            @pl.when(me_c != d)
            def _():
                pl.semaphore_signal(barrier, inc=1, device_id=(0, d), device_id_type=MESH_ID)

    is_first = (me_s == 0).astype(jnp.int32)
    peers = owners * (
        (me_s > 0).astype(jnp.int32) + (me_s < sections - 1).astype(jnp.int32)
    ) + is_first * (owners - 1)
    pl.semaphore_wait(barrier, peers)

    def first_copy(m, d):
        return pltpu.make_async_remote_copy(
            src_ref=send0[m].at[pl.ds(d * CAP, CAP)],
            dst_ref=recv[m].at[pl.ds(me_c * CAP, CAP)],
            send_sem=send0_sem.at[m, d],
            recv_sem=recv_sem.at[m, me_c],
            device_id=(0, d),
            device_id_type=MESH_ID,
        )

    def first_local(m):
        return pltpu.make_async_copy(
            send0[m].at[pl.ds(me_c * CAP, CAP)],
            recv[m].at[pl.ds(me_c * CAP, CAP)],
            local_sem.at[m],
        )

    @pl.when(me_s == 0)
    def _():
        for m in range(batches):

            def stage_first(i, carry):
                send0[m][i] = first_ref[m, first_list_ref[i]]
                return carry

            lax.fori_loop(0, owners * CAP, stage_first, 0, unroll=True)
            for d in range(owners):

                @pl.when(me_c != d)
                def _():
                    first_copy(m, d).start()

            first_local(m).start()

    def outgoing_copy(m, d):
        return pltpu.make_async_remote_copy(
            src_ref=out_ref.at[m, pl.ds(d * CAP, CAP)],
            dst_ref=recv[m].at[pl.ds(me_c * CAP, CAP)],
            send_sem=send_sem.at[m, d],
            recv_sem=recv_sem.at[m, me_c],
            device_id=(me_s + 1, d),
            device_id_type=MESH_ID,
        )

    for m in range(batches):

        @pl.when(me_s == 0)
        def _():
            first_local(m).wait()
            for e in range(owners):

                @pl.when(me_c != e)
                def _():
                    pltpu.make_async_remote_copy(
                        src_ref=send0[m].at[pl.ds(e * CAP, CAP)],
                        dst_ref=recv[m].at[pl.ds(e * CAP, CAP)],
                        send_sem=send0_sem.at[m, e],
                        recv_sem=recv_sem.at[m, e],
                        device_id=(0, e),
                        device_id_type=MESH_ID,
                    ).wait_recv()

        @pl.when(me_s > 0)
        def _():
            for e in range(owners):
                pltpu.make_async_remote_copy(
                    src_ref=out_ref.at[m, pl.ds(e * CAP, CAP)],
                    dst_ref=recv[m].at[pl.ds(e * CAP, CAP)],
                    send_sem=send_sem.at[m, e],
                    recv_sem=recv_sem.at[m, e],
                    device_id=(me_s - 1, e),
                    device_id_type=MESH_ID,
                ).wait_recv()

        def block_step(j, carry):
            block = next_ref[j]
            picked = jnp.concatenate(
                [recv[m][slot_ref[block * nonzero_count + k]] for k in range(nonzero_count)],
                axis=-1,
            )
            acc = jnp.dot(picked, w_ref[block], preferred_element_type=jnp.float32)
            out_ref[m, j] = jnp.clip(acc + b_ref[block], 0.0, 32.0).astype(out_ref.dtype)
            return carry

        lax.fori_loop(0, blocks_own, block_step, 0, unroll=True)

        @pl.when(me_s < sections - 1)
        def _():
            for d in range(owners):
                outgoing_copy(m, d).start()

    @pl.when(me_s < sections - 1)
    def _():
        for m in range(batches):
            for d in range(owners):
                outgoing_copy(m, d).wait_send()

    @pl.when(me_s == 0)
    def _():
        for m in range(batches):
            for d in range(owners):

                @pl.when(me_c != d)
                def _():
                    first_copy(m, d).wait_send()


def run_pipeline(
    first_blocks, local_w, local_bias, slot_of, outgoing_next, outgoing, sections, owners
):
    batches = first_blocks.shape[0]
    blocks_own = local_w.shape[0]
    rows = first_blocks.shape[2]
    slots_shape = (owners * CAP,) + first_blocks.shape[2:]
    block_size = local_w.shape[-1]
    vmem = pl.BlockSpec(memory_space=pltpu.VMEM)
    smem = pl.BlockSpec(memory_space=pltpu.SMEM)
    return pl.pallas_call(
        functools.partial(pipeline_kernel, sections, owners, batches),
        out_shape=jax.ShapeDtypeStruct((batches, blocks_own, rows, block_size), jnp.bfloat16),
        in_specs=[vmem, vmem, vmem, smem, smem, smem],
        out_specs=vmem,
        scratch_shapes=[
            *[pltpu.VMEM(slots_shape, jnp.bfloat16) for _ in range(2 * batches)],
            pltpu.SemaphoreType.DMA((batches, owners)),
            pltpu.SemaphoreType.DMA((batches, owners)),
            pltpu.SemaphoreType.DMA((batches,)),
            pltpu.SemaphoreType.DMA((batches, owners)),
        ],
        compiler_params=pltpu.CompilerParams(collective_id=0, has_side_effects=True),
    )(first_blocks, local_w, local_bias, slot_of, outgoing_next, outgoing)


def pattern_kernel(sections, owners, src_ref, feat_ref, own_ref, nxt_ref, rows_ref, *sems):
    own_send, own_recv, nxt_send, nxt_recv, local_sem, rows_send, rows_recv, rows_sem = sems
    me_s = lax.axis_index("section")
    me_c = lax.axis_index("col")
    barrier = pltpu.get_barrier_semaphore()
    for d in range(owners):

        @pl.when(me_c != d)
        def _():
            pl.semaphore_signal(barrier, inc=1, device_id=(me_s, d), device_id_type=MESH_ID)

    @pl.when(me_s > 0)
    def _():
        for d in range(owners):
            pl.semaphore_signal(barrier, inc=1, device_id=(me_s - 1, d), device_id_type=MESH_ID)

    @pl.when(me_s < sections - 1)
    def _():
        for d in range(owners):
            pl.semaphore_signal(barrier, inc=1, device_id=(me_s + 1, d), device_id_type=MESH_ID)

    @pl.when(me_s > 0)
    def _():
        pl.semaphore_signal(barrier, inc=1, device_id=(0, me_c), device_id_type=MESH_ID)

    @pl.when(me_s == 0)
    def _():
        for r in range(1, sections):
            pl.semaphore_signal(barrier, inc=1, device_id=(r, me_c), device_id_type=MESH_ID)

    is_first = (me_s == 0).astype(jnp.int32)
    peers = (owners - 1) + owners * (
        (me_s > 0).astype(jnp.int32) + (me_s < sections - 1).astype(jnp.int32)
    ) + is_first * (sections - 1) + (1 - is_first)
    pl.semaphore_wait(barrier, peers)

    def own_copy(d, e):
        return pltpu.make_async_remote_copy(
            src_ref=src_ref,
            dst_ref=own_ref.at[e],
            send_sem=own_send.at[d],
            recv_sem=own_recv.at[e],
            device_id=(me_s, d),
            device_id_type=MESH_ID,
        )

    def nxt_copy(dev_s, d, e):
        return pltpu.make_async_remote_copy(
            src_ref=src_ref,
            dst_ref=nxt_ref.at[e],
            send_sem=nxt_send.at[d],
            recv_sem=nxt_recv.at[e],
            device_id=(dev_s, d),
            device_id_type=MESH_ID,
        )

    for d in range(owners):

        @pl.when(me_c != d)
        def _():
            own_copy(d, me_c).start()

    @pl.when(me_s > 0)
    def _():
        for d in range(owners):
            nxt_copy(me_s - 1, d, me_c).start()

    def rows_copy(r):
        return pltpu.make_async_remote_copy(
            src_ref=feat_ref,
            dst_ref=rows_ref.at[r],
            send_sem=rows_send,
            recv_sem=rows_recv.at[r],
            device_id=(0, me_c),
            device_id_type=MESH_ID,
        )

    @pl.when(me_s > 0)
    def _():
        rows_copy(me_s).start()

    @pl.when(me_s == 0)
    def _():
        own_rows = pltpu.make_async_copy(feat_ref, rows_ref.at[0], rows_sem)
        own_rows.start()
        own_rows.wait()

    mine = pltpu.make_async_copy(src_ref, own_ref.at[me_c], local_sem)
    mine.start()
    mine.wait()
    for d in range(owners):

        @pl.when(me_c != d)
        def _():
            own_copy(d, me_c).wait_send()
            own_copy(d, d).wait_recv()

    @pl.when(me_s > 0)
    def _():
        for d in range(owners):
            nxt_copy(me_s - 1, d, me_c).wait_send()

    @pl.when(me_s < sections - 1)
    def _():
        for e in range(owners):
            nxt_copy(me_s + 1, e, e).wait_recv()

    @pl.when(me_s == sections - 1)
    def _():
        nxt_ref[...] = jnp.zeros_like(nxt_ref)

    @pl.when(me_s > 0)
    def _():
        rows_copy(me_s).wait_send()
        rows_ref[...] = jnp.zeros_like(rows_ref)

    @pl.when(me_s == 0)
    def _():
        for r in range(1, sections):
            rows_copy(r).wait_recv()


def exchange_patterns(local_sources, features, sections, owners):
    table = jax.ShapeDtypeStruct((owners,) + local_sources.shape, local_sources.dtype)
    rows = jax.ShapeDtypeStruct((sections,) + features.shape, features.dtype)
    vmem = pl.BlockSpec(memory_space=pltpu.VMEM)
    return pl.pallas_call(
        functools.partial(pattern_kernel, sections, owners),
        out_shape=(table, table, rows),
        in_specs=[vmem, vmem],
        out_specs=(vmem, vmem, vmem),
        scratch_shapes=[pltpu.SemaphoreType.DMA((owners,)) for _ in range(4)]
        + [
            pltpu.SemaphoreType.DMA(()),
            pltpu.SemaphoreType.DMA(()),
            pltpu.SemaphoreType.DMA((sections,)),
            pltpu.SemaphoreType.DMA(()),
        ],
        compiler_params=pltpu.CompilerParams(collective_id=1, has_side_effects=True),
    )(local_sources, features)


def rows_kernel(sections, src_ref, out_ref, send_sem, recv_sem, local_sem):
    me_s = lax.axis_index("section")
    me_c = lax.axis_index("col")
    last = sections - 1
    barrier = pltpu.get_barrier_semaphore()

    @pl.when(me_s == last)
    def _():
        for r in range(last):
            pl.semaphore_signal(barrier, inc=1, device_id=(r, me_c), device_id_type=MESH_ID)

    @pl.when(me_s != last)
    def _():
        pl.semaphore_signal(barrier, inc=1, device_id=(last, me_c), device_id_type=MESH_ID)

    is_last = (me_s == last).astype(jnp.int32)
    pl.semaphore_wait(barrier, is_last * last + (1 - is_last))

    def row_copy(r):
        return pltpu.make_async_remote_copy(
            src_ref=src_ref.at[r],
            dst_ref=out_ref,
            send_sem=send_sem.at[r],
            recv_sem=recv_sem,
            device_id=(r, me_c),
            device_id_type=MESH_ID,
        )

    @pl.when(me_s == last)
    def _():
        for r in range(last):
            row_copy(r).start()
        mine = pltpu.make_async_copy(src_ref.at[last], out_ref, local_sem)
        mine.start()
        mine.wait()
        for r in range(last):
            row_copy(r).wait_send()

    @pl.when(me_s != last)
    def _():
        row_copy(0).wait_recv()


def deliver_rows(row_parts, sections):
    anywhere = pl.BlockSpec(memory_space=pl.ANY)
    return pl.pallas_call(
        functools.partial(rows_kernel, sections),
        out_shape=jax.ShapeDtypeStruct(row_parts.shape[1:], row_parts.dtype),
        in_specs=[anywhere],
        out_specs=anywhere,
        scratch_shapes=[
            pltpu.SemaphoreType.DMA((sections,)),
            pltpu.SemaphoreType.DMA(()),
            pltpu.SemaphoreType.DMA(()),
        ],
        compiler_params=pltpu.CompilerParams(collective_id=2, has_side_effects=True),
    )(row_parts)


def body(features, weights, sources, bias, batch_rows):
    sections = lax.axis_size("section")
    owners = lax.axis_size("col")
    section_idx = lax.axis_index("section")
    col_idx = lax.axis_index("col")
    local_w = weights[0]
    blocks_own = local_w.shape[0]
    nonzero_count = local_w.shape[1]
    block_size = local_w.shape[2]
    local_src = sources[0].reshape(blocks_own * nonzero_count)
    own_table, next_table, row_parts = exchange_patterns(sources[0], features, sections, owners)
    both_positions, both_present = jax.vmap(
        lambda table: request_lists(table, owners, blocks_own, CAP)
    )(jnp.stack([own_table, next_table]))
    positions, present = both_positions[0], both_present[0]
    outgoing = lax.dynamic_index_in_dim(positions, col_idx, 1, keepdims=False)
    outgoing = outgoing.reshape(owners * CAP)
    outgoing_next = lax.dynamic_index_in_dim(both_positions[1], col_idx, 1, keepdims=False)
    outgoing_next = jnp.where(
        section_idx == sections - 1,
        jnp.arange(owners * CAP, dtype=jnp.int32),
        outgoing_next.reshape(owners * CAP),
    )
    incoming = lax.dynamic_index_in_dim(positions, col_idx, 0, keepdims=False)
    incoming_ok = lax.dynamic_index_in_dim(present, col_idx, 0, keepdims=False)
    global_ids = incoming + blocks_own * jnp.arange(owners, dtype=jnp.int32)[:, None]
    matches = (local_src[:, None] == global_ids.reshape(-1)[None, :]) & incoming_ok.reshape(-1)[
        None, :
    ]
    slot_of = jnp.sum(
        matches.astype(jnp.int32) * jnp.arange(owners * CAP, dtype=jnp.int32)[None, :], axis=1
    )
    batches = features.shape[0]
    row_total = features.shape[1] * sections
    all_inputs = row_parts.transpose(1, 0, 2, 3).reshape(batches, row_total, -1)
    piece_rows = 8
    splits = row_total // piece_rows
    first_blocks = all_inputs.reshape(batches * splits, piece_rows, blocks_own, block_size)
    first_blocks = first_blocks.transpose(0, 2, 1, 3)
    finished = run_pipeline(
        first_blocks,
        local_w.reshape(blocks_own, nonzero_count * block_size, block_size),
        bias[0].reshape(blocks_own, 1, block_size),
        slot_of,
        outgoing_next,
        outgoing,
        sections,
        owners,
    )
    finished = finished.reshape(batches, splits, blocks_own, piece_rows, block_size)
    completed = finished.transpose(0, 1, 3, 2, 4).reshape(
        batches, row_total, blocks_own * block_size
    )
    own_rows = row_total // sections
    outgoing_rows = completed.reshape(batches, sections, own_rows, blocks_own * block_size)
    own_result = deliver_rows(outgoing_rows.transpose(1, 0, 2, 3), sections)
    row_ids = section_idx * own_rows + jnp.arange(own_rows, dtype=jnp.int32)
    row_mask = row_ids[None, :] < batch_rows[:, None]
    return jnp.where(row_mask[:, :, None], own_result, jnp.zeros_like(own_result))


def solution(mesh):
    in_specs = (
        P(None, "section", "col"),
        P("section", "col", None, None, None),
        P("section", "col", None),
        P("section", "col"),
        P(),
    )
    out_specs = P(None, "section", "col")
    return jax.shard_map(body, mesh=mesh, in_specs=in_specs, out_specs=out_specs, check_vma=False)
```

```python
import functools

import jax
import jax.numpy as jnp
from jax import lax
from jax.experimental import pallas as pl
from jax.experimental.pallas import tpu as pltpu
from jax.sharding import PartitionSpec as P

CAP = 2
MESH_ID = pl.DeviceIdType.MESH


def pipeline_kernel(
    sections, owners, batches, first_ref, w_ref, b_ref, slot_ref, next_ref, first_list_ref,
    out_ref, *scratch,
):
    recv = scratch[:batches]
    send0 = scratch[batches:2 * batches]
    send_sem, recv_sem, local_sem, send0_sem = scratch[2 * batches:]
    me_s = lax.axis_index("section")
    me_c = lax.axis_index("col")
    blocks_own = w_ref.shape[0]
    nonzero_count = slot_ref.shape[0] // blocks_own
    barrier = pltpu.get_barrier_semaphore()

    @pl.when(me_s > 0)
    def _():
        for d in range(owners):
            pl.semaphore_signal(barrier, inc=1, device_id=(me_s - 1, d), device_id_type=MESH_ID)

    @pl.when(me_s < sections - 1)
    def _():
        for d in range(owners):
            pl.semaphore_signal(barrier, inc=1, device_id=(me_s + 1, d), device_id_type=MESH_ID)

    @pl.when(me_s == 0)
    def _():
        for d in range(owners):

            @pl.when(me_c != d)
            def _():
                pl.semaphore_signal(barrier, inc=1, device_id=(0, d), device_id_type=MESH_ID)

    is_first = (me_s == 0).astype(jnp.int32)
    peers = owners * (
        (me_s > 0).astype(jnp.int32) + (me_s < sections - 1).astype(jnp.int32)
    ) + is_first * (owners - 1)
    pl.semaphore_wait(barrier, peers)

    def first_copy(m, d):
        return pltpu.make_async_remote_copy(
            src_ref=send0[m].at[pl.ds(d * CAP, CAP)],
            dst_ref=recv[m].at[pl.ds(me_c * CAP, CAP)],
            send_sem=send0_sem.at[m, d],
            recv_sem=recv_sem.at[m, me_c],
            device_id=(0, d),
            device_id_type=MESH_ID,
        )

    def first_local(m):
        return pltpu.make_async_copy(
            send0[m].at[pl.ds(me_c * CAP, CAP)],
            recv[m].at[pl.ds(me_c * CAP, CAP)],
            local_sem.at[m],
        )

    @pl.when(me_s == 0)
    def _():
        for m in range(batches):

            def stage_first(i, carry):
                send0[m][i] = first_ref[m, first_list_ref[i]]
                return carry

            lax.fori_loop(0, owners * CAP, stage_first, 0, unroll=True)
            for d in range(owners):

                @pl.when(me_c != d)
                def _():
                    first_copy(m, d).start()

            first_local(m).start()

    def outgoing_copy(m, d):
        return pltpu.make_async_remote_copy(
            src_ref=out_ref.at[m, pl.ds(d * CAP, CAP)],
            dst_ref=recv[m].at[pl.ds(me_c * CAP, CAP)],
            send_sem=send_sem.at[m, d],
            recv_sem=recv_sem.at[m, me_c],
            device_id=(me_s + 1, d),
            device_id_type=MESH_ID,
        )

    for m in range(batches):

        @pl.when(me_s == 0)
        def _():
            first_local(m).wait()
            for e in range(owners):

                @pl.when(me_c != e)
                def _():
                    pltpu.make_async_remote_copy(
                        src_ref=send0[m].at[pl.ds(e * CAP, CAP)],
                        dst_ref=recv[m].at[pl.ds(e * CAP, CAP)],
                        send_sem=send0_sem.at[m, e],
                        recv_sem=recv_sem.at[m, e],
                        device_id=(0, e),
                        device_id_type=MESH_ID,
                    ).wait_recv()

        @pl.when(me_s > 0)
        def _():
            for e in range(owners):
                pltpu.make_async_remote_copy(
                    src_ref=out_ref.at[m, pl.ds(e * CAP, CAP)],
                    dst_ref=recv[m].at[pl.ds(e * CAP, CAP)],
                    send_sem=send_sem.at[m, e],
                    recv_sem=recv_sem.at[m, e],
                    device_id=(me_s - 1, e),
                    device_id_type=MESH_ID,
                ).wait_recv()

        def block_step(j, carry):
            block = next_ref[j]
            picked = jnp.concatenate(
                [recv[m][slot_ref[block * nonzero_count + k]] for k in range(nonzero_count)],
                axis=-1,
            )
            acc = jnp.dot(picked, w_ref[block], preferred_element_type=jnp.float32)
            out_ref[m, j] = jnp.clip(acc + b_ref[block], 0.0, 32.0).astype(out_ref.dtype)
            return carry

        lax.fori_loop(0, blocks_own, block_step, 0, unroll=True)

        @pl.when(me_s < sections - 1)
        def _():
            for d in range(owners):
                outgoing_copy(m, d).start()

    @pl.when(me_s < sections - 1)
    def _():
        for m in range(batches):
            for d in range(owners):
                outgoing_copy(m, d).wait_send()

    @pl.when(me_s == 0)
    def _():
        for m in range(batches):
            for d in range(owners):

                @pl.when(me_c != d)
                def _():
                    first_copy(m, d).wait_send()


def run_pipeline(
    first_blocks, local_w, local_bias, slot_of, outgoing_next, outgoing, sections, owners
):
    batches = first_blocks.shape[0]
    blocks_own = local_w.shape[0]
    rows = first_blocks.shape[2]
    slots_shape = (owners * CAP,) + first_blocks.shape[2:]
    block_size = local_w.shape[-1]
    vmem = pl.BlockSpec(memory_space=pltpu.VMEM)
    smem = pl.BlockSpec(memory_space=pltpu.SMEM)
    return pl.pallas_call(
        functools.partial(pipeline_kernel, sections, owners, batches),
        out_shape=jax.ShapeDtypeStruct((batches, blocks_own, rows, block_size), jnp.bfloat16),
        in_specs=[vmem, vmem, vmem, smem, smem, smem],
        out_specs=vmem,
        scratch_shapes=[
            *[pltpu.VMEM(slots_shape, jnp.bfloat16) for _ in range(2 * batches)],
            pltpu.SemaphoreType.DMA((batches, owners)),
            pltpu.SemaphoreType.DMA((batches, owners)),
            pltpu.SemaphoreType.DMA((batches,)),
            pltpu.SemaphoreType.DMA((batches, owners)),
        ],
        compiler_params=pltpu.CompilerParams(collective_id=0, has_side_effects=True),
    )(first_blocks, local_w, local_bias, slot_of, outgoing_next, outgoing)


def pattern_kernel(sections, owners, src_ref, feat_ref, own_ref, nxt_ref, rows_ref, *sems):
    own_send, own_recv, nxt_send, nxt_recv, local_sem, rows_send, rows_recv, rows_sem = sems
    me_s = lax.axis_index("section")
    me_c = lax.axis_index("col")
    barrier = pltpu.get_barrier_semaphore()
    for d in range(owners):

        @pl.when(me_c != d)
        def _():
            pl.semaphore_signal(barrier, inc=1, device_id=(me_s, d), device_id_type=MESH_ID)

    @pl.when(me_s > 0)
    def _():
        for d in range(owners):
            pl.semaphore_signal(barrier, inc=1, device_id=(me_s - 1, d), device_id_type=MESH_ID)

    @pl.when(me_s < sections - 1)
    def _():
        for d in range(owners):
            pl.semaphore_signal(barrier, inc=1, device_id=(me_s + 1, d), device_id_type=MESH_ID)

    @pl.when(me_s > 0)
    def _():
        pl.semaphore_signal(barrier, inc=1, device_id=(0, me_c), device_id_type=MESH_ID)

    @pl.when(me_s == 0)
    def _():
        for r in range(1, sections):
            pl.semaphore_signal(barrier, inc=1, device_id=(r, me_c), device_id_type=MESH_ID)

    is_first = (me_s == 0).astype(jnp.int32)
    peers = (owners - 1) + owners * (
        (me_s > 0).astype(jnp.int32) + (me_s < sections - 1).astype(jnp.int32)
    ) + is_first * (sections - 1) + (1 - is_first)
    pl.semaphore_wait(barrier, peers)

    def own_copy(d, e):
        return pltpu.make_async_remote_copy(
            src_ref=src_ref,
            dst_ref=own_ref.at[e],
            send_sem=own_send.at[d],
            recv_sem=own_recv.at[e],
            device_id=(me_s, d),
            device_id_type=MESH_ID,
        )

    def nxt_copy(dev_s, d, e):
        return pltpu.make_async_remote_copy(
            src_ref=src_ref,
            dst_ref=nxt_ref.at[e],
            send_sem=nxt_send.at[d],
            recv_sem=nxt_recv.at[e],
            device_id=(dev_s, d),
            device_id_type=MESH_ID,
        )

    for d in range(owners):

        @pl.when(me_c != d)
        def _():
            own_copy(d, me_c).start()

    @pl.when(me_s > 0)
    def _():
        for d in range(owners):
            nxt_copy(me_s - 1, d, me_c).start()

    def rows_copy(r):
        return pltpu.make_async_remote_copy(
            src_ref=feat_ref,
            dst_ref=rows_ref.at[r],
            send_sem=rows_send,
            recv_sem=rows_recv.at[r],
            device_id=(0, me_c),
            device_id_type=MESH_ID,
        )

    @pl.when(me_s > 0)
    def _():
        rows_copy(me_s).start()

    @pl.when(me_s == 0)
    def _():
        own_rows = pltpu.make_async_copy(feat_ref, rows_ref.at[0], rows_sem)
        own_rows.start()
        own_rows.wait()

    mine = pltpu.make_async_copy(src_ref, own_ref.at[me_c], local_sem)
    mine.start()
    mine.wait()
    for d in range(owners):

        @pl.when(me_c != d)
        def _():
            own_copy(d, me_c).wait_send()
            own_copy(d, d).wait_recv()

    @pl.when(me_s > 0)
    def _():
        for d in range(owners):
            nxt_copy(me_s - 1, d, me_c).wait_send()

    @pl.when(me_s < sections - 1)
    def _():
        for e in range(owners):
            nxt_copy(me_s + 1, e, e).wait_recv()

    @pl.when(me_s == sections - 1)
    def _():
        nxt_ref[...] = jnp.zeros_like(nxt_ref)

    @pl.when(me_s > 0)
    def _():
        rows_copy(me_s).wait_send()
        rows_ref[...] = jnp.zeros_like(rows_ref)

    @pl.when(me_s == 0)
    def _():
        for r in range(1, sections):
            rows_copy(r).wait_recv()


def exchange_patterns(local_sources, features, sections, owners):
    table = jax.ShapeDtypeStruct((owners,) + local_sources.shape, local_sources.dtype)
    rows = jax.ShapeDtypeStruct((sections,) + features.shape, features.dtype)
    vmem = pl.BlockSpec(memory_space=pltpu.VMEM)
    return pl.pallas_call(
        functools.partial(pattern_kernel, sections, owners),
        out_shape=(table, table, rows),
        in_specs=[vmem, vmem],
        out_specs=(vmem, vmem, vmem),
        scratch_shapes=[pltpu.SemaphoreType.DMA((owners,)) for _ in range(4)]
        + [
            pltpu.SemaphoreType.DMA(()),
            pltpu.SemaphoreType.DMA(()),
            pltpu.SemaphoreType.DMA((sections,)),
            pltpu.SemaphoreType.DMA(()),
        ],
        compiler_params=pltpu.CompilerParams(collective_id=1, has_side_effects=True),
    )(local_sources, features)


def rows_kernel(sections, src_ref, out_ref, send_sem, recv_sem, local_sem):
    me_s = lax.axis_index("section")
    me_c = lax.axis_index("col")
    last = sections - 1
    barrier = pltpu.get_barrier_semaphore()

    @pl.when(me_s == last)
    def _():
        for r in range(last):
            pl.semaphore_signal(barrier, inc=1, device_id=(r, me_c), device_id_type=MESH_ID)

    @pl.when(me_s != last)
    def _():
        pl.semaphore_signal(barrier, inc=1, device_id=(last, me_c), device_id_type=MESH_ID)

    is_last = (me_s == last).astype(jnp.int32)
    pl.semaphore_wait(barrier, is_last * last + (1 - is_last))

    def row_copy(r):
        return pltpu.make_async_remote_copy(
            src_ref=src_ref.at[r],
            dst_ref=out_ref,
            send_sem=send_sem.at[r],
            recv_sem=recv_sem,
            device_id=(r, me_c),
            device_id_type=MESH_ID,
        )

    @pl.when(me_s == last)
    def _():
        for r in range(last):
            row_copy(r).start()
        mine = pltpu.make_async_copy(src_ref.at[last], out_ref, local_sem)
        mine.start()
        mine.wait()
        for r in range(last):
            row_copy(r).wait_send()

    @pl.when(me_s != last)
    def _():
        row_copy(0).wait_recv()


def deliver_rows(row_parts, sections):
    anywhere = pl.BlockSpec(memory_space=pl.ANY)
    return pl.pallas_call(
        functools.partial(rows_kernel, sections),
        out_shape=jax.ShapeDtypeStruct(row_parts.shape[1:], row_parts.dtype),
        in_specs=[anywhere],
        out_specs=anywhere,
        scratch_shapes=[
            pltpu.SemaphoreType.DMA((sections,)),
            pltpu.SemaphoreType.DMA(()),
            pltpu.SemaphoreType.DMA(()),
        ],
        compiler_params=pltpu.CompilerParams(collective_id=2, has_side_effects=True),
    )(row_parts)


def body(features, weights, sources, bias, batch_rows):
    sections = lax.axis_size("section")
    owners = lax.axis_size("col")
    section_idx = lax.axis_index("section")
    col_idx = lax.axis_index("col")
    local_w = weights[0]
    blocks_own = local_w.shape[0]
    nonzero_count = local_w.shape[1]
    block_size = local_w.shape[2]
    local_src = sources[0].reshape(blocks_own * nonzero_count)
    own_table, next_table, row_parts = exchange_patterns(sources[0], features, sections, owners)
    local_rows = jnp.arange(blocks_own, dtype=jnp.int32)
    below = (local_rows[:, None] <= local_rows[None, :]).astype(jnp.float32)
    slot_ids = jnp.arange(CAP, dtype=jnp.int32)

    def ranks_of(wanted):
        return jnp.einsum("...i,ij->...j", wanted.astype(jnp.float32), below).astype(jnp.int32) - 1

    def sender_list(table):
        flat = table.reshape(owners, blocks_own * nonzero_count)
        mine = col_idx * blocks_own + local_rows
        wanted = jnp.any(flat[:, :, None] == mine[None, None, :], axis=1)
        chosen = wanted[:, None, :] & (ranks_of(wanted)[:, None, :] == slot_ids[None, :, None])
        return jnp.sum(chosen.astype(jnp.int32) * local_rows[None, None, :], axis=2)

    both_lists = jax.vmap(sender_list)(jnp.stack([own_table, next_table]))
    outgoing = both_lists[0].reshape(owners * CAP)
    outgoing_next = jnp.where(
        section_idx == sections - 1,
        jnp.arange(owners * CAP, dtype=jnp.int32),
        both_lists[1].reshape(owners * CAP),
    )
    catalog = jnp.arange(owners * blocks_own, dtype=jnp.int32)
    requested = jnp.any(local_src[:, None] == catalog[None, :], axis=0).reshape(owners, blocks_own)
    slot_table = jnp.arange(owners, dtype=jnp.int32)[:, None] * CAP + ranks_of(requested)
    slot_of = jnp.sum(
        (local_src[:, None] == catalog[None, :]).astype(jnp.int32) * slot_table.reshape(-1)[None, :],
        axis=1,
    )
    batches = features.shape[0]
    row_total = features.shape[1] * sections
    all_inputs = row_parts.transpose(1, 0, 2, 3).reshape(batches, row_total, -1)
    piece_rows = 8
    splits = row_total // piece_rows
    first_blocks = all_inputs.reshape(batches * splits, piece_rows, blocks_own, block_size)
    first_blocks = first_blocks.transpose(0, 2, 1, 3)
    finished = run_pipeline(
        first_blocks,
        local_w.reshape(blocks_own, nonzero_count * block_size, block_size),
        bias[0].reshape(blocks_own, 1, block_size),
        slot_of,
        outgoing_next,
        outgoing,
        sections,
        owners,
    )
    finished = finished.reshape(batches, splits, blocks_own, piece_rows, block_size)
    completed = finished.transpose(0, 1, 3, 2, 4).reshape(
        batches, row_total, blocks_own * block_size
    )
    own_rows = row_total // sections
    outgoing_rows = completed.reshape(batches, sections, own_rows, blocks_own * block_size)
    own_result = deliver_rows(outgoing_rows.transpose(1, 0, 2, 3), sections)
    row_ids = section_idx * own_rows + jnp.arange(own_rows, dtype=jnp.int32)
    row_mask = row_ids[None, :] < batch_rows[:, None]
    return jnp.where(row_mask[:, :, None], own_result, jnp.zeros_like(own_result))


def solution(mesh):
    in_specs = (
        P(None, "section", "col"),
        P("section", "col", None, None, None),
        P("section", "col", None),
        P("section", "col"),
        P(),
    )
    out_specs = P(None, "section", "col")
    return jax.shard_map(body, mesh=mesh, in_specs=in_specs, out_specs=out_specs, check_vma=False)
```

```python
import functools

import jax
import jax.numpy as jnp
from jax import lax
from jax.experimental import pallas as pl
from jax.experimental.pallas import tpu as pltpu
from jax.sharding import PartitionSpec as P

CAP = 2
MESH_ID = pl.DeviceIdType.MESH


def pipeline_kernel(
    sections, owners, batches, first_ref, w_ref, b_ref, slot_ref, next_ref, first_list_ref,
    out_ref, *scratch,
):
    recv = scratch[:batches]
    send0 = scratch[batches:2 * batches]
    send_sem, recv_sem, local_sem, send0_sem = scratch[2 * batches:]
    me_s = lax.axis_index("section")
    me_c = lax.axis_index("col")
    blocks_own = w_ref.shape[0]
    nonzero_count = slot_ref.shape[0] // blocks_own
    barrier = pltpu.get_barrier_semaphore()

    @pl.when(me_s > 0)
    def _():
        for d in range(owners):
            pl.semaphore_signal(barrier, inc=1, device_id=(me_s - 1, d), device_id_type=MESH_ID)

    @pl.when(me_s < sections - 1)
    def _():
        for d in range(owners):
            pl.semaphore_signal(barrier, inc=1, device_id=(me_s + 1, d), device_id_type=MESH_ID)

    @pl.when(me_s == 0)
    def _():
        for d in range(owners):

            @pl.when(me_c != d)
            def _():
                pl.semaphore_signal(barrier, inc=1, device_id=(0, d), device_id_type=MESH_ID)

    is_first = (me_s == 0).astype(jnp.int32)
    peers = owners * (
        (me_s > 0).astype(jnp.int32) + (me_s < sections - 1).astype(jnp.int32)
    ) + is_first * (owners - 1)
    pl.semaphore_wait(barrier, peers)

    def first_copy(m, d):
        return pltpu.make_async_remote_copy(
            src_ref=send0[m].at[pl.ds(d * CAP, CAP)],
            dst_ref=recv[m].at[pl.ds(me_c * CAP, CAP)],
            send_sem=send0_sem.at[m, d],
            recv_sem=recv_sem.at[m, me_c],
            device_id=(0, d),
            device_id_type=MESH_ID,
        )

    def first_local(m):
        return pltpu.make_async_copy(
            send0[m].at[pl.ds(me_c * CAP, CAP)],
            recv[m].at[pl.ds(me_c * CAP, CAP)],
            local_sem.at[m],
        )

    @pl.when(me_s == 0)
    def _():
        for m in range(batches):

            def stage_first(i, carry):
                send0[m][i] = first_ref[m, first_list_ref[i]]
                return carry

            lax.fori_loop(0, owners * CAP, stage_first, 0, unroll=True)
            for d in range(owners):

                @pl.when(me_c != d)
                def _():
                    first_copy(m, d).start()

            first_local(m).start()

    def outgoing_copy(m, d):
        return pltpu.make_async_remote_copy(
            src_ref=out_ref.at[m, pl.ds(d * CAP, CAP)],
            dst_ref=recv[m].at[pl.ds(me_c * CAP, CAP)],
            send_sem=send_sem.at[m, d],
            recv_sem=recv_sem.at[m, me_c],
            device_id=(me_s + 1, d),
            device_id_type=MESH_ID,
        )

    for m in range(batches):

        @pl.when(me_s == 0)
        def _():
            first_local(m).wait()
            for e in range(owners):

                @pl.when(me_c != e)
                def _():
                    pltpu.make_async_remote_copy(
                        src_ref=send0[m].at[pl.ds(e * CAP, CAP)],
                        dst_ref=recv[m].at[pl.ds(e * CAP, CAP)],
                        send_sem=send0_sem.at[m, e],
                        recv_sem=recv_sem.at[m, e],
                        device_id=(0, e),
                        device_id_type=MESH_ID,
                    ).wait_recv()

        @pl.when(me_s > 0)
        def _():
            for e in range(owners):
                pltpu.make_async_remote_copy(
                    src_ref=out_ref.at[m, pl.ds(e * CAP, CAP)],
                    dst_ref=recv[m].at[pl.ds(e * CAP, CAP)],
                    send_sem=send_sem.at[m, e],
                    recv_sem=recv_sem.at[m, e],
                    device_id=(me_s - 1, e),
                    device_id_type=MESH_ID,
                ).wait_recv()

        def block_step(j, carry):
            block = next_ref[j]
            picked = jnp.concatenate(
                [recv[m][slot_ref[block * nonzero_count + k]] for k in range(nonzero_count)],
                axis=-1,
            )
            acc = jnp.dot(picked, w_ref[block], preferred_element_type=jnp.float32)
            out_ref[m, j] = jnp.clip(acc + b_ref[block], 0.0, 32.0).astype(out_ref.dtype)
            return carry

        lax.fori_loop(0, blocks_own, block_step, 0, unroll=True)

        @pl.when(me_s < sections - 1)
        def _():
            for d in range(owners):
                outgoing_copy(m, d).start()

    @pl.when(me_s < sections - 1)
    def _():
        for m in range(batches):
            for d in range(owners):
                outgoing_copy(m, d).wait_send()

    @pl.when(me_s == 0)
    def _():
        for m in range(batches):
            for d in range(owners):

                @pl.when(me_c != d)
                def _():
                    first_copy(m, d).wait_send()


def run_pipeline(
    first_blocks, local_w, local_bias, slot_of, outgoing_next, outgoing, sections, owners
):
    batches = first_blocks.shape[0]
    blocks_own = local_w.shape[0]
    rows = first_blocks.shape[2]
    slots_shape = (owners * CAP,) + first_blocks.shape[2:]
    block_size = local_w.shape[-1]
    vmem = pl.BlockSpec(memory_space=pltpu.VMEM)
    smem = pl.BlockSpec(memory_space=pltpu.SMEM)
    return pl.pallas_call(
        functools.partial(pipeline_kernel, sections, owners, batches),
        out_shape=jax.ShapeDtypeStruct((batches, blocks_own, rows, block_size), jnp.bfloat16),
        in_specs=[vmem, vmem, vmem, smem, smem, smem],
        out_specs=vmem,
        scratch_shapes=[
            *[pltpu.VMEM(slots_shape, jnp.bfloat16) for _ in range(2 * batches)],
            pltpu.SemaphoreType.DMA((batches, owners)),
            pltpu.SemaphoreType.DMA((batches, owners)),
            pltpu.SemaphoreType.DMA((batches,)),
            pltpu.SemaphoreType.DMA((batches, owners)),
        ],
        compiler_params=pltpu.CompilerParams(collective_id=0, has_side_effects=True),
    )(first_blocks, local_w, local_bias, slot_of, outgoing_next, outgoing)


def pattern_kernel(sections, owners, src_ref, feat_ref, own_ref, nxt_ref, rows_ref, *sems):
    own_send, own_recv, nxt_send, nxt_recv, local_sem, rows_send, rows_recv, rows_sem = sems
    me_s = lax.axis_index("section")
    me_c = lax.axis_index("col")
    barrier = pltpu.get_barrier_semaphore()
    for d in range(owners):

        @pl.when(me_c != d)
        def _():
            pl.semaphore_signal(barrier, inc=1, device_id=(me_s, d), device_id_type=MESH_ID)

    @pl.when(me_s > 0)
    def _():
        for d in range(owners):
            pl.semaphore_signal(barrier, inc=1, device_id=(me_s - 1, d), device_id_type=MESH_ID)

    @pl.when(me_s < sections - 1)
    def _():
        for d in range(owners):
            pl.semaphore_signal(barrier, inc=1, device_id=(me_s + 1, d), device_id_type=MESH_ID)

    @pl.when(me_s > 0)
    def _():
        pl.semaphore_signal(barrier, inc=1, device_id=(0, me_c), device_id_type=MESH_ID)

    @pl.when(me_s == 0)
    def _():
        for r in range(1, sections):
            pl.semaphore_signal(barrier, inc=1, device_id=(r, me_c), device_id_type=MESH_ID)

    is_first = (me_s == 0).astype(jnp.int32)
    peers = (owners - 1) + owners * (
        (me_s > 0).astype(jnp.int32) + (me_s < sections - 1).astype(jnp.int32)
    ) + is_first * (sections - 1) + (1 - is_first)
    pl.semaphore_wait(barrier, peers)

    def own_copy(d, e):
        return pltpu.make_async_remote_copy(
            src_ref=src_ref,
            dst_ref=own_ref.at[e],
            send_sem=own_send.at[d],
            recv_sem=own_recv.at[e],
            device_id=(me_s, d),
            device_id_type=MESH_ID,
        )

    def nxt_copy(dev_s, d, e):
        return pltpu.make_async_remote_copy(
            src_ref=src_ref,
            dst_ref=nxt_ref.at[e],
            send_sem=nxt_send.at[d],
            recv_sem=nxt_recv.at[e],
            device_id=(dev_s, d),
            device_id_type=MESH_ID,
        )

    for d in range(owners):

        @pl.when(me_c != d)
        def _():
            own_copy(d, me_c).start()

    @pl.when(me_s > 0)
    def _():
        for d in range(owners):
            nxt_copy(me_s - 1, d, me_c).start()

    def rows_copy(r):
        return pltpu.make_async_remote_copy(
            src_ref=feat_ref,
            dst_ref=rows_ref.at[r],
            send_sem=rows_send,
            recv_sem=rows_recv.at[r],
            device_id=(0, me_c),
            device_id_type=MESH_ID,
        )

    @pl.when(me_s > 0)
    def _():
        rows_copy(me_s).start()

    @pl.when(me_s == 0)
    def _():
        own_rows = pltpu.make_async_copy(feat_ref, rows_ref.at[0], rows_sem)
        own_rows.start()
        own_rows.wait()

    mine = pltpu.make_async_copy(src_ref, own_ref.at[me_c], local_sem)
    mine.start()
    mine.wait()
    for d in range(owners):

        @pl.when(me_c != d)
        def _():
            own_copy(d, me_c).wait_send()
            own_copy(d, d).wait_recv()

    @pl.when(me_s > 0)
    def _():
        for d in range(owners):
            nxt_copy(me_s - 1, d, me_c).wait_send()

    @pl.when(me_s < sections - 1)
    def _():
        for e in range(owners):
            nxt_copy(me_s + 1, e, e).wait_recv()

    @pl.when(me_s > 0)
    def _():
        rows_copy(me_s).wait_send()

    @pl.when(me_s == 0)
    def _():
        for r in range(1, sections):
            rows_copy(r).wait_recv()


def exchange_patterns(local_sources, features, sections, owners):
    table = jax.ShapeDtypeStruct((owners,) + local_sources.shape, local_sources.dtype)
    rows = jax.ShapeDtypeStruct((sections,) + features.shape, features.dtype)
    anywhere = pl.BlockSpec(memory_space=pl.ANY)
    return pl.pallas_call(
        functools.partial(pattern_kernel, sections, owners),
        out_shape=(table, table, rows),
        in_specs=[anywhere, anywhere],
        out_specs=(anywhere, anywhere, anywhere),
        scratch_shapes=[pltpu.SemaphoreType.DMA((owners,)) for _ in range(4)]
        + [
            pltpu.SemaphoreType.DMA(()),
            pltpu.SemaphoreType.DMA(()),
            pltpu.SemaphoreType.DMA((sections,)),
            pltpu.SemaphoreType.DMA(()),
        ],
        compiler_params=pltpu.CompilerParams(collective_id=1, has_side_effects=True),
    )(local_sources, features)


def rows_kernel(sections, src_ref, out_ref, send_sem, recv_sem, local_sem):
    me_s = lax.axis_index("section")
    me_c = lax.axis_index("col")
    last = sections - 1
    barrier = pltpu.get_barrier_semaphore()

    @pl.when(me_s == last)
    def _():
        for r in range(last):
            pl.semaphore_signal(barrier, inc=1, device_id=(r, me_c), device_id_type=MESH_ID)

    @pl.when(me_s != last)
    def _():
        pl.semaphore_signal(barrier, inc=1, device_id=(last, me_c), device_id_type=MESH_ID)

    is_last = (me_s == last).astype(jnp.int32)
    pl.semaphore_wait(barrier, is_last * last + (1 - is_last))

    def row_copy(r):
        return pltpu.make_async_remote_copy(
            src_ref=src_ref.at[r],
            dst_ref=out_ref,
            send_sem=send_sem.at[r],
            recv_sem=recv_sem,
            device_id=(r, me_c),
            device_id_type=MESH_ID,
        )

    @pl.when(me_s == last)
    def _():
        for r in range(last):
            row_copy(r).start()
        mine = pltpu.make_async_copy(src_ref.at[last], out_ref, local_sem)
        mine.start()
        mine.wait()
        for r in range(last):
            row_copy(r).wait_send()

    @pl.when(me_s != last)
    def _():
        row_copy(0).wait_recv()


def deliver_rows(row_parts, sections):
    anywhere = pl.BlockSpec(memory_space=pl.ANY)
    return pl.pallas_call(
        functools.partial(rows_kernel, sections),
        out_shape=jax.ShapeDtypeStruct(row_parts.shape[1:], row_parts.dtype),
        in_specs=[anywhere],
        out_specs=anywhere,
        scratch_shapes=[
            pltpu.SemaphoreType.DMA((sections,)),
            pltpu.SemaphoreType.DMA(()),
            pltpu.SemaphoreType.DMA(()),
        ],
        compiler_params=pltpu.CompilerParams(collective_id=2, has_side_effects=True),
    )(row_parts)


def body(features, weights, sources, bias, batch_rows):
    sections = lax.axis_size("section")
    owners = lax.axis_size("col")
    section_idx = lax.axis_index("section")
    col_idx = lax.axis_index("col")
    local_w = weights[0]
    blocks_own = local_w.shape[0]
    nonzero_count = local_w.shape[1]
    block_size = local_w.shape[2]
    local_src = sources[0].reshape(blocks_own * nonzero_count)
    own_table, next_table, row_parts = exchange_patterns(sources[0], features, sections, owners)
    local_rows = jnp.arange(blocks_own, dtype=jnp.int32)
    below = (local_rows[:, None] <= local_rows[None, :]).astype(jnp.float32)
    slot_ids = jnp.arange(CAP, dtype=jnp.int32)

    def ranks_of(wanted):
        return jnp.einsum("...i,ij->...j", wanted.astype(jnp.float32), below).astype(jnp.int32) - 1

    def sender_list(table):
        flat = table.reshape(owners, blocks_own * nonzero_count)
        mine = col_idx * blocks_own + local_rows
        wanted = jnp.any(flat[:, :, None] == mine[None, None, :], axis=1)
        chosen = wanted[:, None, :] & (ranks_of(wanted)[:, None, :] == slot_ids[None, :, None])
        return jnp.sum(chosen.astype(jnp.int32) * local_rows[None, None, :], axis=2)

    both_lists = jax.vmap(sender_list)(jnp.stack([own_table, next_table]))
    outgoing = both_lists[0].reshape(owners * CAP)
    outgoing_next = jnp.where(
        section_idx == sections - 1,
        jnp.arange(owners * CAP, dtype=jnp.int32),
        both_lists[1].reshape(owners * CAP),
    )
    catalog = jnp.arange(owners * blocks_own, dtype=jnp.int32)
    requested = jnp.any(local_src[:, None] == catalog[None, :], axis=0).reshape(owners, blocks_own)
    slot_table = jnp.arange(owners, dtype=jnp.int32)[:, None] * CAP + ranks_of(requested)
    slot_of = jnp.sum(
        (local_src[:, None] == catalog[None, :]).astype(jnp.int32) * slot_table.reshape(-1)[None, :],
        axis=1,
    )
    batches = features.shape[0]
    row_total = features.shape[1] * sections
    all_inputs = row_parts.transpose(1, 0, 2, 3).reshape(batches, row_total, -1)
    piece_rows = 8
    splits = row_total // piece_rows
    first_blocks = all_inputs.reshape(batches * splits, piece_rows, blocks_own, block_size)
    first_blocks = first_blocks.transpose(0, 2, 1, 3)
    finished = run_pipeline(
        first_blocks,
        local_w.reshape(blocks_own, nonzero_count * block_size, block_size),
        bias[0].reshape(blocks_own, 1, block_size),
        slot_of,
        outgoing_next,
        outgoing,
        sections,
        owners,
    )
    finished = finished.reshape(batches, splits, blocks_own, piece_rows, block_size)
    completed = finished.transpose(0, 1, 3, 2, 4).reshape(
        batches, row_total, blocks_own * block_size
    )
    own_rows = row_total // sections
    outgoing_rows = completed.reshape(batches, sections, own_rows, blocks_own * block_size)
    own_result = deliver_rows(outgoing_rows.transpose(1, 0, 2, 3), sections)
    row_ids = section_idx * own_rows + jnp.arange(own_rows, dtype=jnp.int32)
    row_mask = row_ids[None, :] < batch_rows[:, None]
    return jnp.where(row_mask[:, :, None], own_result, jnp.zeros_like(own_result))


def solution(mesh):
    in_specs = (
        P(None, "section", "col"),
        P("section", "col", None, None, None),
        P("section", "col", None),
        P("section", "col"),
        P(),
    )
    out_specs = P(None, "section", "col")
    return jax.shard_map(body, mesh=mesh, in_specs=in_specs, out_specs=out_specs, check_vma=False)
```

```python
import functools

import jax
import jax.numpy as jnp
from jax import lax
from jax.experimental import pallas as pl
from jax.experimental.pallas import tpu as pltpu
from jax.sharding import PartitionSpec as P

CAP = 2
MESH_ID = pl.DeviceIdType.MESH


def pipeline_kernel(
    sections, owners, batches, first_ref, w_ref, b_ref, slot_ref, next_ref, first_list_ref,
    out_ref, *scratch,
):
    recv = scratch[:batches]
    send0 = scratch[batches:2 * batches]
    send_sem, recv_sem, local_sem, send0_sem = scratch[2 * batches:]
    me_s = lax.axis_index("section")
    me_c = lax.axis_index("col")
    blocks_own = w_ref.shape[0]
    nonzero_count = slot_ref.shape[0] // blocks_own
    barrier = pltpu.get_barrier_semaphore()

    @pl.when(me_s > 0)
    def _():
        for d in range(owners):
            pl.semaphore_signal(barrier, inc=1, device_id=(me_s - 1, d), device_id_type=MESH_ID)

    @pl.when(me_s < sections - 1)
    def _():
        for d in range(owners):
            pl.semaphore_signal(barrier, inc=1, device_id=(me_s + 1, d), device_id_type=MESH_ID)

    @pl.when(me_s == 0)
    def _():
        for d in range(owners):

            @pl.when(me_c != d)
            def _():
                pl.semaphore_signal(barrier, inc=1, device_id=(0, d), device_id_type=MESH_ID)

    is_first = (me_s == 0).astype(jnp.int32)
    peers = owners * (
        (me_s > 0).astype(jnp.int32) + (me_s < sections - 1).astype(jnp.int32)
    ) + is_first * (owners - 1)
    pl.semaphore_wait(barrier, peers)

    def first_copy(m, d):
        return pltpu.make_async_remote_copy(
            src_ref=send0[m].at[pl.ds(d * CAP, CAP)],
            dst_ref=recv[m].at[pl.ds(me_c * CAP, CAP)],
            send_sem=send0_sem.at[m, d],
            recv_sem=recv_sem.at[m, me_c],
            device_id=(0, d),
            device_id_type=MESH_ID,
        )

    def first_local(m):
        return pltpu.make_async_copy(
            send0[m].at[pl.ds(me_c * CAP, CAP)],
            recv[m].at[pl.ds(me_c * CAP, CAP)],
            local_sem.at[m],
        )

    @pl.when(me_s == 0)
    def _():
        for m in range(batches):

            def stage_first(i, carry):
                send0[m][i] = first_ref[m, first_list_ref[i]]
                return carry

            lax.fori_loop(0, owners * CAP, stage_first, 0, unroll=True)
            for d in range(owners):

                @pl.when(me_c != d)
                def _():
                    first_copy(m, d).start()

            first_local(m).start()

    def outgoing_copy(m, d):
        return pltpu.make_async_remote_copy(
            src_ref=out_ref.at[m, pl.ds(d * CAP, CAP)],
            dst_ref=recv[m].at[pl.ds(me_c * CAP, CAP)],
            send_sem=send_sem.at[m, d],
            recv_sem=recv_sem.at[m, me_c],
            device_id=(me_s + 1, d),
            device_id_type=MESH_ID,
        )

    for m in range(batches):

        @pl.when(me_s == 0)
        def _():
            first_local(m).wait()
            for e in range(owners):

                @pl.when(me_c != e)
                def _():
                    pltpu.make_async_remote_copy(
                        src_ref=send0[m].at[pl.ds(e * CAP, CAP)],
                        dst_ref=recv[m].at[pl.ds(e * CAP, CAP)],
                        send_sem=send0_sem.at[m, e],
                        recv_sem=recv_sem.at[m, e],
                        device_id=(0, e),
                        device_id_type=MESH_ID,
                    ).wait_recv()

        @pl.when(me_s > 0)
        def _():
            for e in range(owners):
                pltpu.make_async_remote_copy(
                    src_ref=out_ref.at[m, pl.ds(e * CAP, CAP)],
                    dst_ref=recv[m].at[pl.ds(e * CAP, CAP)],
                    send_sem=send_sem.at[m, e],
                    recv_sem=recv_sem.at[m, e],
                    device_id=(me_s - 1, e),
                    device_id_type=MESH_ID,
                ).wait_recv()

        def block_step(j, carry):
            block = next_ref[j]
            picked = jnp.concatenate(
                [recv[m][slot_ref[block * nonzero_count + k]] for k in range(nonzero_count)],
                axis=-1,
            )
            acc = jnp.dot(picked, w_ref[block], preferred_element_type=jnp.float32)
            out_ref[m, j] = jnp.clip(acc + b_ref[block], 0.0, 32.0).astype(out_ref.dtype)
            return carry

        lax.fori_loop(0, blocks_own, block_step, 0, unroll=True)

        @pl.when(me_s < sections - 1)
        def _():
            for d in range(owners):
                outgoing_copy(m, d).start()

    @pl.when(me_s < sections - 1)
    def _():
        for m in range(batches):
            for d in range(owners):
                outgoing_copy(m, d).wait_send()

    @pl.when(me_s == 0)
    def _():
        for m in range(batches):
            for d in range(owners):

                @pl.when(me_c != d)
                def _():
                    first_copy(m, d).wait_send()


def run_pipeline(
    first_blocks, local_w, local_bias, slot_of, outgoing_next, outgoing, sections, owners
):
    batches = first_blocks.shape[0]
    blocks_own = local_w.shape[0]
    rows = first_blocks.shape[2]
    slots_shape = (owners * CAP,) + first_blocks.shape[2:]
    block_size = local_w.shape[-1]
    vmem = pl.BlockSpec(memory_space=pltpu.VMEM)
    smem = pl.BlockSpec(memory_space=pltpu.SMEM)
    return pl.pallas_call(
        functools.partial(pipeline_kernel, sections, owners, batches),
        out_shape=jax.ShapeDtypeStruct((batches, blocks_own, rows, block_size), jnp.bfloat16),
        in_specs=[vmem, vmem, vmem, smem, smem, smem],
        out_specs=vmem,
        scratch_shapes=[
            *[pltpu.VMEM(slots_shape, jnp.bfloat16) for _ in range(2 * batches)],
            pltpu.SemaphoreType.DMA((batches, owners)),
            pltpu.SemaphoreType.DMA((batches, owners)),
            pltpu.SemaphoreType.DMA((batches,)),
            pltpu.SemaphoreType.DMA((batches, owners)),
        ],
        compiler_params=pltpu.CompilerParams(collective_id=0, has_side_effects=True),
    )(first_blocks, local_w, local_bias, slot_of, outgoing_next, outgoing)


def pattern_kernel(sections, owners, src_ref, feat_ref, own_ref, nxt_ref, rows_ref, *sems):
    own_send, own_recv, nxt_send, nxt_recv, local_sem, rows_send, rows_recv, rows_sem = sems
    me_s = lax.axis_index("section")
    me_c = lax.axis_index("col")
    barrier = pltpu.get_barrier_semaphore()
    for d in range(owners):

        @pl.when(me_c != d)
        def _():
            pl.semaphore_signal(barrier, inc=1, device_id=(me_s, d), device_id_type=MESH_ID)

    @pl.when(me_s > 0)
    def _():
        for d in range(owners):
            pl.semaphore_signal(barrier, inc=1, device_id=(me_s - 1, d), device_id_type=MESH_ID)

    @pl.when(me_s < sections - 1)
    def _():
        for d in range(owners):
            pl.semaphore_signal(barrier, inc=1, device_id=(me_s + 1, d), device_id_type=MESH_ID)

    @pl.when(me_s > 0)
    def _():
        pl.semaphore_signal(barrier, inc=1, device_id=(0, me_c), device_id_type=MESH_ID)

    @pl.when(me_s == 0)
    def _():
        for r in range(1, sections):
            pl.semaphore_signal(barrier, inc=1, device_id=(r, me_c), device_id_type=MESH_ID)

    is_first = (me_s == 0).astype(jnp.int32)
    peers = (owners - 1) + owners * (
        (me_s > 0).astype(jnp.int32) + (me_s < sections - 1).astype(jnp.int32)
    ) + is_first * (sections - 1) + (1 - is_first)
    pl.semaphore_wait(barrier, peers)

    def own_copy(d, e):
        return pltpu.make_async_remote_copy(
            src_ref=src_ref,
            dst_ref=own_ref.at[e],
            send_sem=own_send.at[d],
            recv_sem=own_recv.at[e],
            device_id=(me_s, d),
            device_id_type=MESH_ID,
        )

    def nxt_copy(dev_s, d, e):
        return pltpu.make_async_remote_copy(
            src_ref=src_ref,
            dst_ref=nxt_ref.at[e],
            send_sem=nxt_send.at[d],
            recv_sem=nxt_recv.at[e],
            device_id=(dev_s, d),
            device_id_type=MESH_ID,
        )

    for d in range(owners):

        @pl.when(me_c != d)
        def _():
            own_copy(d, me_c).start()

    @pl.when(me_s > 0)
    def _():
        for d in range(owners):
            nxt_copy(me_s - 1, d, me_c).start()

    def rows_copy(r):
        return pltpu.make_async_remote_copy(
            src_ref=feat_ref,
            dst_ref=rows_ref.at[:, r],
            send_sem=rows_send,
            recv_sem=rows_recv.at[r],
            device_id=(0, me_c),
            device_id_type=MESH_ID,
        )

    @pl.when(me_s > 0)
    def _():
        rows_copy(me_s).start()

    @pl.when(me_s == 0)
    def _():
        own_rows = pltpu.make_async_copy(feat_ref, rows_ref.at[:, 0], rows_sem)
        own_rows.start()
        own_rows.wait()

    mine = pltpu.make_async_copy(src_ref, own_ref.at[me_c], local_sem)
    mine.start()
    mine.wait()
    for d in range(owners):

        @pl.when(me_c != d)
        def _():
            own_copy(d, me_c).wait_send()
            own_copy(d, d).wait_recv()

    @pl.when(me_s > 0)
    def _():
        for d in range(owners):
            nxt_copy(me_s - 1, d, me_c).wait_send()

    @pl.when(me_s < sections - 1)
    def _():
        for e in range(owners):
            nxt_copy(me_s + 1, e, e).wait_recv()

    @pl.when(me_s > 0)
    def _():
        rows_copy(me_s).wait_send()

    @pl.when(me_s == 0)
    def _():
        for r in range(1, sections):
            rows_copy(r).wait_recv()


def exchange_patterns(local_sources, features, sections, owners):
    table = jax.ShapeDtypeStruct((owners,) + local_sources.shape, local_sources.dtype)
    rows = jax.ShapeDtypeStruct(
        (features.shape[0], sections) + features.shape[1:], features.dtype
    )
    anywhere = pl.BlockSpec(memory_space=pl.ANY)
    return pl.pallas_call(
        functools.partial(pattern_kernel, sections, owners),
        out_shape=(table, table, rows),
        in_specs=[anywhere, anywhere],
        out_specs=(anywhere, anywhere, anywhere),
        scratch_shapes=[pltpu.SemaphoreType.DMA((owners,)) for _ in range(4)]
        + [
            pltpu.SemaphoreType.DMA(()),
            pltpu.SemaphoreType.DMA(()),
            pltpu.SemaphoreType.DMA((sections,)),
            pltpu.SemaphoreType.DMA(()),
        ],
        compiler_params=pltpu.CompilerParams(collective_id=1, has_side_effects=True),
    )(local_sources, features)


def rows_kernel(sections, src_ref, out_ref, send_sem, recv_sem, local_sem):
    me_s = lax.axis_index("section")
    me_c = lax.axis_index("col")
    last = sections - 1
    barrier = pltpu.get_barrier_semaphore()

    @pl.when(me_s == last)
    def _():
        for r in range(last):
            pl.semaphore_signal(barrier, inc=1, device_id=(r, me_c), device_id_type=MESH_ID)

    @pl.when(me_s != last)
    def _():
        pl.semaphore_signal(barrier, inc=1, device_id=(last, me_c), device_id_type=MESH_ID)

    is_last = (me_s == last).astype(jnp.int32)
    pl.semaphore_wait(barrier, is_last * last + (1 - is_last))

    def row_copy(r):
        return pltpu.make_async_remote_copy(
            src_ref=src_ref.at[r],
            dst_ref=out_ref,
            send_sem=send_sem.at[r],
            recv_sem=recv_sem,
            device_id=(r, me_c),
            device_id_type=MESH_ID,
        )

    @pl.when(me_s == last)
    def _():
        for r in range(last):
            row_copy(r).start()
        mine = pltpu.make_async_copy(src_ref.at[last], out_ref, local_sem)
        mine.start()
        mine.wait()
        for r in range(last):
            row_copy(r).wait_send()

    @pl.when(me_s != last)
    def _():
        row_copy(0).wait_recv()


def deliver_rows(row_parts, sections):
    anywhere = pl.BlockSpec(memory_space=pl.ANY)
    return pl.pallas_call(
        functools.partial(rows_kernel, sections),
        out_shape=jax.ShapeDtypeStruct(row_parts.shape[1:], row_parts.dtype),
        in_specs=[anywhere],
        out_specs=anywhere,
        scratch_shapes=[
            pltpu.SemaphoreType.DMA((sections,)),
            pltpu.SemaphoreType.DMA(()),
            pltpu.SemaphoreType.DMA(()),
        ],
        compiler_params=pltpu.CompilerParams(collective_id=2, has_side_effects=True),
    )(row_parts)


def body(features, weights, sources, bias, batch_rows):
    sections = lax.axis_size("section")
    owners = lax.axis_size("col")
    section_idx = lax.axis_index("section")
    col_idx = lax.axis_index("col")
    local_w = weights[0]
    blocks_own = local_w.shape[0]
    nonzero_count = local_w.shape[1]
    block_size = local_w.shape[2]
    local_src = sources[0].reshape(blocks_own * nonzero_count)
    own_table, next_table, row_parts = exchange_patterns(sources[0], features, sections, owners)
    local_rows = jnp.arange(blocks_own, dtype=jnp.int32)
    below = (local_rows[:, None] <= local_rows[None, :]).astype(jnp.float32)
    slot_ids = jnp.arange(CAP, dtype=jnp.int32)

    def ranks_of(wanted):
        return jnp.einsum("...i,ij->...j", wanted.astype(jnp.float32), below).astype(jnp.int32) - 1

    def sender_list(table):
        flat = table.reshape(owners, blocks_own * nonzero_count)
        mine = col_idx * blocks_own + local_rows
        wanted = jnp.any(flat[:, :, None] == mine[None, None, :], axis=1)
        chosen = wanted[:, None, :] & (ranks_of(wanted)[:, None, :] == slot_ids[None, :, None])
        return jnp.sum(chosen.astype(jnp.int32) * local_rows[None, None, :], axis=2)

    both_lists = jax.vmap(sender_list)(jnp.stack([own_table, next_table]))
    outgoing = both_lists[0].reshape(owners * CAP)
    outgoing_next = jnp.where(
        section_idx == sections - 1,
        jnp.arange(owners * CAP, dtype=jnp.int32),
        both_lists[1].reshape(owners * CAP),
    )
    catalog = jnp.arange(owners * blocks_own, dtype=jnp.int32)
    requested = jnp.any(local_src[:, None] == catalog[None, :], axis=0).reshape(owners, blocks_own)
    slot_table = jnp.arange(owners, dtype=jnp.int32)[:, None] * CAP + ranks_of(requested)
    slot_of = jnp.sum(
        (local_src[:, None] == catalog[None, :]).astype(jnp.int32) * slot_table.reshape(-1)[None, :],
        axis=1,
    )
    batches = features.shape[0]
    row_total = features.shape[1] * sections
    all_inputs = row_parts.reshape(batches, row_total, -1)
    piece_rows = 8
    splits = row_total // piece_rows
    first_blocks = all_inputs.reshape(batches * splits, piece_rows, blocks_own, block_size)
    first_blocks = first_blocks.transpose(0, 2, 1, 3)
    finished = run_pipeline(
        first_blocks,
        local_w.reshape(blocks_own, nonzero_count * block_size, block_size),
        bias[0].reshape(blocks_own, 1, block_size),
        slot_of,
        outgoing_next,
        outgoing,
        sections,
        owners,
    )
    finished = finished.reshape(batches, splits, blocks_own, piece_rows, block_size)
    completed = finished.transpose(0, 1, 3, 2, 4).reshape(
        batches, row_total, blocks_own * block_size
    )
    own_rows = row_total // sections
    outgoing_rows = completed.reshape(batches, sections, own_rows, blocks_own * block_size)
    own_result = deliver_rows(outgoing_rows.transpose(1, 0, 2, 3), sections)
    row_ids = section_idx * own_rows + jnp.arange(own_rows, dtype=jnp.int32)
    row_mask = row_ids[None, :] < batch_rows[:, None]
    return jnp.where(row_mask[:, :, None], own_result, jnp.zeros_like(own_result))


def solution(mesh):
    in_specs = (
        P(None, "section", "col"),
        P("section", "col", None, None, None),
        P("section", "col", None),
        P("section", "col"),
        P(),
    )
    out_specs = P(None, "section", "col")
    return jax.shard_map(body, mesh=mesh, in_specs=in_specs, out_specs=out_specs, check_vma=False)
```

```python
import functools

import jax
import jax.numpy as jnp
from jax import lax
from jax.experimental import pallas as pl
from jax.experimental.pallas import tpu as pltpu
from jax.sharding import PartitionSpec as P

CAP = 2
MESH_ID = pl.DeviceIdType.MESH


def pipeline_kernel(
    sections, owners, batches, first_ref, w_ref, b_ref, slot_ref, next_ref, first_list_ref,
    out_ref, *scratch,
):
    recv = scratch[:batches]
    send0 = scratch[batches:2 * batches]
    send_sem, recv_sem, local_sem, send0_sem = scratch[2 * batches:]
    me_s = lax.axis_index("section")
    me_c = lax.axis_index("col")
    blocks_own = w_ref.shape[0]
    nonzero_count = slot_ref.shape[0] // blocks_own
    barrier = pltpu.get_barrier_semaphore()

    @pl.when(me_s > 0)
    def _():
        for d in range(owners):
            pl.semaphore_signal(barrier, inc=1, device_id=(me_s - 1, d), device_id_type=MESH_ID)

    @pl.when(me_s < sections - 1)
    def _():
        for d in range(owners):
            pl.semaphore_signal(barrier, inc=1, device_id=(me_s + 1, d), device_id_type=MESH_ID)

    @pl.when(me_s == 0)
    def _():
        for d in range(owners):

            @pl.when(me_c != d)
            def _():
                pl.semaphore_signal(barrier, inc=1, device_id=(0, d), device_id_type=MESH_ID)

    is_first = (me_s == 0).astype(jnp.int32)
    peers = owners * (
        (me_s > 0).astype(jnp.int32) + (me_s < sections - 1).astype(jnp.int32)
    ) + is_first * (owners - 1)
    pl.semaphore_wait(barrier, peers)

    def first_copy(m, d):
        return pltpu.make_async_remote_copy(
            src_ref=send0[m].at[pl.ds(d * CAP, CAP)],
            dst_ref=recv[m].at[pl.ds(me_c * CAP, CAP)],
            send_sem=send0_sem.at[m, d],
            recv_sem=recv_sem.at[m, me_c],
            device_id=(0, d),
            device_id_type=MESH_ID,
        )

    def first_local(m):
        return pltpu.make_async_copy(
            send0[m].at[pl.ds(me_c * CAP, CAP)],
            recv[m].at[pl.ds(me_c * CAP, CAP)],
            local_sem.at[m],
        )

    @pl.when(me_s == 0)
    def _():
        for m in range(batches):

            def stage_first(i, carry):
                send0[m][i] = first_ref[m, first_list_ref[i]]
                return carry

            lax.fori_loop(0, owners * CAP, stage_first, 0, unroll=True)
            for d in range(owners):

                @pl.when(me_c != d)
                def _():
                    first_copy(m, d).start()

            first_local(m).start()

    def outgoing_copy(m, d):
        return pltpu.make_async_remote_copy(
            src_ref=out_ref.at[m, pl.ds(d * CAP, CAP)],
            dst_ref=recv[m].at[pl.ds(me_c * CAP, CAP)],
            send_sem=send_sem.at[m, d],
            recv_sem=recv_sem.at[m, me_c],
            device_id=(me_s + 1, d),
            device_id_type=MESH_ID,
        )

    for m in range(batches):

        @pl.when(me_s == 0)
        def _():
            first_local(m).wait()
            for e in range(owners):

                @pl.when(me_c != e)
                def _():
                    pltpu.make_async_remote_copy(
                        src_ref=send0[m].at[pl.ds(e * CAP, CAP)],
                        dst_ref=recv[m].at[pl.ds(e * CAP, CAP)],
                        send_sem=send0_sem.at[m, e],
                        recv_sem=recv_sem.at[m, e],
                        device_id=(0, e),
                        device_id_type=MESH_ID,
                    ).wait_recv()

        @pl.when(me_s > 0)
        def _():
            for e in range(owners):
                pltpu.make_async_remote_copy(
                    src_ref=out_ref.at[m, pl.ds(e * CAP, CAP)],
                    dst_ref=recv[m].at[pl.ds(e * CAP, CAP)],
                    send_sem=send_sem.at[m, e],
                    recv_sem=recv_sem.at[m, e],
                    device_id=(me_s - 1, e),
                    device_id_type=MESH_ID,
                ).wait_recv()

        def block_step(j, carry):
            block = next_ref[j]
            picked = jnp.concatenate(
                [recv[m][slot_ref[block * nonzero_count + k]] for k in range(nonzero_count)],
                axis=-1,
            )
            acc = jnp.dot(picked, w_ref[block], preferred_element_type=jnp.float32)
            out_ref[m, j] = jnp.clip(acc + b_ref[block], 0.0, 32.0).astype(out_ref.dtype)
            return carry

        lax.fori_loop(0, blocks_own, block_step, 0, unroll=True)

        @pl.when(me_s < sections - 1)
        def _():
            for k in range(owners):
                outgoing_copy(m, lax.rem(me_c + k, owners)).start()

    @pl.when(me_s < sections - 1)
    def _():
        for m in range(batches):
            for d in range(owners):
                outgoing_copy(m, d).wait_send()

    @pl.when(me_s == 0)
    def _():
        for m in range(batches):
            for d in range(owners):

                @pl.when(me_c != d)
                def _():
                    first_copy(m, d).wait_send()


def run_pipeline(
    first_blocks, local_w, local_bias, slot_of, outgoing_next, outgoing, sections, owners
):
    batches = first_blocks.shape[0]
    blocks_own = local_w.shape[0]
    rows = first_blocks.shape[2]
    slots_shape = (owners * CAP,) + first_blocks.shape[2:]
    block_size = local_w.shape[-1]
    vmem = pl.BlockSpec(memory_space=pltpu.VMEM)
    smem = pl.BlockSpec(memory_space=pltpu.SMEM)
    return pl.pallas_call(
        functools.partial(pipeline_kernel, sections, owners, batches),
        out_shape=jax.ShapeDtypeStruct((batches, blocks_own, rows, block_size), jnp.bfloat16),
        in_specs=[vmem, vmem, vmem, smem, smem, smem],
        out_specs=vmem,
        scratch_shapes=[
            *[pltpu.VMEM(slots_shape, jnp.bfloat16) for _ in range(2 * batches)],
            pltpu.SemaphoreType.DMA((batches, owners)),
            pltpu.SemaphoreType.DMA((batches, owners)),
            pltpu.SemaphoreType.DMA((batches,)),
            pltpu.SemaphoreType.DMA((batches, owners)),
        ],
        compiler_params=pltpu.CompilerParams(collective_id=0, has_side_effects=True),
    )(first_blocks, local_w, local_bias, slot_of, outgoing_next, outgoing)


def pattern_kernel(sections, owners, src_ref, feat_ref, own_ref, nxt_ref, rows_ref, *sems):
    own_send, own_recv, nxt_send, nxt_recv, local_sem, rows_send, rows_recv, rows_sem = sems
    me_s = lax.axis_index("section")
    me_c = lax.axis_index("col")
    barrier = pltpu.get_barrier_semaphore()
    for d in range(owners):

        @pl.when(me_c != d)
        def _():
            pl.semaphore_signal(barrier, inc=1, device_id=(me_s, d), device_id_type=MESH_ID)

    @pl.when(me_s > 0)
    def _():
        for d in range(owners):
            pl.semaphore_signal(barrier, inc=1, device_id=(me_s - 1, d), device_id_type=MESH_ID)

    @pl.when(me_s < sections - 1)
    def _():
        for d in range(owners):
            pl.semaphore_signal(barrier, inc=1, device_id=(me_s + 1, d), device_id_type=MESH_ID)

    @pl.when(me_s > 0)
    def _():
        pl.semaphore_signal(barrier, inc=1, device_id=(0, me_c), device_id_type=MESH_ID)

    @pl.when(me_s == 0)
    def _():
        for r in range(1, sections):
            pl.semaphore_signal(barrier, inc=1, device_id=(r, me_c), device_id_type=MESH_ID)

    is_first = (me_s == 0).astype(jnp.int32)
    peers = (owners - 1) + owners * (
        (me_s > 0).astype(jnp.int32) + (me_s < sections - 1).astype(jnp.int32)
    ) + is_first * (sections - 1) + (1 - is_first)
    pl.semaphore_wait(barrier, peers)

    def own_copy(d, e):
        return pltpu.make_async_remote_copy(
            src_ref=src_ref,
            dst_ref=own_ref.at[e],
            send_sem=own_send.at[d],
            recv_sem=own_recv.at[e],
            device_id=(me_s, d),
            device_id_type=MESH_ID,
        )

    def nxt_copy(dev_s, d, e):
        return pltpu.make_async_remote_copy(
            src_ref=src_ref,
            dst_ref=nxt_ref.at[e],
            send_sem=nxt_send.at[d],
            recv_sem=nxt_recv.at[e],
            device_id=(dev_s, d),
            device_id_type=MESH_ID,
        )

    for d in range(owners):

        @pl.when(me_c != d)
        def _():
            own_copy(d, me_c).start()

    @pl.when(me_s > 0)
    def _():
        for d in range(owners):
            nxt_copy(me_s - 1, d, me_c).start()

    def rows_copy(r):
        return pltpu.make_async_remote_copy(
            src_ref=feat_ref,
            dst_ref=rows_ref.at[:, r],
            send_sem=rows_send,
            recv_sem=rows_recv.at[r],
            device_id=(0, me_c),
            device_id_type=MESH_ID,
        )

    @pl.when(me_s > 0)
    def _():
        rows_copy(me_s).start()

    @pl.when(me_s == 0)
    def _():
        own_rows = pltpu.make_async_copy(feat_ref, rows_ref.at[:, 0], rows_sem)
        own_rows.start()
        own_rows.wait()

    mine = pltpu.make_async_copy(src_ref, own_ref.at[me_c], local_sem)
    mine.start()
    mine.wait()
    for d in range(owners):

        @pl.when(me_c != d)
        def _():
            own_copy(d, me_c).wait_send()
            own_copy(d, d).wait_recv()

    @pl.when(me_s > 0)
    def _():
        for d in range(owners):
            nxt_copy(me_s - 1, d, me_c).wait_send()

    @pl.when(me_s < sections - 1)
    def _():
        for e in range(owners):
            nxt_copy(me_s + 1, e, e).wait_recv()

    @pl.when(me_s > 0)
    def _():
        rows_copy(me_s).wait_send()

    @pl.when(me_s == 0)
    def _():
        for r in range(1, sections):
            rows_copy(r).wait_recv()


def exchange_patterns(local_sources, features, sections, owners):
    table = jax.ShapeDtypeStruct((owners,) + local_sources.shape, local_sources.dtype)
    rows = jax.ShapeDtypeStruct(
        (features.shape[0], sections) + features.shape[1:], features.dtype
    )
    anywhere = pl.BlockSpec(memory_space=pl.ANY)
    return pl.pallas_call(
        functools.partial(pattern_kernel, sections, owners),
        out_shape=(table, table, rows),
        in_specs=[anywhere, anywhere],
        out_specs=(anywhere, anywhere, anywhere),
        scratch_shapes=[pltpu.SemaphoreType.DMA((owners,)) for _ in range(4)]
        + [
            pltpu.SemaphoreType.DMA(()),
            pltpu.SemaphoreType.DMA(()),
            pltpu.SemaphoreType.DMA((sections,)),
            pltpu.SemaphoreType.DMA(()),
        ],
        compiler_params=pltpu.CompilerParams(collective_id=1, has_side_effects=True),
    )(local_sources, features)


def rows_kernel(sections, src_ref, out_ref, send_sem, recv_sem, local_sem):
    me_s = lax.axis_index("section")
    me_c = lax.axis_index("col")
    last = sections - 1
    barrier = pltpu.get_barrier_semaphore()

    @pl.when(me_s == last)
    def _():
        for r in range(last):
            pl.semaphore_signal(barrier, inc=1, device_id=(r, me_c), device_id_type=MESH_ID)

    @pl.when(me_s != last)
    def _():
        pl.semaphore_signal(barrier, inc=1, device_id=(last, me_c), device_id_type=MESH_ID)

    is_last = (me_s == last).astype(jnp.int32)
    pl.semaphore_wait(barrier, is_last * last + (1 - is_last))

    def row_copy(r):
        return pltpu.make_async_remote_copy(
            src_ref=src_ref.at[r],
            dst_ref=out_ref,
            send_sem=send_sem.at[r],
            recv_sem=recv_sem,
            device_id=(r, me_c),
            device_id_type=MESH_ID,
        )

    @pl.when(me_s == last)
    def _():
        for r in range(last):
            row_copy(r).start()
        mine = pltpu.make_async_copy(src_ref.at[last], out_ref, local_sem)
        mine.start()
        mine.wait()
        for r in range(last):
            row_copy(r).wait_send()

    @pl.when(me_s != last)
    def _():
        row_copy(0).wait_recv()


def deliver_rows(row_parts, sections):
    anywhere = pl.BlockSpec(memory_space=pl.ANY)
    return pl.pallas_call(
        functools.partial(rows_kernel, sections),
        out_shape=jax.ShapeDtypeStruct(row_parts.shape[1:], row_parts.dtype),
        in_specs=[anywhere],
        out_specs=anywhere,
        scratch_shapes=[
            pltpu.SemaphoreType.DMA((sections,)),
            pltpu.SemaphoreType.DMA(()),
            pltpu.SemaphoreType.DMA(()),
        ],
        compiler_params=pltpu.CompilerParams(collective_id=2, has_side_effects=True),
    )(row_parts)


def body(features, weights, sources, bias, batch_rows):
    sections = lax.axis_size("section")
    owners = lax.axis_size("col")
    section_idx = lax.axis_index("section")
    col_idx = lax.axis_index("col")
    local_w = weights[0]
    blocks_own = local_w.shape[0]
    nonzero_count = local_w.shape[1]
    block_size = local_w.shape[2]
    local_src = sources[0].reshape(blocks_own * nonzero_count)
    own_table, next_table, row_parts = exchange_patterns(sources[0], features, sections, owners)
    local_rows = jnp.arange(blocks_own, dtype=jnp.int32)
    below = (local_rows[:, None] <= local_rows[None, :]).astype(jnp.float32)
    slot_ids = jnp.arange(CAP, dtype=jnp.int32)

    def ranks_of(wanted):
        return jnp.einsum("...i,ij->...j", wanted.astype(jnp.float32), below).astype(jnp.int32) - 1

    def sender_list(table):
        flat = table.reshape(owners, blocks_own * nonzero_count)
        mine = col_idx * blocks_own + local_rows
        wanted = jnp.any(flat[:, :, None] == mine[None, None, :], axis=1)
        chosen = wanted[:, None, :] & (ranks_of(wanted)[:, None, :] == slot_ids[None, :, None])
        return jnp.sum(chosen.astype(jnp.int32) * local_rows[None, None, :], axis=2)

    both_lists = jax.vmap(sender_list)(jnp.stack([own_table, next_table]))
    outgoing = both_lists[0].reshape(owners * CAP)
    outgoing_next = jnp.where(
        section_idx == sections - 1,
        jnp.arange(owners * CAP, dtype=jnp.int32),
        both_lists[1].reshape(owners * CAP),
    )
    catalog = jnp.arange(owners * blocks_own, dtype=jnp.int32)
    requested = jnp.any(local_src[:, None] == catalog[None, :], axis=0).reshape(owners, blocks_own)
    slot_table = jnp.arange(owners, dtype=jnp.int32)[:, None] * CAP + ranks_of(requested)
    slot_of = jnp.sum(
        (local_src[:, None] == catalog[None, :]).astype(jnp.int32) * slot_table.reshape(-1)[None, :],
        axis=1,
    )
    batches = features.shape[0]
    row_total = features.shape[1] * sections
    all_inputs = row_parts.reshape(batches, row_total, -1)
    piece_rows = 8
    splits = row_total // piece_rows
    first_blocks = all_inputs.reshape(batches * splits, piece_rows, blocks_own, block_size)
    first_blocks = first_blocks.transpose(0, 2, 1, 3)
    finished = run_pipeline(
        first_blocks,
        local_w.reshape(blocks_own, nonzero_count * block_size, block_size),
        bias[0].reshape(blocks_own, 1, block_size),
        slot_of,
        outgoing_next,
        outgoing,
        sections,
        owners,
    )
    finished = finished.reshape(batches, splits, blocks_own, piece_rows, block_size)
    completed = finished.transpose(0, 1, 3, 2, 4).reshape(
        batches, row_total, blocks_own * block_size
    )
    own_rows = row_total // sections
    outgoing_rows = completed.reshape(batches, sections, own_rows, blocks_own * block_size)
    own_result = deliver_rows(outgoing_rows.transpose(1, 0, 2, 3), sections)
    row_ids = section_idx * own_rows + jnp.arange(own_rows, dtype=jnp.int32)
    row_mask = row_ids[None, :] < batch_rows[:, None]
    return jnp.where(row_mask[:, :, None], own_result, jnp.zeros_like(own_result))


def solution(mesh):
    in_specs = (
        P(None, "section", "col"),
        P("section", "col", None, None, None),
        P("section", "col", None),
        P("section", "col"),
        P(),
    )
    out_specs = P(None, "section", "col")
    return jax.shard_map(body, mesh=mesh, in_specs=in_specs, out_specs=out_specs, check_vma=False)
```

```python
import functools

import jax
import jax.numpy as jnp
from jax import lax
from jax.experimental import pallas as pl
from jax.experimental.pallas import tpu as pltpu
from jax.sharding import PartitionSpec as P

CAP = 2
MESH_ID = pl.DeviceIdType.MESH


def pipeline_kernel(
    sections, owners, batches, first_ref, w_ref, b_ref, slot_ref, next_ref, first_list_ref,
    out_ref, *scratch,
):
    recv = scratch[:batches]
    send0 = scratch[batches:2 * batches]
    send_sem, recv_sem, local_sem, send0_sem = scratch[2 * batches:]
    me_s = lax.axis_index("section")
    me_c = lax.axis_index("col")
    blocks_own = w_ref.shape[0]
    nonzero_count = slot_ref.shape[0] // blocks_own
    barrier = pltpu.get_barrier_semaphore()

    @pl.when(me_s > 0)
    def _():
        for d in range(owners):
            pl.semaphore_signal(barrier, inc=1, device_id=(me_s - 1, d), device_id_type=MESH_ID)

    @pl.when(me_s < sections - 1)
    def _():
        for d in range(owners):
            pl.semaphore_signal(barrier, inc=1, device_id=(me_s + 1, d), device_id_type=MESH_ID)

    @pl.when(me_s == 0)
    def _():
        for d in range(owners):

            @pl.when(me_c != d)
            def _():
                pl.semaphore_signal(barrier, inc=1, device_id=(0, d), device_id_type=MESH_ID)

    is_first = (me_s == 0).astype(jnp.int32)
    peers = owners * (
        (me_s > 0).astype(jnp.int32) + (me_s < sections - 1).astype(jnp.int32)
    ) + is_first * (owners - 1)
    pl.semaphore_wait(barrier, peers)

    def first_copy(m, d):
        return pltpu.make_async_remote_copy(
            src_ref=send0[m].at[pl.ds(d * CAP, CAP)],
            dst_ref=recv[m].at[pl.ds(me_c * CAP, CAP)],
            send_sem=send0_sem.at[m, d],
            recv_sem=recv_sem.at[m, me_c],
            device_id=(0, d),
            device_id_type=MESH_ID,
        )

    def first_local(m):
        return pltpu.make_async_copy(
            send0[m].at[pl.ds(me_c * CAP, CAP)],
            recv[m].at[pl.ds(me_c * CAP, CAP)],
            local_sem.at[m],
        )

    @pl.when(me_s == 0)
    def _():
        for m in range(batches):

            def stage_first(i, carry):
                send0[m][i] = first_ref[m, first_list_ref[i]]
                return carry

            lax.fori_loop(0, owners * CAP, stage_first, 0, unroll=True)
            for d in range(owners):

                @pl.when(me_c != d)
                def _():
                    first_copy(m, d).start()

            first_local(m).start()

    def outgoing_copy(m, d):
        return pltpu.make_async_remote_copy(
            src_ref=out_ref.at[m, pl.ds(d * CAP, CAP)],
            dst_ref=recv[m].at[pl.ds(me_c * CAP, CAP)],
            send_sem=send_sem.at[m, d],
            recv_sem=recv_sem.at[m, me_c],
            device_id=(me_s + 1, d),
            device_id_type=MESH_ID,
        )

    for m in range(batches):

        @pl.when(me_s == 0)
        def _():
            first_local(m).wait()
            for e in range(owners):

                @pl.when(me_c != e)
                def _():
                    pltpu.make_async_remote_copy(
                        src_ref=send0[m].at[pl.ds(e * CAP, CAP)],
                        dst_ref=recv[m].at[pl.ds(e * CAP, CAP)],
                        send_sem=send0_sem.at[m, e],
                        recv_sem=recv_sem.at[m, e],
                        device_id=(0, e),
                        device_id_type=MESH_ID,
                    ).wait_recv()

        @pl.when(me_s > 0)
        def _():
            for e in range(owners):
                pltpu.make_async_remote_copy(
                    src_ref=out_ref.at[m, pl.ds(e * CAP, CAP)],
                    dst_ref=recv[m].at[pl.ds(e * CAP, CAP)],
                    send_sem=send_sem.at[m, e],
                    recv_sem=recv_sem.at[m, e],
                    device_id=(me_s - 1, e),
                    device_id_type=MESH_ID,
                ).wait_recv()

        def block_step(j, carry):
            block = next_ref[j]
            picked = jnp.concatenate(
                [recv[m][slot_ref[block * nonzero_count + k]] for k in range(nonzero_count)],
                axis=-1,
            )
            acc = jnp.dot(picked, w_ref[block], preferred_element_type=jnp.float32)
            out_ref[m, j] = jnp.clip(acc + b_ref[block], 0.0, 32.0).astype(out_ref.dtype)
            return carry

        lax.fori_loop(0, blocks_own, block_step, 0, unroll=True)

        @pl.when(me_s < sections - 1)
        def _():
            for d in range(owners):
                outgoing_copy(m, d).start()

    @pl.when(me_s < sections - 1)
    def _():
        for m in range(batches):
            for d in range(owners):
                outgoing_copy(m, d).wait_send()

    @pl.when(me_s == 0)
    def _():
        for m in range(batches):
            for d in range(owners):

                @pl.when(me_c != d)
                def _():
                    first_copy(m, d).wait_send()


def run_pipeline(
    first_blocks, local_w, local_bias, slot_of, outgoing_next, outgoing, sections, owners
):
    batches = first_blocks.shape[0]
    blocks_own = local_w.shape[0]
    rows = first_blocks.shape[2]
    slots_shape = (owners * CAP,) + first_blocks.shape[2:]
    block_size = local_w.shape[-1]
    vmem = pl.BlockSpec(memory_space=pltpu.VMEM)
    smem = pl.BlockSpec(memory_space=pltpu.SMEM)
    return pl.pallas_call(
        functools.partial(pipeline_kernel, sections, owners, batches),
        out_shape=jax.ShapeDtypeStruct((batches, blocks_own, rows, block_size), jnp.bfloat16),
        in_specs=[vmem, vmem, vmem, smem, smem, smem],
        out_specs=vmem,
        scratch_shapes=[
            *[pltpu.VMEM(slots_shape, jnp.bfloat16) for _ in range(2 * batches)],
            pltpu.SemaphoreType.DMA((batches, owners)),
            pltpu.SemaphoreType.DMA((batches, owners)),
            pltpu.SemaphoreType.DMA((batches,)),
            pltpu.SemaphoreType.DMA((batches, owners)),
        ],
        compiler_params=pltpu.CompilerParams(collective_id=0, has_side_effects=True),
    )(first_blocks, local_w, local_bias, slot_of, outgoing_next, outgoing)


def pattern_kernel(sections, owners, src_ref, feat_ref, own_ref, nxt_ref, rows_ref, *sems):
    own_send, own_recv, nxt_send, nxt_recv, local_sem, rows_send, rows_recv, rows_sem = sems
    me_s = lax.axis_index("section")
    me_c = lax.axis_index("col")
    barrier = pltpu.get_barrier_semaphore()
    for d in range(owners):

        @pl.when(me_c != d)
        def _():
            pl.semaphore_signal(barrier, inc=1, device_id=(me_s, d), device_id_type=MESH_ID)

    @pl.when(me_s > 0)
    def _():
        for d in range(owners):
            pl.semaphore_signal(barrier, inc=1, device_id=(me_s - 1, d), device_id_type=MESH_ID)

    @pl.when(me_s < sections - 1)
    def _():
        for d in range(owners):
            pl.semaphore_signal(barrier, inc=1, device_id=(me_s + 1, d), device_id_type=MESH_ID)

    @pl.when(me_s > 0)
    def _():
        pl.semaphore_signal(barrier, inc=1, device_id=(0, me_c), device_id_type=MESH_ID)

    @pl.when(me_s == 0)
    def _():
        for r in range(1, sections):
            pl.semaphore_signal(barrier, inc=1, device_id=(r, me_c), device_id_type=MESH_ID)

    is_first = (me_s == 0).astype(jnp.int32)
    peers = (owners - 1) + owners * (
        (me_s > 0).astype(jnp.int32) + (me_s < sections - 1).astype(jnp.int32)
    ) + is_first * (sections - 1) + (1 - is_first)
    pl.semaphore_wait(barrier, peers)

    def own_copy(d, e):
        return pltpu.make_async_remote_copy(
            src_ref=src_ref,
            dst_ref=own_ref.at[e],
            send_sem=own_send.at[d],
            recv_sem=own_recv.at[e],
            device_id=(me_s, d),
            device_id_type=MESH_ID,
        )

    def nxt_copy(dev_s, d, e):
        return pltpu.make_async_remote_copy(
            src_ref=src_ref,
            dst_ref=nxt_ref.at[e],
            send_sem=nxt_send.at[d],
            recv_sem=nxt_recv.at[e],
            device_id=(dev_s, d),
            device_id_type=MESH_ID,
        )

    for d in range(owners):

        @pl.when(me_c != d)
        def _():
            own_copy(d, me_c).start()

    @pl.when(me_s > 0)
    def _():
        for d in range(owners):
            nxt_copy(me_s - 1, d, me_c).start()

    def rows_copy(r):
        return pltpu.make_async_remote_copy(
            src_ref=feat_ref,
            dst_ref=rows_ref.at[:, r],
            send_sem=rows_send,
            recv_sem=rows_recv.at[r],
            device_id=(0, me_c),
            device_id_type=MESH_ID,
        )

    @pl.when(me_s > 0)
    def _():
        rows_copy(me_s).start()

    @pl.when(me_s == 0)
    def _():
        own_rows = pltpu.make_async_copy(feat_ref, rows_ref.at[:, 0], rows_sem)
        own_rows.start()
        own_rows.wait()

    mine = pltpu.make_async_copy(src_ref, own_ref.at[me_c], local_sem)
    mine.start()
    mine.wait()
    for d in range(owners):

        @pl.when(me_c != d)
        def _():
            own_copy(d, me_c).wait_send()
            own_copy(d, d).wait_recv()

    @pl.when(me_s > 0)
    def _():
        for d in range(owners):
            nxt_copy(me_s - 1, d, me_c).wait_send()

    @pl.when(me_s < sections - 1)
    def _():
        for e in range(owners):
            nxt_copy(me_s + 1, e, e).wait_recv()

    @pl.when(me_s > 0)
    def _():
        rows_copy(me_s).wait_send()

    @pl.when(me_s == 0)
    def _():
        for r in range(1, sections):
            rows_copy(r).wait_recv()


def exchange_patterns(local_sources, features, sections, owners):
    table = jax.ShapeDtypeStruct((owners,) + local_sources.shape, local_sources.dtype)
    rows = jax.ShapeDtypeStruct(
        (features.shape[0], sections) + features.shape[1:], features.dtype
    )
    anywhere = pl.BlockSpec(memory_space=pl.ANY)
    return pl.pallas_call(
        functools.partial(pattern_kernel, sections, owners),
        out_shape=(table, table, rows),
        in_specs=[anywhere, anywhere],
        out_specs=(anywhere, anywhere, anywhere),
        scratch_shapes=[pltpu.SemaphoreType.DMA((owners,)) for _ in range(4)]
        + [
            pltpu.SemaphoreType.DMA(()),
            pltpu.SemaphoreType.DMA(()),
            pltpu.SemaphoreType.DMA((sections,)),
            pltpu.SemaphoreType.DMA(()),
        ],
        compiler_params=pltpu.CompilerParams(collective_id=1, has_side_effects=True),
    )(local_sources, features)


def rows_kernel(sections, src_ref, out_ref, send_sem, recv_sem, local_sem):
    me_s = lax.axis_index("section")
    me_c = lax.axis_index("col")
    last = sections - 1
    barrier = pltpu.get_barrier_semaphore()

    @pl.when(me_s == last)
    def _():
        for r in range(last):
            pl.semaphore_signal(barrier, inc=1, device_id=(r, me_c), device_id_type=MESH_ID)

    @pl.when(me_s != last)
    def _():
        pl.semaphore_signal(barrier, inc=1, device_id=(last, me_c), device_id_type=MESH_ID)

    is_last = (me_s == last).astype(jnp.int32)
    pl.semaphore_wait(barrier, is_last * last + (1 - is_last))

    own_rows = out_ref.shape[2]
    piece_rows = src_ref.shape[3]

    def part(r):
        first = r * own_rows
        return src_ref.at[:, first // piece_rows, :, pl.ds(first % piece_rows, own_rows), :]

    def row_copy(r):
        return pltpu.make_async_remote_copy(
            src_ref=part(r),
            dst_ref=out_ref,
            send_sem=send_sem.at[r],
            recv_sem=recv_sem,
            device_id=(r, me_c),
            device_id_type=MESH_ID,
        )

    @pl.when(me_s == last)
    def _():
        for r in range(last):
            row_copy(r).start()
        mine = pltpu.make_async_copy(part(last), out_ref, local_sem)
        mine.start()
        mine.wait()
        for r in range(last):
            row_copy(r).wait_send()

    @pl.when(me_s != last)
    def _():
        row_copy(0).wait_recv()


def deliver_rows(row_parts, sections, own_rows):
    anywhere = pl.BlockSpec(memory_space=pl.ANY)
    batches, _, blocks, _, lanes = row_parts.shape
    return pl.pallas_call(
        functools.partial(rows_kernel, sections),
        out_shape=jax.ShapeDtypeStruct((batches, blocks, own_rows, lanes), row_parts.dtype),
        in_specs=[anywhere],
        out_specs=anywhere,
        scratch_shapes=[
            pltpu.SemaphoreType.DMA((sections,)),
            pltpu.SemaphoreType.DMA(()),
            pltpu.SemaphoreType.DMA(()),
        ],
        compiler_params=pltpu.CompilerParams(collective_id=2, has_side_effects=True),
    )(row_parts)


def body(features, weights, sources, bias, batch_rows):
    sections = lax.axis_size("section")
    owners = lax.axis_size("col")
    section_idx = lax.axis_index("section")
    col_idx = lax.axis_index("col")
    local_w = weights[0]
    blocks_own = local_w.shape[0]
    nonzero_count = local_w.shape[1]
    block_size = local_w.shape[2]
    local_src = sources[0].reshape(blocks_own * nonzero_count)
    own_table, next_table, row_parts = exchange_patterns(sources[0], features, sections, owners)
    local_rows = jnp.arange(blocks_own, dtype=jnp.int32)
    below = (local_rows[:, None] <= local_rows[None, :]).astype(jnp.float32)
    slot_ids = jnp.arange(CAP, dtype=jnp.int32)

    def ranks_of(wanted):
        return jnp.einsum("...i,ij->...j", wanted.astype(jnp.float32), below).astype(jnp.int32) - 1

    def sender_list(table):
        flat = table.reshape(owners, blocks_own * nonzero_count)
        mine = col_idx * blocks_own + local_rows
        wanted = jnp.any(flat[:, :, None] == mine[None, None, :], axis=1)
        chosen = wanted[:, None, :] & (ranks_of(wanted)[:, None, :] == slot_ids[None, :, None])
        return jnp.sum(chosen.astype(jnp.int32) * local_rows[None, None, :], axis=2)

    both_lists = jax.vmap(sender_list)(jnp.stack([own_table, next_table]))
    outgoing = both_lists[0].reshape(owners * CAP)
    outgoing_next = jnp.where(
        section_idx == sections - 1,
        jnp.arange(owners * CAP, dtype=jnp.int32),
        both_lists[1].reshape(owners * CAP),
    )
    catalog = jnp.arange(owners * blocks_own, dtype=jnp.int32)
    requested = jnp.any(local_src[:, None] == catalog[None, :], axis=0).reshape(owners, blocks_own)
    slot_table = jnp.arange(owners, dtype=jnp.int32)[:, None] * CAP + ranks_of(requested)
    slot_of = jnp.sum(
        (local_src[:, None] == catalog[None, :]).astype(jnp.int32) * slot_table.reshape(-1)[None, :],
        axis=1,
    )
    batches = features.shape[0]
    row_total = features.shape[1] * sections
    all_inputs = row_parts.reshape(batches, row_total, -1)
    piece_rows = 8
    splits = row_total // piece_rows
    first_blocks = all_inputs.reshape(batches * splits, piece_rows, blocks_own, block_size)
    first_blocks = first_blocks.transpose(0, 2, 1, 3)
    finished = run_pipeline(
        first_blocks,
        local_w.reshape(blocks_own, nonzero_count * block_size, block_size),
        bias[0].reshape(blocks_own, 1, block_size),
        slot_of,
        outgoing_next,
        outgoing,
        sections,
        owners,
    )
    finished = finished.reshape(batches, splits, blocks_own, piece_rows, block_size)
    own_rows = row_total // sections
    own_result = deliver_rows(finished, sections, own_rows).transpose(0, 2, 1, 3).reshape(
        batches, own_rows, blocks_own * block_size
    )
    row_ids = section_idx * own_rows + jnp.arange(own_rows, dtype=jnp.int32)
    row_mask = row_ids[None, :] < batch_rows[:, None]
    return jnp.where(row_mask[:, :, None], own_result, jnp.zeros_like(own_result))


def solution(mesh):
    in_specs = (
        P(None, "section", "col"),
        P("section", "col", None, None, None),
        P("section", "col", None),
        P("section", "col"),
        P(),
    )
    out_specs = P(None, "section", "col")
    return jax.shard_map(body, mesh=mesh, in_specs=in_specs, out_specs=out_specs, check_vma=False)
```

```python
import functools

import jax
import jax.numpy as jnp
from jax import lax
from jax.experimental import pallas as pl
from jax.experimental.pallas import tpu as pltpu
from jax.sharding import PartitionSpec as P

CAP = 2
MESH_ID = pl.DeviceIdType.MESH


def pipeline_kernel(
    sections, owners, batches, first_ref, w_ref, b_ref, slot_ref, next_ref, first_list_ref,
    out_ref, *scratch,
):
    recv = scratch[:batches]
    send0 = scratch[batches:2 * batches]
    send_sem, recv_sem, local_sem, send0_sem = scratch[2 * batches:]
    me_s = lax.axis_index("section")
    me_c = lax.axis_index("col")
    blocks_own = w_ref.shape[0]
    nonzero_count = slot_ref.shape[0] // blocks_own
    barrier = pltpu.get_barrier_semaphore()

    @pl.when(me_s > 0)
    def _():
        for d in range(owners):
            pl.semaphore_signal(barrier, inc=1, device_id=(me_s - 1, d), device_id_type=MESH_ID)

    @pl.when(me_s < sections - 1)
    def _():
        for d in range(owners):
            pl.semaphore_signal(barrier, inc=1, device_id=(me_s + 1, d), device_id_type=MESH_ID)

    @pl.when(me_s == 0)
    def _():
        for d in range(owners):

            @pl.when(me_c != d)
            def _():
                pl.semaphore_signal(barrier, inc=1, device_id=(0, d), device_id_type=MESH_ID)

    is_first = (me_s == 0).astype(jnp.int32)
    peers = owners * (
        (me_s > 0).astype(jnp.int32) + (me_s < sections - 1).astype(jnp.int32)
    ) + is_first * (owners - 1)
    pl.semaphore_wait(barrier, peers)

    def first_copy(m, d):
        return pltpu.make_async_remote_copy(
            src_ref=send0[m].at[pl.ds(d * CAP, CAP)],
            dst_ref=recv[m].at[pl.ds(me_c * CAP, CAP)],
            send_sem=send0_sem.at[m, d],
            recv_sem=recv_sem.at[m, me_c],
            device_id=(0, d),
            device_id_type=MESH_ID,
        )

    def first_local(m):
        return pltpu.make_async_copy(
            send0[m].at[pl.ds(me_c * CAP, CAP)],
            recv[m].at[pl.ds(me_c * CAP, CAP)],
            local_sem.at[m],
        )

    @pl.when(me_s == 0)
    def _():
        for m in range(batches):

            def stage_first(i, carry):
                send0[m][i] = first_ref[m, first_list_ref[i]]
                return carry

            lax.fori_loop(0, owners * CAP, stage_first, 0, unroll=True)
            for d in range(owners):

                @pl.when(me_c != d)
                def _():
                    first_copy(m, d).start()

            first_local(m).start()

    def outgoing_copy(m, d):
        return pltpu.make_async_remote_copy(
            src_ref=out_ref.at[m, pl.ds(d * CAP, CAP)],
            dst_ref=recv[m].at[pl.ds(me_c * CAP, CAP)],
            send_sem=send_sem.at[m, d],
            recv_sem=recv_sem.at[m, me_c],
            device_id=(me_s + 1, d),
            device_id_type=MESH_ID,
        )

    for m in range(batches):

        @pl.when(me_s == 0)
        def _():
            first_local(m).wait()
            for e in range(owners):

                @pl.when(me_c != e)
                def _():
                    pltpu.make_async_remote_copy(
                        src_ref=send0[m].at[pl.ds(e * CAP, CAP)],
                        dst_ref=recv[m].at[pl.ds(e * CAP, CAP)],
                        send_sem=send0_sem.at[m, e],
                        recv_sem=recv_sem.at[m, e],
                        device_id=(0, e),
                        device_id_type=MESH_ID,
                    ).wait_recv()

        @pl.when(me_s > 0)
        def _():
            for e in range(owners):
                pltpu.make_async_remote_copy(
                    src_ref=out_ref.at[m, pl.ds(e * CAP, CAP)],
                    dst_ref=recv[m].at[pl.ds(e * CAP, CAP)],
                    send_sem=send_sem.at[m, e],
                    recv_sem=recv_sem.at[m, e],
                    device_id=(me_s - 1, e),
                    device_id_type=MESH_ID,
                ).wait_recv()

        def block_step(j, carry):
            block = next_ref[j]
            picked = jnp.concatenate(
                [recv[m][slot_ref[block * nonzero_count + k]] for k in range(nonzero_count)],
                axis=-1,
            )
            acc = jnp.dot(picked, w_ref[block], preferred_element_type=jnp.float32)
            out_ref[m, j] = jnp.clip(acc + b_ref[block], 0.0, 32.0).astype(out_ref.dtype)
            return carry

        lax.fori_loop(0, blocks_own, block_step, 0, unroll=True)

        @pl.when(me_s < sections - 1)
        def _():
            for d in range(owners):
                outgoing_copy(m, d).start()

    @pl.when(me_s < sections - 1)
    def _():
        for m in range(batches):
            for d in range(owners):
                outgoing_copy(m, d).wait_send()

    @pl.when(me_s == 0)
    def _():
        for m in range(batches):
            for d in range(owners):

                @pl.when(me_c != d)
                def _():
                    first_copy(m, d).wait_send()


def run_pipeline(
    first_blocks, local_w, local_bias, slot_of, outgoing_next, outgoing, sections, owners
):
    batches = first_blocks.shape[0]
    blocks_own = local_w.shape[0]
    rows = first_blocks.shape[2]
    slots_shape = (owners * CAP,) + first_blocks.shape[2:]
    block_size = local_w.shape[-1]
    vmem = pl.BlockSpec(memory_space=pltpu.VMEM)
    smem = pl.BlockSpec(memory_space=pltpu.SMEM)
    return pl.pallas_call(
        functools.partial(pipeline_kernel, sections, owners, batches),
        out_shape=jax.ShapeDtypeStruct((batches, blocks_own, rows, block_size), jnp.bfloat16),
        in_specs=[vmem, vmem, vmem, smem, smem, smem],
        out_specs=vmem,
        scratch_shapes=[
            *[pltpu.VMEM(slots_shape, jnp.bfloat16) for _ in range(2 * batches)],
            pltpu.SemaphoreType.DMA((batches, owners)),
            pltpu.SemaphoreType.DMA((batches, owners)),
            pltpu.SemaphoreType.DMA((batches,)),
            pltpu.SemaphoreType.DMA((batches, owners)),
        ],
        compiler_params=pltpu.CompilerParams(collective_id=0, has_side_effects=True),
    )(first_blocks, local_w, local_bias, slot_of, outgoing_next, outgoing)


def pattern_kernel(sections, owners, src_ref, feat_ref, own_ref, nxt_ref, rows_ref, *sems):
    own_send, own_recv, nxt_send, nxt_recv, local_sem, rows_send, rows_recv, rows_sem = sems
    me_s = lax.axis_index("section")
    me_c = lax.axis_index("col")
    barrier = pltpu.get_barrier_semaphore()
    for d in range(owners):

        @pl.when(me_c != d)
        def _():
            pl.semaphore_signal(barrier, inc=1, device_id=(me_s, d), device_id_type=MESH_ID)

    @pl.when(me_s > 0)
    def _():
        for d in range(owners):
            pl.semaphore_signal(barrier, inc=1, device_id=(me_s - 1, d), device_id_type=MESH_ID)

    @pl.when(me_s < sections - 1)
    def _():
        for d in range(owners):
            pl.semaphore_signal(barrier, inc=1, device_id=(me_s + 1, d), device_id_type=MESH_ID)

    @pl.when(me_s > 0)
    def _():
        pl.semaphore_signal(barrier, inc=1, device_id=(0, me_c), device_id_type=MESH_ID)

    @pl.when(me_s == 0)
    def _():
        for r in range(1, sections):
            pl.semaphore_signal(barrier, inc=1, device_id=(r, me_c), device_id_type=MESH_ID)

    is_first = (me_s == 0).astype(jnp.int32)
    peers = (owners - 1) + owners * (
        (me_s > 0).astype(jnp.int32) + (me_s < sections - 1).astype(jnp.int32)
    ) + is_first * (sections - 1) + (1 - is_first)
    pl.semaphore_wait(barrier, peers)

    def own_copy(d, e):
        return pltpu.make_async_remote_copy(
            src_ref=src_ref,
            dst_ref=own_ref.at[e],
            send_sem=own_send.at[d],
            recv_sem=own_recv.at[e],
            device_id=(me_s, d),
            device_id_type=MESH_ID,
        )

    def nxt_copy(dev_s, d, e):
        return pltpu.make_async_remote_copy(
            src_ref=src_ref,
            dst_ref=nxt_ref.at[e],
            send_sem=nxt_send.at[d],
            recv_sem=nxt_recv.at[e],
            device_id=(dev_s, d),
            device_id_type=MESH_ID,
        )

    for d in range(owners):

        @pl.when(me_c != d)
        def _():
            own_copy(d, me_c).start()

    @pl.when(me_s > 0)
    def _():
        for d in range(owners):
            nxt_copy(me_s - 1, d, me_c).start()

    sent_rows = feat_ref.shape[2]
    piece_rows = rows_ref.shape[3]

    def rows_part(r):
        first = r * sent_rows
        return rows_ref.at[:, first // piece_rows, :, pl.ds(first % piece_rows, sent_rows), :]

    def rows_copy(r):
        return pltpu.make_async_remote_copy(
            src_ref=feat_ref,
            dst_ref=rows_part(r),
            send_sem=rows_send,
            recv_sem=rows_recv.at[r],
            device_id=(0, me_c),
            device_id_type=MESH_ID,
        )

    for r in range(1, sections):

        @pl.when(me_s == r)
        def _():
            rows_copy(r).start()

    @pl.when(me_s == 0)
    def _():
        own_rows = pltpu.make_async_copy(feat_ref, rows_part(0), rows_sem)
        own_rows.start()
        own_rows.wait()

    mine = pltpu.make_async_copy(src_ref, own_ref.at[me_c], local_sem)
    mine.start()
    mine.wait()
    for d in range(owners):

        @pl.when(me_c != d)
        def _():
            own_copy(d, me_c).wait_send()
            own_copy(d, d).wait_recv()

    @pl.when(me_s > 0)
    def _():
        for d in range(owners):
            nxt_copy(me_s - 1, d, me_c).wait_send()

    @pl.when(me_s < sections - 1)
    def _():
        for e in range(owners):
            nxt_copy(me_s + 1, e, e).wait_recv()

    for r in range(1, sections):

        @pl.when(me_s == r)
        def _():
            rows_copy(r).wait_send()

    @pl.when(me_s == 0)
    def _():
        for r in range(1, sections):
            rows_copy(r).wait_recv()


def exchange_patterns(local_sources, features, sections, owners, piece_rows, lanes):
    table = jax.ShapeDtypeStruct((owners,) + local_sources.shape, local_sources.dtype)
    batches, sent_rows, width = features.shape
    row_total = sent_rows * sections
    rows = jax.ShapeDtypeStruct(
        (batches, row_total // piece_rows, width // lanes, piece_rows, lanes), features.dtype
    )
    features = features.reshape(batches, sent_rows, width // lanes, lanes).transpose(0, 2, 1, 3)
    anywhere = pl.BlockSpec(memory_space=pl.ANY)
    return pl.pallas_call(
        functools.partial(pattern_kernel, sections, owners),
        out_shape=(table, table, rows),
        in_specs=[anywhere, anywhere],
        out_specs=(anywhere, anywhere, anywhere),
        scratch_shapes=[pltpu.SemaphoreType.DMA((owners,)) for _ in range(4)]
        + [
            pltpu.SemaphoreType.DMA(()),
            pltpu.SemaphoreType.DMA(()),
            pltpu.SemaphoreType.DMA((sections,)),
            pltpu.SemaphoreType.DMA(()),
        ],
        compiler_params=pltpu.CompilerParams(collective_id=1, has_side_effects=True),
    )(local_sources, features)


def rows_kernel(sections, src_ref, out_ref, send_sem, recv_sem, local_sem):
    me_s = lax.axis_index("section")
    me_c = lax.axis_index("col")
    last = sections - 1
    barrier = pltpu.get_barrier_semaphore()

    @pl.when(me_s == last)
    def _():
        for r in range(last):
            pl.semaphore_signal(barrier, inc=1, device_id=(r, me_c), device_id_type=MESH_ID)

    @pl.when(me_s != last)
    def _():
        pl.semaphore_signal(barrier, inc=1, device_id=(last, me_c), device_id_type=MESH_ID)

    is_last = (me_s == last).astype(jnp.int32)
    pl.semaphore_wait(barrier, is_last * last + (1 - is_last))

    own_rows = out_ref.shape[2]
    piece_rows = src_ref.shape[3]

    def part(r):
        first = r * own_rows
        return src_ref.at[:, first // piece_rows, :, pl.ds(first % piece_rows, own_rows), :]

    def row_copy(r):
        return pltpu.make_async_remote_copy(
            src_ref=part(r),
            dst_ref=out_ref,
            send_sem=send_sem.at[r],
            recv_sem=recv_sem,
            device_id=(r, me_c),
            device_id_type=MESH_ID,
        )

    @pl.when(me_s == last)
    def _():
        for r in range(last):
            row_copy(r).start()
        mine = pltpu.make_async_copy(part(last), out_ref, local_sem)
        mine.start()
        mine.wait()
        for r in range(last):
            row_copy(r).wait_send()

    @pl.when(me_s != last)
    def _():
        row_copy(0).wait_recv()


def deliver_rows(row_parts, sections, own_rows):
    anywhere = pl.BlockSpec(memory_space=pl.ANY)
    batches, _, blocks, _, lanes = row_parts.shape
    return pl.pallas_call(
        functools.partial(rows_kernel, sections),
        out_shape=jax.ShapeDtypeStruct((batches, blocks, own_rows, lanes), row_parts.dtype),
        in_specs=[anywhere],
        out_specs=anywhere,
        scratch_shapes=[
            pltpu.SemaphoreType.DMA((sections,)),
            pltpu.SemaphoreType.DMA(()),
            pltpu.SemaphoreType.DMA(()),
        ],
        compiler_params=pltpu.CompilerParams(collective_id=2, has_side_effects=True),
    )(row_parts)


def body(features, weights, sources, bias, batch_rows):
    sections = lax.axis_size("section")
    owners = lax.axis_size("col")
    section_idx = lax.axis_index("section")
    col_idx = lax.axis_index("col")
    local_w = weights[0]
    blocks_own = local_w.shape[0]
    nonzero_count = local_w.shape[1]
    block_size = local_w.shape[2]
    local_src = sources[0].reshape(blocks_own * nonzero_count)
    own_table, next_table, row_parts = exchange_patterns(
        sources[0], features, sections, owners, 8, block_size
    )
    local_rows = jnp.arange(blocks_own, dtype=jnp.int32)
    below = (local_rows[:, None] <= local_rows[None, :]).astype(jnp.float32)
    slot_ids = jnp.arange(CAP, dtype=jnp.int32)

    def ranks_of(wanted):
        return jnp.einsum("...i,ij->...j", wanted.astype(jnp.float32), below).astype(jnp.int32) - 1

    def sender_list(table):
        flat = table.reshape(owners, blocks_own * nonzero_count)
        mine = col_idx * blocks_own + local_rows
        wanted = jnp.any(flat[:, :, None] == mine[None, None, :], axis=1)
        chosen = wanted[:, None, :] & (ranks_of(wanted)[:, None, :] == slot_ids[None, :, None])
        return jnp.sum(chosen.astype(jnp.int32) * local_rows[None, None, :], axis=2)

    both_lists = jax.vmap(sender_list)(jnp.stack([own_table, next_table]))
    outgoing = both_lists[0].reshape(owners * CAP)
    outgoing_next = jnp.where(
        section_idx == sections - 1,
        jnp.arange(owners * CAP, dtype=jnp.int32),
        both_lists[1].reshape(owners * CAP),
    )
    catalog = jnp.arange(owners * blocks_own, dtype=jnp.int32)
    requested = jnp.any(local_src[:, None] == catalog[None, :], axis=0).reshape(owners, blocks_own)
    slot_table = jnp.arange(owners, dtype=jnp.int32)[:, None] * CAP + ranks_of(requested)
    slot_of = jnp.sum(
        (local_src[:, None] == catalog[None, :]).astype(jnp.int32) * slot_table.reshape(-1)[None, :],
        axis=1,
    )
    batches = features.shape[0]
    row_total = features.shape[1] * sections
    piece_rows = 8
    splits = row_total // piece_rows
    first_blocks = row_parts.reshape(batches * splits, blocks_own, piece_rows, block_size)
    finished = run_pipeline(
        first_blocks,
        local_w.reshape(blocks_own, nonzero_count * block_size, block_size),
        bias[0].reshape(blocks_own, 1, block_size),
        slot_of,
        outgoing_next,
        outgoing,
        sections,
        owners,
    )
    finished = finished.reshape(batches, splits, blocks_own, piece_rows, block_size)
    own_rows = row_total // sections
    own_result = deliver_rows(finished, sections, own_rows).transpose(0, 2, 1, 3).reshape(
        batches, own_rows, blocks_own * block_size
    )
    row_ids = section_idx * own_rows + jnp.arange(own_rows, dtype=jnp.int32)
    row_mask = row_ids[None, :] < batch_rows[:, None]
    return jnp.where(row_mask[:, :, None], own_result, jnp.zeros_like(own_result))


def solution(mesh):
    in_specs = (
        P(None, "section", "col"),
        P("section", "col", None, None, None),
        P("section", "col", None),
        P("section", "col"),
        P(),
    )
    out_specs = P(None, "section", "col")
    return jax.shard_map(body, mesh=mesh, in_specs=in_specs, out_specs=out_specs, check_vma=False)
```
